256 devices in a mesh: ply: 4 (over z_hi, core), tile: 64 (over z_lo, y, x).
Axes of the slice: x: 4, y: 4, z: 8 (z_hi: 2, z_lo: 4; z = z_hi * 4 + z_lo), core: 2. Of those that a mesh axis runs over, the one named last changes fastest.
Arguments:
- displacement: float32 [3, 24, 512, 1024], P(None, 'ply', 'tile'), may hold values from -0.2 to 0.2
- angle_index: int32 [24], P('ply'), may hold values from 0 to 3
- bond_table: float32 [4, 14], replicated, may hold values from 5 to 50
- interface_stiffness: float32 [23], replicated, may hold values from 2 to 20
Outputs:
- force_density: float32 [3, 24, 512, 1024], P(None, 'ply', 'tile')
The draws below stay inside these ranges and needn't reach their ends.
Inputs may be any that keep to these rules, and one draw needn't show every extreme that they name: `angle_index`: each ply's fibre orientation is an index into the rows of bond_table.
All inputs are finite; a program needn't handle non-finite values.
Results may differ from the reference program's by a relative error of at most 0.000058.
Values sent between devices are 32-bit elements; how exact they have to be, the bound alone decides.
A program may use at most 128 MiB of HBM per device.

```python
import math
import jax
import jax.numpy as jnp

NY = 1024
NANG = 4
NBOND = 14
PLIES = 24
NX = 512


def set_ends(drawn, own_key, least, largest):
    spot = [jax.random.randint(jax.random.fold_in(own_key, axis), (), 0, length) for axis, length in enumerate(drawn.shape)]
    longest = drawn.shape.index(max(drawn.shape))
    beside = spot[:longest] + [(spot[longest] + 1) % drawn.shape[longest]] + spot[longest + 1:]
    return drawn.at[tuple(spot)].set(least).at[tuple(beside)].set(largest)


def level_of(own_key, dims, cuts, low, top_value):
    factor_of, own = 1.0, jax.random.fold_in(own_key, 6)
    for dim, blocks in cuts:
        steps = jnp.exp(jax.random.uniform(jax.random.fold_in(own, dim), (blocks,), jnp.float32, low / len(cuts), top_value / len(cuts)))
        factor_of = factor_of * jnp.repeat(steps, dims[dim] // blocks).reshape([-1 if axis == dim else 1 for axis in range(len(dims))])
    return factor_of


def normal_values(key, extent, deviation, bound, shards=(), held_as=jnp.bfloat16):
    level = level_of(key, extent, shards, -0.22, 0.18) if shards else 1.0
    values = jax.random.normal(key, extent, jnp.float32) * deviation * level
    return jnp.minimum(jnp.maximum(values, -bound), bound).astype(held_as)


def setup_inputs(seed: int = 0) -> dict:
    seeds = jax.random.split(jax.random.key(seed), 5)
    return {
        "displacement": normal_values(seeds[0], (3, PLIES, NX, NY), 0.04, 0.2, ((1, 4), (2, 64)), jnp.float32),
        "angle_index": set_ends(jax.random.randint(seeds[1], (PLIES,), 0, NANG), jax.random.fold_in(seeds[1], 1), 0, NANG - 1).astype(jnp.int32),
        "bond_table": jnp.clip(jnp.exp(jax.random.uniform(seeds[2], (NANG, NBOND), jnp.float32, math.log(5.0), math.log(50.0))), 5.0, 50.0),
        "interface_stiffness": jnp.clip(jnp.exp(jax.random.uniform(seeds[3], (PLIES - 1,), jnp.float32, math.log(2.0), math.log(20.0))), 2.0, 20.0),
    }


bulk_modulus = 40.0

def bond_list():
    halves = []
    for shift_x in range(-3, 4):
        for shift_y in range(-3, 4):
            radius = shift_x * shift_x + shift_y * shift_y
            if 0 < radius <= 9 and (shift_x > 0 or (shift_x == 0 and shift_y > 0)):
                halves.append((shift_x, shift_y))
    result = []
    for shift_x in range(-3, 4):
        for shift_y in range(-3, 4):
            radius = shift_x * shift_x + shift_y * shift_y
            if 0 < radius <= 9:
                if (shift_x, shift_y) in halves:
                    column = halves.index((shift_x, shift_y))
                else:
                    column = halves.index((-shift_x, -shift_y))
                result.append((shift_x, shift_y, math.sqrt(radius), column))
    return result

def inside(x_coord, y_coord, shift_x, shift_y, x_total, y_total):
    x_next = x_coord + shift_x
    y_next = y_coord + shift_y
    return (x_next >= 0) & (x_next < x_total) & (y_next >= 0) & (y_next < y_total)

def weight_sum(x_coord, y_coord, x_total, y_total):
    total = jnp.zeros((x_coord.shape[0], y_coord.shape[1]), jnp.float32)
    for shift_x, shift_y, length, column in bond_list():
        total = total + jnp.where(inside(x_coord, y_coord, shift_x, shift_y, x_total, y_total), length, 0.0)
    return total

def stretch(anchor, neighbour, shift_x, shift_y, length):
    gap = neighbour - anchor
    sep_x = shift_x + gap[0]
    sep_y = shift_y + gap[1]
    sep_z = gap[2]
    span = jnp.sqrt(sep_x * sep_x + sep_y * sep_y + sep_z * sep_z)
    return (sep_x, sep_y, sep_z, span, span - length)

def bond_terms(theta_here, mass_here, theta_there, mass_there, shear, extension, length):
    first_side = 3.0 * bulk_modulus * theta_here / mass_here + 15.0 * shear * (extension - theta_here * length / 3.0) / (mass_here * length)
    second_side = 3.0 * bulk_modulus * theta_there / mass_there + 15.0 * shear * (extension - theta_there * length / 3.0) / (mass_there * length)
    return first_side + second_side

def reference(displacement, angle_index, bond_table, interface_stiffness):
    x_total = displacement.shape[2]
    y_total = displacement.shape[3]
    bond_set = bond_list()
    x_grid = jnp.arange(x_total, dtype=jnp.int32)[:, None]
    y_grid = jnp.arange(y_total, dtype=jnp.int32)[None, :]
    x_wide = jnp.arange(-3, x_total + 3, dtype=jnp.int32)[:, None]
    y_wide = jnp.arange(-3, y_total + 3, dtype=jnp.int32)[None, :]
    mass_here = weight_sum(x_grid, y_grid, x_total, y_total)
    mass_wide = weight_sum(x_wide, y_wide, x_total, y_total)
    mass_wide = jnp.where(mass_wide > 0, mass_wide, 1.0)
    padded = jnp.pad(displacement, ((0, 0), (0, 0), (3, 3), (3, 3)))
    dilation = jnp.zeros(displacement.shape[1:], jnp.float32)
    for shift_x, shift_y, length, column in bond_set:
        neighbour = padded[:, :, 3 + shift_x:3 + shift_x + x_total, 3 + shift_y:3 + shift_y + y_total]
        stretched = stretch(displacement, neighbour, shift_x, shift_y, length)
        dilation = dilation + jnp.where(inside(x_grid, y_grid, shift_x, shift_y, x_total, y_total), stretched[4], 0.0)
    dilation = 3.0 * dilation / mass_here
    dilation_wide = jnp.pad(dilation, ((0, 0), (3, 3), (3, 3)))
    shear_table = bond_table[angle_index]
    force_x = jnp.zeros(displacement.shape[1:], jnp.float32)
    force_y = jnp.zeros(displacement.shape[1:], jnp.float32)
    force_z = jnp.zeros(displacement.shape[1:], jnp.float32)
    for shift_x, shift_y, length, column in bond_set:
        neighbour = padded[:, :, 3 + shift_x:3 + shift_x + x_total, 3 + shift_y:3 + shift_y + y_total]
        sep_x, sep_y, sep_z, span, extension = stretch(displacement, neighbour, shift_x, shift_y, length)
        theta_there = dilation_wide[:, 3 + shift_x:3 + shift_x + x_total, 3 + shift_y:3 + shift_y + y_total]
        mass_there = mass_wide[3 + shift_x:3 + shift_x + x_total, 3 + shift_y:3 + shift_y + y_total]
        shear = shear_table[:, column][:, None, None]
        scalar = bond_terms(dilation, mass_here, theta_there, mass_there, shear, extension, length)
        scalar = jnp.where(inside(x_grid, y_grid, shift_x, shift_y, x_total, y_total), scalar / span, 0.0)
        force_x = force_x + scalar * sep_x
        force_y = force_y + scalar * sep_y
        force_z = force_z + scalar * sep_z
    zero_end = jnp.zeros((1,), jnp.float32)
    coupling = jnp.concatenate([zero_end, interface_stiffness, zero_end])
    above = coupling[1:][None, :, None, None]
    below = coupling[:-1][None, :, None, None]
    upper = jnp.pad(displacement[:, 1:], ((0, 0), (0, 1), (0, 0), (0, 0)))
    lower = jnp.pad(displacement[:, :-1], ((0, 0), (1, 0), (0, 0), (0, 0)))
    layered = above * (upper - displacement) + below * (lower - displacement)
    return jnp.stack([force_x, force_y, force_z]) + layered
```

```python
import math

import jax
import jax.numpy as jnp
from jax import lax
from jax.experimental import pallas as pl
from jax.experimental.pallas import tpu as pltpu
from jax.sharding import PartitionSpec as P

bulk_modulus = 40.0


def bond_list():
    halves = []
    for shift_x in range(-3, 4):
        for shift_y in range(-3, 4):
            radius = shift_x * shift_x + shift_y * shift_y
            if 0 < radius <= 9 and (shift_x > 0 or (shift_x == 0 and shift_y > 0)):
                halves.append((shift_x, shift_y))
    result = []
    for shift_x in range(-3, 4):
        for shift_y in range(-3, 4):
            radius = shift_x * shift_x + shift_y * shift_y
            if 0 < radius <= 9:
                if (shift_x, shift_y) in halves:
                    column = halves.index((shift_x, shift_y))
                else:
                    column = halves.index((-shift_x, -shift_y))
                result.append((shift_x, shift_y, math.sqrt(radius), column))
    return result


def halo(shard, axis, dim, width):
    peers, length = lax.axis_size(axis), shard.shape[dim]
    up = [(i, (i + 1) % peers) for i in range(peers)]
    down = [(j, i) for i, j in up]
    last = lax.slice_in_dim(shard, length - width, length, axis=dim)
    first = lax.slice_in_dim(shard, 0, width, axis=dim)
    before = lax.ppermute(last, axis, up)
    after = lax.ppermute(first, axis, down)
    return jnp.concatenate([before, shard, after], axis=dim)


def shift_lanes(x, b):
    if b == 0:
        return x
    return pltpu.roll(x, (-b) % x.shape[-1], 1)


def make_kernel(cols, rows, x_total, nbond):
    bonds = bond_list()
    wide = cols + 6
    shifts = sorted({a for a, _, _, _ in bonds})
    lanes = sorted({b for _, b, _, _ in bonds})

    def kernel(x0_ref, coef_ref, u_ref, lo_ref, hi_ref, o_ref, wq_ref):
        p = pl.program_id(0)
        x0 = x0_ref[0]

        def masks(n, start):
            r = lax.broadcasted_iota(jnp.int32, (n, rows), 0) + (x0 + start)
            c = lax.broadcasted_iota(jnp.int32, (n, rows), 1)
            own = (r >= 0) & (r < x_total)
            xm = {a: own & (r + a >= 0) & (r + a < x_total) for a in shifts}
            ym = {b: (c + b >= 0) & (c + b < rows) for b in lanes}
            return xm, ym

        xm, ym = masks(wide, -3)
        mass = jnp.zeros((wide, rows), jnp.float32)
        for a, b, length, column in bonds:
            mass = mass + jnp.where(xm[a] & ym[b], length, 0.0)
        w = jnp.where(mass > 0, 1.0 / jnp.where(mass > 0, mass, 1.0), 0.0)
        ud = [u_ref[k, 0, 3:3 + wide, :] for k in range(3)]
        dil = jnp.zeros((wide, rows), jnp.float32)
        for a, b, length, column in bonds:
            nb = [shift_lanes(u_ref[k, 0, 3 + a:3 + a + wide, :], b) for k in range(3)]
            sx = (nb[0] - ud[0]) + a
            sy = (nb[1] - ud[1]) + b
            sz = nb[2] - ud[2]
            span = jnp.sqrt(sx * sx + sy * sy + sz * sz)
            dil = dil + jnp.where(xm[a] & ym[b], span - length, 0.0)
        theta = 3.0 * dil * w
        wq_ref[0] = w
        wq_ref[1] = theta * w

        xm, ym = masks(cols, 0)
        uc = [u_ref[k, 0, 6:6 + cols, :] for k in range(3)]
        wi = wq_ref[0, 3:3 + cols, :]
        qi = wq_ref[1, 3:3 + cols, :]
        fx = jnp.zeros((cols, rows), jnp.float32)
        fy = jnp.zeros((cols, rows), jnp.float32)
        fz = jnp.zeros((cols, rows), jnp.float32)
        for a, b, length, column in bonds:
            nb = [shift_lanes(u_ref[k, 0, 6 + a:6 + a + cols, :], b) for k in range(3)]
            wj = shift_lanes(wq_ref[0, 3 + a:3 + a + cols, :], b)
            qj = shift_lanes(wq_ref[1, 3 + a:3 + a + cols, :], b)
            sx = (nb[0] - uc[0]) + a
            sy = (nb[1] - uc[1]) + b
            sz = nb[2] - uc[2]
            span = jnp.sqrt(sx * sx + sy * sy + sz * sz)
            alpha = coef_ref[p, column]
            beta = coef_ref[p, nbond + column]
            t = alpha * (span - length) * (wi + wj) + beta * (qi + qj)
            f = jnp.where(xm[a] & ym[b], t / span, 0.0)
            fx = fx + f * sx
            fy = fy + f * sy
            fz = fz + f * sz
        above = coef_ref[p, 2 * nbond]
        below = coef_ref[p, 2 * nbond + 1]
        for k, fk in enumerate((fx, fy, fz)):
            hi = hi_ref[k, 0]
            lo = lo_ref[k, 0]
            o_ref[k, 0] = fk + (above * (hi - uc[k]) + below * (lo - uc[k]))

    return kernel


def local(displacement, angle_index, bond_table, interface_stiffness):
    comp_count, ply_count, col_count, row_count = displacement.shape
    nbond = bond_table.shape[1]
    x_total = col_count * lax.axis_size("tile")
    x0 = (lax.axis_index("tile") * col_count).astype(jnp.int32).reshape(1)
    lengths = [0.0] * nbond
    for a, b, length, column in bond_list():
        lengths[column] = length
    lengths = jnp.asarray(lengths, jnp.float32)
    selector = (
        angle_index[:, None] == jnp.arange(bond_table.shape[0], dtype=jnp.int32)[None, :]
    ).astype(jnp.float32)
    shear = jnp.dot(selector, bond_table, precision=lax.Precision.HIGHEST)
    alpha = 15.0 * shear / lengths[None, :]
    beta = 3.0 * bulk_modulus - 5.0 * shear
    zero_end = jnp.zeros((1,), jnp.float32)
    coupling = jnp.concatenate([zero_end, interface_stiffness, zero_end])
    local_coupling = lax.dynamic_slice_in_dim(
        coupling, lax.axis_index("ply") * ply_count, ply_count + 1
    )
    coef = jnp.concatenate(
        [alpha, beta, local_coupling[1:, None], local_coupling[:-1, None]], axis=1
    )
    ext = halo(displacement, "tile", 2, 6)
    stacked = halo(displacement, "ply", 1, 1)
    extended = col_count + 12
    kernel = make_kernel(col_count, row_count, x_total, nbond)
    smem = pltpu.MemorySpace.SMEM if hasattr(pltpu, "MemorySpace") else pltpu.SMEM
    return pl.pallas_call(
        kernel,
        grid=(ply_count,),
        in_specs=[
            pl.BlockSpec(memory_space=smem),
            pl.BlockSpec(memory_space=smem),
            pl.BlockSpec((3, 1, extended, row_count), lambda p: (0, p, 0, 0)),
            pl.BlockSpec((3, 1, col_count, row_count), lambda p: (0, p, 0, 0)),
            pl.BlockSpec((3, 1, col_count, row_count), lambda p: (0, p + 2, 0, 0)),
        ],
        out_specs=pl.BlockSpec((3, 1, col_count, row_count), lambda p: (0, p, 0, 0)),
        out_shape=jax.ShapeDtypeStruct(displacement.shape, jnp.float32),
        scratch_shapes=[pltpu.VMEM((2, col_count + 6, row_count), jnp.float32)],
    )(x0, coef, ext, stacked, stacked)


def solution(mesh):
    placed = (P(None, "ply", "tile", None), P("ply"), P(), P())
    return jax.shard_map(
        local, mesh=mesh, in_specs=placed, out_specs=P(None, "ply", "tile", None), check_vma=False
    )
```

```python
import math

import jax
import jax.numpy as jnp
from jax import lax
from jax.experimental import pallas as pl
from jax.experimental.pallas import tpu as pltpu
from jax.sharding import PartitionSpec as P

bulk_modulus = 40.0


def bond_list():
    halves = []
    for shift_x in range(-3, 4):
        for shift_y in range(-3, 4):
            radius = shift_x * shift_x + shift_y * shift_y
            if 0 < radius <= 9 and (shift_x > 0 or (shift_x == 0 and shift_y > 0)):
                halves.append((shift_x, shift_y))
    result = []
    for shift_x in range(-3, 4):
        for shift_y in range(-3, 4):
            radius = shift_x * shift_x + shift_y * shift_y
            if 0 < radius <= 9:
                if (shift_x, shift_y) in halves:
                    column = halves.index((shift_x, shift_y))
                else:
                    column = halves.index((-shift_x, -shift_y))
                result.append((shift_x, shift_y, math.sqrt(radius), column))
    return result


def halo(shard, axis, dim, width):
    peers, length = lax.axis_size(axis), shard.shape[dim]
    up = [(i, (i + 1) % peers) for i in range(peers)]
    down = [(j, i) for i, j in up]
    last = lax.slice_in_dim(shard, length - width, length, axis=dim)
    first = lax.slice_in_dim(shard, 0, width, axis=dim)
    before = lax.ppermute(last, axis, up)
    after = lax.ppermute(first, axis, down)
    return jnp.concatenate([before, shard, after], axis=dim)


def shift_lanes(x, b):
    if b == 0:
        return x
    return pltpu.roll(x, (-b) % x.shape[-1], 1)


MESH = pl.DeviceIdType.MESH


def make_kernel(plies, cols, rows, x_total, nbond):
    bonds = bond_list()
    wide = cols + 6
    shifts = sorted({a for a, _, _, _ in bonds})
    lanes = sorted({b for _, b, _, _ in bonds})

    def kernel(coef_ref, u_hbm, o_ref, ext, ply_halo, wq_ref, sems):
        t = lax.axis_index("tile")
        nt = lax.axis_size("tile")
        q = lax.axis_index("ply")
        nq = lax.axis_size("ply")
        x0 = t * cols
        own = pltpu.make_async_copy(u_hbm, ext.at[:, :, cols:2 * cols, :], sems.at[0])
        own.start()
        has = ((t > 0), (t < nt - 1), (q > 0), (q < nq - 1))
        peers = ({"tile": t - 1}, {"tile": t + 1}, {"ply": q - 1}, {"ply": q + 1})
        barrier = pltpu.get_barrier_semaphore()
        for cond, dev in zip(has, peers):
            @pl.when(cond)
            def _():
                pl.semaphore_signal(barrier, inc=1, device_id=dev, device_id_type=MESH)
        count = sum(c.astype(jnp.int32) for c in has)
        pl.semaphore_wait(barrier, count)
        copies = (
            pltpu.make_async_remote_copy(
                u_hbm, ext.at[:, :, 2 * cols:3 * cols, :], sems.at[1], sems.at[5],
                device_id=peers[0], device_id_type=MESH),
            pltpu.make_async_remote_copy(
                u_hbm, ext.at[:, :, 0:cols, :], sems.at[2], sems.at[6],
                device_id=peers[1], device_id_type=MESH),
            pltpu.make_async_remote_copy(
                u_hbm.at[:, 0], ply_halo.at[1], sems.at[3], sems.at[7],
                device_id=peers[2], device_id_type=MESH),
            pltpu.make_async_remote_copy(
                u_hbm.at[:, plies - 1], ply_halo.at[0], sems.at[4], sems.at[8],
                device_id=peers[3], device_id_type=MESH),
        )
        for cond, cp in zip(has, copies):
            pl.when(cond)(cp.start)

        r = lax.broadcasted_iota(jnp.int32, (wide, rows), 0) + (x0 - 3)
        c = lax.broadcasted_iota(jnp.int32, (wide, rows), 1)
        own_x = (r >= 0) & (r < x_total)
        mass = jnp.zeros((wide, rows), jnp.float32)
        for a, b, length, column in bonds:
            ok = own_x & (r + a >= 0) & (r + a < x_total) & (c + b >= 0) & (c + b < rows)
            mass = mass + jnp.where(ok, length, 0.0)
        wq_ref[0] = jnp.where(mass > 0, 1.0 / jnp.where(mass > 0, mass, 1.0), 0.0)

        @pl.when(t == 0)
        def _():
            ext[:, :, 0:cols, :] = jnp.zeros((3, plies, cols, rows), jnp.float32)

        @pl.when(t == nt - 1)
        def _():
            ext[:, :, 2 * cols:3 * cols, :] = jnp.zeros((3, plies, cols, rows), jnp.float32)

        @pl.when(q == 0)
        def _():
            ply_halo[0] = jnp.zeros((3, cols, rows), jnp.float32)

        @pl.when(q == nq - 1)
        def _():
            ply_halo[1] = jnp.zeros((3, cols, rows), jnp.float32)

        own.wait()
        pl.when(has[1])(copies[0].wait_recv)
        pl.when(has[0])(copies[1].wait_recv)
        pl.when(has[3])(copies[2].wait_recv)
        pl.when(has[2])(copies[3].wait_recv)

        def masks(n, start):
            r = lax.broadcasted_iota(jnp.int32, (n, rows), 0) + (x0 + start)
            c = lax.broadcasted_iota(jnp.int32, (n, rows), 1)
            own = (r >= 0) & (r < x_total)
            xm = {a: own & (r + a >= 0) & (r + a < x_total) for a in shifts}
            ym = {b: (c + b >= 0) & (c + b < rows) for b in lanes}
            return xm, ym

        base = cols - 3

        def ply_body(p, carry):
            xm, ym = masks(wide, -3)
            w = wq_ref[0]
            ud = [ext[k, p, base:base + wide, :] for k in range(3)]
            dil = jnp.zeros((wide, rows), jnp.float32)
            for a, b, length, column in bonds:
                nb = [shift_lanes(ext[k, p, base + a:base + a + wide, :], b) for k in range(3)]
                sx = (nb[0] - ud[0]) + a
                sy = (nb[1] - ud[1]) + b
                sz = nb[2] - ud[2]
                span = jnp.sqrt(sx * sx + sy * sy + sz * sz)
                dil = dil + jnp.where(xm[a] & ym[b], span - length, 0.0)
            theta = 3.0 * dil * w
            wq_ref[1] = theta * w

            xm, ym = masks(cols, 0)
            uc = [ext[k, p, cols:2 * cols, :] for k in range(3)]
            wi = wq_ref[0, 3:3 + cols, :]
            qi = wq_ref[1, 3:3 + cols, :]
            fx = jnp.zeros((cols, rows), jnp.float32)
            fy = jnp.zeros((cols, rows), jnp.float32)
            fz = jnp.zeros((cols, rows), jnp.float32)
            for a, b, length, column in bonds:
                nb = [shift_lanes(ext[k, p, cols + a:2 * cols + a, :], b) for k in range(3)]
                wj = shift_lanes(wq_ref[0, 3 + a:3 + a + cols, :], b)
                qj = shift_lanes(wq_ref[1, 3 + a:3 + a + cols, :], b)
                sx = (nb[0] - uc[0]) + a
                sy = (nb[1] - uc[1]) + b
                sz = nb[2] - uc[2]
                span = jnp.sqrt(sx * sx + sy * sy + sz * sz)
                alpha = coef_ref[p, column]
                beta = coef_ref[p, nbond + column]
                tb = alpha * (span - length) * (wi + wj) + beta * (qi + qj)
                f = jnp.where(xm[a] & ym[b], tb / span, 0.0)
                fx = fx + f * sx
                fy = fy + f * sy
                fz = fz + f * sz
            above = coef_ref[p, 2 * nbond]
            below = coef_ref[p, 2 * nbond + 1]
            hi_p = jnp.minimum(p + 1, plies - 1)
            lo_p = jnp.maximum(p - 1, 0)
            for k, fk in enumerate((fx, fy, fz)):
                hi = jnp.where(p == plies - 1, ply_halo[1, k], ext[k, hi_p, cols:2 * cols, :])
                lo = jnp.where(p == 0, ply_halo[0, k], ext[k, lo_p, cols:2 * cols, :])
                o_ref[k, p] = fk + (above * (hi - uc[k]) + below * (lo - uc[k]))
            return carry

        lax.fori_loop(0, plies, ply_body, 0)
        for cond, cp in zip(has, copies):
            pl.when(cond)(cp.wait_send)

    return kernel


def local(displacement, angle_index, bond_table, interface_stiffness):
    comp_count, ply_count, col_count, row_count = displacement.shape
    nbond = bond_table.shape[1]
    x_total = col_count * lax.axis_size("tile")
    lengths = [0.0] * nbond
    for a, b, length, column in bond_list():
        lengths[column] = length
    lengths = jnp.asarray(lengths, jnp.float32)
    selector = (
        angle_index[:, None] == jnp.arange(bond_table.shape[0], dtype=jnp.int32)[None, :]
    ).astype(jnp.float32)
    shear = jnp.dot(selector, bond_table, precision=lax.Precision.HIGHEST)
    alpha = 15.0 * shear / lengths[None, :]
    beta = 3.0 * bulk_modulus - 5.0 * shear
    zero_end = jnp.zeros((1,), jnp.float32)
    coupling = jnp.concatenate([zero_end, interface_stiffness, zero_end])
    local_coupling = lax.dynamic_slice_in_dim(
        coupling, lax.axis_index("ply") * ply_count, ply_count + 1
    )
    coef = jnp.concatenate(
        [alpha, beta, local_coupling[1:, None], local_coupling[:-1, None]], axis=1
    )
    kernel = make_kernel(ply_count, col_count, row_count, x_total, nbond)
    return pl.pallas_call(
        kernel,
        in_specs=[
            pl.BlockSpec(memory_space=pltpu.SMEM),
            pl.BlockSpec(memory_space=pl.ANY),
        ],
        out_specs=pl.BlockSpec(memory_space=pltpu.VMEM),
        out_shape=jax.ShapeDtypeStruct(displacement.shape, jnp.float32),
        scratch_shapes=[
            pltpu.VMEM((3, ply_count, 3 * col_count, row_count), jnp.float32),
            pltpu.VMEM((2, 3, col_count, row_count), jnp.float32),
            pltpu.VMEM((2, col_count + 6, row_count), jnp.float32),
            pltpu.SemaphoreType.DMA((9,)),
        ],
        compiler_params=pltpu.CompilerParams(collective_id=0, has_side_effects=True),
    )(coef, displacement)


def solution(mesh):
    placed = (P(None, "ply", "tile", None), P("ply"), P(), P())
    return jax.shard_map(
        local, mesh=mesh, in_specs=placed, out_specs=P(None, "ply", "tile", None), check_vma=False
    )
```

```python
import math

import jax
import jax.numpy as jnp
from jax import lax
from jax.experimental import pallas as pl
from jax.experimental.pallas import tpu as pltpu
from jax.sharding import PartitionSpec as P

bulk_modulus = 40.0


def bond_list():
    halves = []
    for shift_x in range(-3, 4):
        for shift_y in range(-3, 4):
            radius = shift_x * shift_x + shift_y * shift_y
            if 0 < radius <= 9 and (shift_x > 0 or (shift_x == 0 and shift_y > 0)):
                halves.append((shift_x, shift_y))
    result = []
    for shift_x in range(-3, 4):
        for shift_y in range(-3, 4):
            radius = shift_x * shift_x + shift_y * shift_y
            if 0 < radius <= 9:
                if (shift_x, shift_y) in halves:
                    column = halves.index((shift_x, shift_y))
                else:
                    column = halves.index((-shift_x, -shift_y))
                result.append((shift_x, shift_y, math.sqrt(radius), column))
    return result


def halo(shard, axis, dim, width):
    peers, length = lax.axis_size(axis), shard.shape[dim]
    up = [(i, (i + 1) % peers) for i in range(peers)]
    down = [(j, i) for i, j in up]
    last = lax.slice_in_dim(shard, length - width, length, axis=dim)
    first = lax.slice_in_dim(shard, 0, width, axis=dim)
    before = lax.ppermute(last, axis, up)
    after = lax.ppermute(first, axis, down)
    return jnp.concatenate([before, shard, after], axis=dim)


def shift_lanes(x, b):
    if b == 0:
        return x
    return pltpu.roll(x, (-b) % x.shape[-1], 1)


MESH = pl.DeviceIdType.MESH


def make_kernel(plies, cols, rows, x_total, nbond):
    bonds = bond_list()
    wide = cols + 6
    shifts = sorted({a for a, _, _, _ in bonds})
    lanes = sorted({b for _, b, _, _ in bonds})

    def kernel(coef_ref, u_hbm, o_ref, ext, ply_halo, wq_ref, sems, send_t, recv_t):
        t = lax.axis_index("tile")
        nt = lax.axis_size("tile")
        q = lax.axis_index("ply")
        nq = lax.axis_size("ply")
        x0 = t * cols
        own = pltpu.make_async_copy(u_hbm, ext.at[:, :, cols:2 * cols, :], sems.at[0])
        own.start()
        has = ((t > 0), (t < nt - 1), (q > 0), (q < nq - 1))
        peers = ({"tile": t - 1}, {"tile": t + 1}, {"ply": q - 1}, {"ply": q + 1})
        barrier = pltpu.get_barrier_semaphore()
        for cond, dev in zip(has, peers):
            @pl.when(cond)
            def _():
                pl.semaphore_signal(barrier, inc=1, device_id=dev, device_id_type=MESH)
        count = sum(c.astype(jnp.int32) for c in has)
        pl.semaphore_wait(barrier, count)
        def tile_copy(d, p):
            rows_at = slice(2 * cols, 3 * cols) if d == 0 else slice(0, cols)
            return pltpu.make_async_remote_copy(
                u_hbm.at[:, p], ext.at[:, p, rows_at, :], send_t.at[d, p], recv_t.at[d, p],
                device_id=peers[d], device_id_type=MESH)

        ply_copies = (
            pltpu.make_async_remote_copy(
                u_hbm.at[:, 0], ply_halo.at[1], sems.at[1], sems.at[3],
                device_id=peers[2], device_id_type=MESH),
            pltpu.make_async_remote_copy(
                u_hbm.at[:, plies - 1], ply_halo.at[0], sems.at[2], sems.at[4],
                device_id=peers[3], device_id_type=MESH),
        )
        ahead = min(2, plies)
        for p in range(ahead):
            for d in range(2):
                pl.when(has[d])(tile_copy(d, p).start)
        for cond, cp in zip(has[2:], ply_copies):
            pl.when(cond)(cp.start)

        r = lax.broadcasted_iota(jnp.int32, (wide, rows), 0) + (x0 - 3)
        c = lax.broadcasted_iota(jnp.int32, (wide, rows), 1)
        own_x = (r >= 0) & (r < x_total)
        mass = jnp.zeros((wide, rows), jnp.float32)
        for a, b, length, column in bonds:
            ok = own_x & (r + a >= 0) & (r + a < x_total) & (c + b >= 0) & (c + b < rows)
            mass = mass + jnp.where(ok, length, 0.0)
        wq_ref[0] = jnp.where(mass > 0, 1.0 / jnp.where(mass > 0, mass, 1.0), 0.0)

        @pl.when(t == 0)
        def _():
            ext[:, :, 0:cols, :] = jnp.zeros((3, plies, cols, rows), jnp.float32)

        @pl.when(t == nt - 1)
        def _():
            ext[:, :, 2 * cols:3 * cols, :] = jnp.zeros((3, plies, cols, rows), jnp.float32)

        @pl.when(q == 0)
        def _():
            ply_halo[0] = jnp.zeros((3, cols, rows), jnp.float32)

        @pl.when(q == nq - 1)
        def _():
            ply_halo[1] = jnp.zeros((3, cols, rows), jnp.float32)

        own.wait()

        def masks(n, start):
            r = lax.broadcasted_iota(jnp.int32, (n, rows), 0) + (x0 + start)
            c = lax.broadcasted_iota(jnp.int32, (n, rows), 1)
            own = (r >= 0) & (r < x_total)
            xm = {a: own & (r + a >= 0) & (r + a < x_total) for a in shifts}
            ym = {b: (c + b >= 0) & (c + b < rows) for b in lanes}
            return xm, ym

        base = cols - 3

        def ply_body(p, carry):
            for d in range(2):
                pl.when(has[d] & (p + ahead < plies))(
                    lambda d=d: tile_copy(d, jnp.minimum(p + ahead, plies - 1)).start())
            pl.when(has[1])(tile_copy(0, p).wait_recv)
            pl.when(has[0])(tile_copy(1, p).wait_recv)
            xm, ym = masks(wide, -3)
            w = wq_ref[0]
            ud = [ext[k, p, base:base + wide, :] for k in range(3)]
            dil = jnp.zeros((wide, rows), jnp.float32)
            for a, b, length, column in bonds:
                nb = [shift_lanes(ext[k, p, base + a:base + a + wide, :], b) for k in range(3)]
                sx = (nb[0] - ud[0]) + a
                sy = (nb[1] - ud[1]) + b
                sz = nb[2] - ud[2]
                span = jnp.sqrt(sx * sx + sy * sy + sz * sz)
                dil = dil + jnp.where(xm[a] & ym[b], span - length, 0.0)
            theta = 3.0 * dil * w
            wq_ref[1] = theta * w

            xm, ym = masks(cols, 0)
            uc = [ext[k, p, cols:2 * cols, :] for k in range(3)]
            wi = wq_ref[0, 3:3 + cols, :]
            qi = wq_ref[1, 3:3 + cols, :]
            fx = jnp.zeros((cols, rows), jnp.float32)
            fy = jnp.zeros((cols, rows), jnp.float32)
            fz = jnp.zeros((cols, rows), jnp.float32)
            for a, b, length, column in bonds:
                nb = [shift_lanes(ext[k, p, cols + a:2 * cols + a, :], b) for k in range(3)]
                wj = shift_lanes(wq_ref[0, 3 + a:3 + a + cols, :], b)
                qj = shift_lanes(wq_ref[1, 3 + a:3 + a + cols, :], b)
                sx = (nb[0] - uc[0]) + a
                sy = (nb[1] - uc[1]) + b
                sz = nb[2] - uc[2]
                span = jnp.sqrt(sx * sx + sy * sy + sz * sz)
                alpha = coef_ref[p, column]
                beta = coef_ref[p, nbond + column]
                tb = alpha * (span - length) * (wi + wj) + beta * (qi + qj)
                f = jnp.where(xm[a] & ym[b], tb / span, 0.0)
                fx = fx + f * sx
                fy = fy + f * sy
                fz = fz + f * sz
            above = coef_ref[p, 2 * nbond]
            below = coef_ref[p, 2 * nbond + 1]
            hi_p = jnp.minimum(p + 1, plies - 1)
            lo_p = jnp.maximum(p - 1, 0)
            for k, fk in enumerate((fx, fy, fz)):
                hi = jnp.where(p == plies - 1, uc[k], ext[k, hi_p, cols:2 * cols, :])
                lo = jnp.where(p == 0, uc[k], ext[k, lo_p, cols:2 * cols, :])
                o_ref[k, p] = fk + (above * (hi - uc[k]) + below * (lo - uc[k]))
            return carry

        lax.fori_loop(0, plies, ply_body, 0)
        pl.when(has[3])(ply_copies[0].wait_recv)
        pl.when(has[2])(ply_copies[1].wait_recv)
        below = coef_ref[0, 2 * nbond + 1]
        above = coef_ref[plies - 1, 2 * nbond]
        for k in range(3):
            o_ref[k, 0] = o_ref[k, 0] + below * (ply_halo[0, k] - ext[k, 0, cols:2 * cols, :])
            o_ref[k, plies - 1] = o_ref[k, plies - 1] + above * (
                ply_halo[1, k] - ext[k, plies - 1, cols:2 * cols, :])
        for p in range(plies):
            for d in range(2):
                pl.when(has[d])(tile_copy(d, p).wait_send)
        for cond, cp in zip(has[2:], ply_copies):
            pl.when(cond)(cp.wait_send)

    return kernel


def local(displacement, angle_index, bond_table, interface_stiffness):
    comp_count, ply_count, col_count, row_count = displacement.shape
    nbond = bond_table.shape[1]
    x_total = col_count * lax.axis_size("tile")
    lengths = [0.0] * nbond
    for a, b, length, column in bond_list():
        lengths[column] = length
    lengths = jnp.asarray(lengths, jnp.float32)
    selector = (
        angle_index[:, None] == jnp.arange(bond_table.shape[0], dtype=jnp.int32)[None, :]
    ).astype(jnp.float32)
    shear = jnp.dot(selector, bond_table, precision=lax.Precision.HIGHEST)
    alpha = 15.0 * shear / lengths[None, :]
    beta = 3.0 * bulk_modulus - 5.0 * shear
    zero_end = jnp.zeros((1,), jnp.float32)
    coupling = jnp.concatenate([zero_end, interface_stiffness, zero_end])
    local_coupling = lax.dynamic_slice_in_dim(
        coupling, lax.axis_index("ply") * ply_count, ply_count + 1
    )
    coef = jnp.concatenate(
        [alpha, beta, local_coupling[1:, None], local_coupling[:-1, None]], axis=1
    )
    kernel = make_kernel(ply_count, col_count, row_count, x_total, nbond)
    return pl.pallas_call(
        kernel,
        in_specs=[
            pl.BlockSpec(memory_space=pltpu.SMEM),
            pl.BlockSpec(memory_space=pl.ANY),
        ],
        out_specs=pl.BlockSpec(memory_space=pltpu.VMEM),
        out_shape=jax.ShapeDtypeStruct(displacement.shape, jnp.float32),
        scratch_shapes=[
            pltpu.VMEM((3, ply_count, 3 * col_count, row_count), jnp.float32),
            pltpu.VMEM((2, 3, col_count, row_count), jnp.float32),
            pltpu.VMEM((2, col_count + 6, row_count), jnp.float32),
            pltpu.SemaphoreType.DMA((5,)),
            pltpu.SemaphoreType.DMA((2, ply_count)),
            pltpu.SemaphoreType.DMA((2, ply_count)),
        ],
        compiler_params=pltpu.CompilerParams(collective_id=0, has_side_effects=True),
    )(coef, displacement)


def solution(mesh):
    placed = (P(None, "ply", "tile", None), P("ply"), P(), P())
    return jax.shard_map(
        local, mesh=mesh, in_specs=placed, out_specs=P(None, "ply", "tile", None), check_vma=False
    )
```

```python
import math

import jax
import jax.numpy as jnp
from jax import lax
from jax.experimental import pallas as pl
from jax.experimental.pallas import tpu as pltpu
from jax.sharding import PartitionSpec as P

bulk_modulus = 40.0


def bond_list():
    halves = []
    for shift_x in range(-3, 4):
        for shift_y in range(-3, 4):
            radius = shift_x * shift_x + shift_y * shift_y
            if 0 < radius <= 9 and (shift_x > 0 or (shift_x == 0 and shift_y > 0)):
                halves.append((shift_x, shift_y))
    result = []
    for shift_x in range(-3, 4):
        for shift_y in range(-3, 4):
            radius = shift_x * shift_x + shift_y * shift_y
            if 0 < radius <= 9:
                if (shift_x, shift_y) in halves:
                    column = halves.index((shift_x, shift_y))
                else:
                    column = halves.index((-shift_x, -shift_y))
                result.append((shift_x, shift_y, math.sqrt(radius), column))
    return result


def halo(shard, axis, dim, width):
    peers, length = lax.axis_size(axis), shard.shape[dim]
    up = [(i, (i + 1) % peers) for i in range(peers)]
    down = [(j, i) for i, j in up]
    last = lax.slice_in_dim(shard, length - width, length, axis=dim)
    first = lax.slice_in_dim(shard, 0, width, axis=dim)
    before = lax.ppermute(last, axis, up)
    after = lax.ppermute(first, axis, down)
    return jnp.concatenate([before, shard, after], axis=dim)


def shift_lanes(x, b):
    if b == 0:
        return x
    return pltpu.roll(x, (-b) % x.shape[-1], 1)


MESH = pl.DeviceIdType.MESH


def make_kernel(plies, cols, rows, x_total, nsprings):
    bonds = bond_list()
    wide = cols + 6
    shifts = sorted({a for a, _, _, _ in bonds})
    lanes = sorted({b for _, b, _, _ in bonds})

    def kernel(angle_ref, table_ref, spring_ref, u_hbm, o_ref, ext, ply_halo, wq_ref, dmask_ref,
               fmask_ref, sems, send_t, recv_t):
        t = lax.axis_index("tile")
        nt = lax.axis_size("tile")
        q = lax.axis_index("ply")
        nq = lax.axis_size("ply")
        x0 = t * cols
        own = pltpu.make_async_copy(u_hbm, ext.at[:, :, cols:2 * cols, :], sems.at[0])
        own.start()
        has = ((t > 0), (t < nt - 1), (q > 0), (q < nq - 1))
        peers = ({"tile": t - 1}, {"tile": t + 1}, {"ply": q - 1}, {"ply": q + 1})
        barrier = pltpu.get_barrier_semaphore()
        for cond, dev in zip(has, peers):
            @pl.when(cond)
            def _():
                pl.semaphore_signal(barrier, inc=1, device_id=dev, device_id_type=MESH)
        count = sum(c.astype(jnp.int32) for c in has)
        pl.semaphore_wait(barrier, count)
        def tile_copy(d, p):
            rows_at = slice(2 * cols, 3 * cols) if d == 0 else slice(0, cols)
            return pltpu.make_async_remote_copy(
                u_hbm.at[:, p], ext.at[:, p, rows_at, :], send_t.at[d, p], recv_t.at[d, p],
                device_id=peers[d], device_id_type=MESH)

        ply_copies = (
            pltpu.make_async_remote_copy(
                u_hbm.at[:, 0], ply_halo.at[1], sems.at[1], sems.at[3],
                device_id=peers[2], device_id_type=MESH),
            pltpu.make_async_remote_copy(
                u_hbm.at[:, plies - 1], ply_halo.at[0], sems.at[2], sems.at[4],
                device_id=peers[3], device_id_type=MESH),
        )
        ahead = min(2, plies)
        for p in range(ahead):
            for d in range(2):
                pl.when(has[d])(tile_copy(d, p).start)
        for cond, cp in zip(has[2:], ply_copies):
            pl.when(cond)(cp.start)

        def bond_masks(n, start, out_ref):
            r = lax.broadcasted_iota(jnp.int32, (n, rows), 0) + (x0 + start)
            c = lax.broadcasted_iota(jnp.int32, (n, rows), 1)
            own_x = (r >= 0) & (r < x_total)
            total = jnp.zeros((n, rows), jnp.float32)
            for i, (a, b, length, column) in enumerate(bonds):
                ok = own_x & (r + a >= 0) & (r + a < x_total) & (c + b >= 0) & (c + b < rows)
                m = jnp.where(ok, 1.0, 0.0)
                out_ref[i] = m
                total = total + m * length
            return total

        mass = bond_masks(wide, -3, dmask_ref)
        bond_masks(cols, 0, fmask_ref)
        wq_ref[0] = jnp.where(mass > 0, 1.0 / jnp.where(mass > 0, mass, 1.0), 0.0)

        @pl.when(t == 0)
        def _():
            ext[:, :, 0:cols, :] = jnp.zeros((3, plies, cols, rows), jnp.float32)

        @pl.when(t == nt - 1)
        def _():
            ext[:, :, 2 * cols:3 * cols, :] = jnp.zeros((3, plies, cols, rows), jnp.float32)

        @pl.when(q == 0)
        def _():
            ply_halo[0] = jnp.zeros((3, cols, rows), jnp.float32)

        @pl.when(q == nq - 1)
        def _():
            ply_halo[1] = jnp.zeros((3, cols, rows), jnp.float32)

        own.wait()

        def masks(n, start):
            r = lax.broadcasted_iota(jnp.int32, (n, rows), 0) + (x0 + start)
            c = lax.broadcasted_iota(jnp.int32, (n, rows), 1)
            own = (r >= 0) & (r < x_total)
            xm = {a: own & (r + a >= 0) & (r + a < x_total) for a in shifts}
            ym = {b: (c + b >= 0) & (c + b < rows) for b in lanes}
            return xm, ym

        base = cols - 3

        groups = {}
        for i, (a, b, length, column) in enumerate(bonds):
            groups.setdefault(a, []).append((i, b, length, column))

        def ply_body(p, carry):
            for d in range(2):
                pl.when(has[d] & (p + ahead < plies))(
                    lambda d=d: tile_copy(d, jnp.minimum(p + ahead, plies - 1)).start())
            pl.when(has[1])(tile_copy(0, p).wait_recv)
            pl.when(has[0])(tile_copy(1, p).wait_recv)
            gp = q * plies + p
            kind = angle_ref[p]
            w = wq_ref[0]
            ud = [ext[k, p, base:base + wide, :] for k in range(3)]
            ud_y = {b: ud[1] - b for b in lanes}
            dil = jnp.zeros((wide, rows), jnp.float32)
            for a, members in groups.items():
                slab = [ext[k, p, base + a:base + a + wide, :] for k in range(3)]
                ud_x = ud[0] - a
                for i, b, length, column in members:
                    sx = shift_lanes(slab[0], b) - ud_x
                    sy = shift_lanes(slab[1], b) - ud_y[b]
                    sz = shift_lanes(slab[2], b) - ud[2]
                    s2 = sx * sx + sy * sy + sz * sz
                    span = s2 * lax.rsqrt(s2)
                    dil = dil + (span - length) * dmask_ref[i]
            theta = 3.0 * dil * w
            wq_ref[1] = theta * w

            uc = [ext[k, p, cols:2 * cols, :] for k in range(3)]
            uc_y = {b: uc[1] - b for b in lanes}
            wi = wq_ref[0, 3:3 + cols, :]
            qi = wq_ref[1, 3:3 + cols, :]
            fx = jnp.zeros((cols, rows), jnp.float32)
            fy = jnp.zeros((cols, rows), jnp.float32)
            fz = jnp.zeros((cols, rows), jnp.float32)
            for a, members in groups.items():
                slab = [ext[k, p, cols + a:2 * cols + a, :] for k in range(3)]
                w_slab = wq_ref[0, 3 + a:3 + a + cols, :]
                q_slab = wq_ref[1, 3 + a:3 + a + cols, :]
                uc_x = uc[0] - a
                for i, b, length, column in members:
                    sx = shift_lanes(slab[0], b) - uc_x
                    sy = shift_lanes(slab[1], b) - uc_y[b]
                    sz = shift_lanes(slab[2], b) - uc[2]
                    s2 = sx * sx + sy * sy + sz * sz
                    inv = lax.rsqrt(s2)
                    span = s2 * inv
                    shear = table_ref[kind, column]
                    alpha = shear * (15.0 / length)
                    beta = 3.0 * bulk_modulus - 5.0 * shear
                    tb = alpha * (span - length) * (wi + shift_lanes(w_slab, b)) + beta * (
                        qi + shift_lanes(q_slab, b))
                    f = (tb * inv) * fmask_ref[i]
                    fx = fx + f * sx
                    fy = fy + f * sy
                    fz = fz + f * sz
            above = jnp.where(gp < nsprings, spring_ref[jnp.minimum(gp, nsprings - 1)], 0.0)
            below = jnp.where(gp > 0, spring_ref[jnp.maximum(gp - 1, 0)], 0.0)
            hi_p = jnp.minimum(p + 1, plies - 1)
            lo_p = jnp.maximum(p - 1, 0)
            for k, fk in enumerate((fx, fy, fz)):
                hi = jnp.where(p == plies - 1, uc[k], ext[k, hi_p, cols:2 * cols, :])
                lo = jnp.where(p == 0, uc[k], ext[k, lo_p, cols:2 * cols, :])
                o_ref[k, p] = fk + (above * (hi - uc[k]) + below * (lo - uc[k]))
            return carry

        lax.fori_loop(0, plies, ply_body, 0)
        pl.when(has[3])(ply_copies[0].wait_recv)
        pl.when(has[2])(ply_copies[1].wait_recv)
        g0 = q * plies
        below = jnp.where(g0 > 0, spring_ref[jnp.maximum(g0 - 1, 0)], 0.0)
        gl = q * plies + plies - 1
        above = jnp.where(gl < nsprings, spring_ref[jnp.minimum(gl, nsprings - 1)], 0.0)
        for k in range(3):
            o_ref[k, 0] = o_ref[k, 0] + below * (ply_halo[0, k] - ext[k, 0, cols:2 * cols, :])
            o_ref[k, plies - 1] = o_ref[k, plies - 1] + above * (
                ply_halo[1, k] - ext[k, plies - 1, cols:2 * cols, :])
        for p in range(plies):
            for d in range(2):
                pl.when(has[d])(tile_copy(d, p).wait_send)
        for cond, cp in zip(has[2:], ply_copies):
            pl.when(cond)(cp.wait_send)

    return kernel


def local(displacement, angle_index, bond_table, interface_stiffness):
    comp_count, ply_count, col_count, row_count = displacement.shape
    x_total = col_count * lax.axis_size("tile")
    kernel = make_kernel(ply_count, col_count, row_count, x_total, interface_stiffness.shape[0])
    nbond = len(bond_list())
    smem = pl.BlockSpec(memory_space=pltpu.SMEM)
    return pl.pallas_call(
        kernel,
        in_specs=[smem, smem, smem, pl.BlockSpec(memory_space=pl.ANY)],
        out_specs=pl.BlockSpec(memory_space=pltpu.VMEM),
        out_shape=jax.ShapeDtypeStruct(displacement.shape, jnp.float32),
        scratch_shapes=[
            pltpu.VMEM((3, ply_count, 3 * col_count, row_count), jnp.float32),
            pltpu.VMEM((2, 3, col_count, row_count), jnp.float32),
            pltpu.VMEM((2, col_count + 6, row_count), jnp.float32),
            pltpu.VMEM((nbond, col_count + 6, row_count), jnp.float32),
            pltpu.VMEM((nbond, col_count, row_count), jnp.float32),
            pltpu.SemaphoreType.DMA((5,)),
            pltpu.SemaphoreType.DMA((2, ply_count)),
            pltpu.SemaphoreType.DMA((2, ply_count)),
        ],
        compiler_params=pltpu.CompilerParams(collective_id=0, has_side_effects=True),
    )(angle_index, bond_table, interface_stiffness, displacement)


def solution(mesh):
    placed = (P(None, "ply", "tile", None), P("ply"), P(), P())
    return jax.shard_map(
        local, mesh=mesh, in_specs=placed, out_specs=P(None, "ply", "tile", None), check_vma=False
    )
```

```python
import math

import jax
import jax.numpy as jnp
from jax import lax
from jax.experimental import pallas as pl
from jax.experimental.pallas import tpu as pltpu
from jax.sharding import PartitionSpec as P

bulk_modulus = 40.0


def bond_list():
    halves = []
    for shift_x in range(-3, 4):
        for shift_y in range(-3, 4):
            radius = shift_x * shift_x + shift_y * shift_y
            if 0 < radius <= 9 and (shift_x > 0 or (shift_x == 0 and shift_y > 0)):
                halves.append((shift_x, shift_y))
    result = []
    for shift_x in range(-3, 4):
        for shift_y in range(-3, 4):
            radius = shift_x * shift_x + shift_y * shift_y
            if 0 < radius <= 9:
                if (shift_x, shift_y) in halves:
                    column = halves.index((shift_x, shift_y))
                else:
                    column = halves.index((-shift_x, -shift_y))
                result.append((shift_x, shift_y, math.sqrt(radius), column))
    return result


def halo(shard, axis, dim, width):
    peers, length = lax.axis_size(axis), shard.shape[dim]
    up = [(i, (i + 1) % peers) for i in range(peers)]
    down = [(j, i) for i, j in up]
    last = lax.slice_in_dim(shard, length - width, length, axis=dim)
    first = lax.slice_in_dim(shard, 0, width, axis=dim)
    before = lax.ppermute(last, axis, up)
    after = lax.ppermute(first, axis, down)
    return jnp.concatenate([before, shard, after], axis=dim)


def shift_lanes(x, b):
    if b == 0:
        return x
    return pltpu.roll(x, (-b) % x.shape[-1], 1)


MESH = pl.DeviceIdType.MESH


def make_kernel(plies, cols, rows, x_total, nsprings):
    bonds = bond_list()
    wide = cols + 6
    shifts = sorted({a for a, _, _, _ in bonds})
    lanes = sorted({b for _, b, _, _ in bonds})

    def kernel(angle_ref, table_ref, spring_ref, u_hbm, o_ref, edge_ref, ext, ply_halo, wq_ref, dmask_ref,
               fmask_ref, sems, send_t, recv_t):
        t = lax.axis_index("tile")
        nt = lax.axis_size("tile")
        q = lax.axis_index("ply")
        nq = lax.axis_size("ply")
        x0 = t * cols
        own = pltpu.make_async_copy(u_hbm, ext.at[:, :, cols:2 * cols, :], sems.at[0])
        own.start()
        has = ((t > 0), (t < nt - 1), (q > 0), (q < nq - 1))
        peers = ({"tile": t - 1}, {"tile": t + 1}, {"ply": q - 1}, {"ply": q + 1})
        barrier = pltpu.get_barrier_semaphore()
        for cond, dev in zip(has, peers):
            @pl.when(cond)
            def _():
                pl.semaphore_signal(barrier, inc=1, device_id=dev, device_id_type=MESH)
        count = sum(c.astype(jnp.int32) for c in has)
        pl.semaphore_wait(barrier, count)
        def tile_copy(d, p):
            rows_at = slice(2 * cols, 3 * cols) if d == 0 else slice(0, cols)
            return pltpu.make_async_remote_copy(
                u_hbm.at[:, p], ext.at[:, p, rows_at, :], send_t.at[d, p], recv_t.at[d, p],
                device_id=peers[d], device_id_type=MESH)

        ply_copies = (
            pltpu.make_async_remote_copy(
                u_hbm.at[:, 0], ply_halo.at[1], sems.at[1], sems.at[3],
                device_id=peers[2], device_id_type=MESH),
            pltpu.make_async_remote_copy(
                u_hbm.at[:, plies - 1], ply_halo.at[0], sems.at[2], sems.at[4],
                device_id=peers[3], device_id_type=MESH),
        )
        ahead = min(2, plies)
        for p in range(ahead):
            for d in range(2):
                pl.when(has[d])(tile_copy(d, p).start)
        for cond, cp in zip(has[2:], ply_copies):
            pl.when(cond)(cp.start)

        def bond_masks(n, start, out_ref):
            r = lax.broadcasted_iota(jnp.int32, (n, rows), 0) + (x0 + start)
            c = lax.broadcasted_iota(jnp.int32, (n, rows), 1)
            own_x = (r >= 0) & (r < x_total)
            total = jnp.zeros((n, rows), jnp.float32)
            for i, (a, b, length, column) in enumerate(bonds):
                ok = own_x & (r + a >= 0) & (r + a < x_total) & (c + b >= 0) & (c + b < rows)
                m = jnp.where(ok, 1.0, 0.0)
                out_ref[i] = m
                total = total + m * length
            return total

        mass = bond_masks(wide, -3, dmask_ref)
        bond_masks(cols, 0, fmask_ref)
        wq_ref[0] = jnp.where(mass > 0, 1.0 / jnp.where(mass > 0, mass, 1.0), 0.0)

        @pl.when(t == 0)
        def _():
            ext[:, :, 0:cols, :] = jnp.zeros((3, plies, cols, rows), jnp.float32)

        @pl.when(t == nt - 1)
        def _():
            ext[:, :, 2 * cols:3 * cols, :] = jnp.zeros((3, plies, cols, rows), jnp.float32)

        @pl.when(q == 0)
        def _():
            ply_halo[0] = jnp.zeros((3, cols, rows), jnp.float32)

        @pl.when(q == nq - 1)
        def _():
            ply_halo[1] = jnp.zeros((3, cols, rows), jnp.float32)

        own.wait()

        def masks(n, start):
            r = lax.broadcasted_iota(jnp.int32, (n, rows), 0) + (x0 + start)
            c = lax.broadcasted_iota(jnp.int32, (n, rows), 1)
            own = (r >= 0) & (r < x_total)
            xm = {a: own & (r + a >= 0) & (r + a < x_total) for a in shifts}
            ym = {b: (c + b >= 0) & (c + b < rows) for b in lanes}
            return xm, ym

        base = cols - 3

        groups = {}
        for i, (a, b, length, column) in enumerate(bonds):
            groups.setdefault(a, []).append((i, b, length, column))

        def ply_body(p, carry):
            for d in range(2):
                pl.when(has[d] & (p + ahead < plies))(
                    lambda d=d: tile_copy(d, jnp.minimum(p + ahead, plies - 1)).start())
            pl.when(has[1])(tile_copy(0, p).wait_recv)
            pl.when(has[0])(tile_copy(1, p).wait_recv)
            gp = q * plies + p
            kind = angle_ref[p]
            w = wq_ref[0]
            ud = [ext[k, p, base:base + wide, :] for k in range(3)]
            ud_y = {b: ud[1] - b for b in lanes}
            dil = jnp.zeros((wide, rows), jnp.float32)
            for a, members in groups.items():
                slab = [ext[k, p, base + a:base + a + wide, :] for k in range(3)]
                ud_x = ud[0] - a
                for i, b, length, column in members:
                    sx = shift_lanes(slab[0], b) - ud_x
                    sy = shift_lanes(slab[1], b) - ud_y[b]
                    sz = shift_lanes(slab[2], b) - ud[2]
                    s2 = sx * sx + sy * sy + sz * sz
                    span = s2 * lax.rsqrt(s2)
                    dil = dil + (span - length) * dmask_ref[i]
            theta = 3.0 * dil * w
            wq_ref[1] = theta * w

            uc = [ext[k, p, cols:2 * cols, :] for k in range(3)]
            uc_y = {b: uc[1] - b for b in lanes}
            wi = wq_ref[0, 3:3 + cols, :]
            qi = wq_ref[1, 3:3 + cols, :]
            fx = jnp.zeros((cols, rows), jnp.float32)
            fy = jnp.zeros((cols, rows), jnp.float32)
            fz = jnp.zeros((cols, rows), jnp.float32)
            for a, members in groups.items():
                slab = [ext[k, p, cols + a:2 * cols + a, :] for k in range(3)]
                w_slab = wq_ref[0, 3 + a:3 + a + cols, :]
                q_slab = wq_ref[1, 3 + a:3 + a + cols, :]
                uc_x = uc[0] - a
                for i, b, length, column in members:
                    sx = shift_lanes(slab[0], b) - uc_x
                    sy = shift_lanes(slab[1], b) - uc_y[b]
                    sz = shift_lanes(slab[2], b) - uc[2]
                    s2 = sx * sx + sy * sy + sz * sz
                    inv = lax.rsqrt(s2)
                    span = s2 * inv
                    shear = table_ref[kind, column]
                    alpha = shear * (15.0 / length)
                    beta = 3.0 * bulk_modulus - 5.0 * shear
                    tb = alpha * (span - length) * (wi + shift_lanes(w_slab, b)) + beta * (
                        qi + shift_lanes(q_slab, b))
                    f = (tb * inv) * fmask_ref[i]
                    fx = fx + f * sx
                    fy = fy + f * sy
                    fz = fz + f * sz
            above = jnp.where(gp < nsprings, spring_ref[jnp.minimum(gp, nsprings - 1)], 0.0)
            below = jnp.where(gp > 0, spring_ref[jnp.maximum(gp - 1, 0)], 0.0)
            hi_p = jnp.minimum(p + 1, plies - 1)
            lo_p = jnp.maximum(p - 1, 0)
            for k, fk in enumerate((fx, fy, fz)):
                hi = jnp.where(p == plies - 1, uc[k], ext[k, hi_p, cols:2 * cols, :])
                lo = jnp.where(p == 0, uc[k], ext[k, lo_p, cols:2 * cols, :])
                o_ref[k, p] = fk + (above * (hi - uc[k]) + below * (lo - uc[k]))
            return carry

        lax.fori_loop(0, plies, ply_body, 0)
        pl.when(has[3])(ply_copies[0].wait_recv)
        pl.when(has[2])(ply_copies[1].wait_recv)
        g0 = q * plies
        below = jnp.where(g0 > 0, spring_ref[jnp.maximum(g0 - 1, 0)], 0.0)
        gl = q * plies + plies - 1
        above = jnp.where(gl < nsprings, spring_ref[jnp.minimum(gl, nsprings - 1)], 0.0)
        for k in range(3):
            edge_ref[0, k] = below * (ply_halo[0, k] - ext[k, 0, cols:2 * cols, :])
            edge_ref[1, k] = above * (ply_halo[1, k] - ext[k, plies - 1, cols:2 * cols, :])
        for p in range(plies):
            for d in range(2):
                pl.when(has[d])(tile_copy(d, p).wait_send)
        for cond, cp in zip(has[2:], ply_copies):
            pl.when(cond)(cp.wait_send)

    return kernel


def add_edges(force_ref, edge_ref, o_ref):
    plies = force_ref.shape[1]
    o_ref[...] = force_ref[...]
    for k in range(3):
        o_ref[k, 0] = force_ref[k, 0] + edge_ref[0, k]
        o_ref[k, plies - 1] = force_ref[k, plies - 1] + edge_ref[1, k]


def local(displacement, angle_index, bond_table, interface_stiffness):
    comp_count, ply_count, col_count, row_count = displacement.shape
    x_total = col_count * lax.axis_size("tile")
    kernel = make_kernel(ply_count, col_count, row_count, x_total, interface_stiffness.shape[0])
    nbond = len(bond_list())
    smem = pl.BlockSpec(memory_space=pltpu.SMEM)
    vmem = pl.BlockSpec(memory_space=pltpu.VMEM)
    force, edges = pl.pallas_call(
        kernel,
        in_specs=[smem, smem, smem, pl.BlockSpec(memory_space=pl.ANY)],
        out_specs=[vmem, vmem],
        out_shape=[
            jax.ShapeDtypeStruct(displacement.shape, jnp.float32),
            jax.ShapeDtypeStruct((2, 3, col_count, row_count), jnp.float32),
        ],
        scratch_shapes=[
            pltpu.VMEM((3, ply_count, 3 * col_count, row_count), jnp.float32),
            pltpu.VMEM((2, 3, col_count, row_count), jnp.float32),
            pltpu.VMEM((2, col_count + 6, row_count), jnp.float32),
            pltpu.VMEM((nbond, col_count + 6, row_count), jnp.float32),
            pltpu.VMEM((nbond, col_count, row_count), jnp.float32),
            pltpu.SemaphoreType.DMA((5,)),
            pltpu.SemaphoreType.DMA((2, ply_count)),
            pltpu.SemaphoreType.DMA((2, ply_count)),
        ],
        compiler_params=pltpu.CompilerParams(collective_id=0, has_side_effects=True),
    )(angle_index, bond_table, interface_stiffness, displacement)
    return pl.pallas_call(
        add_edges,
        in_specs=[vmem, vmem],
        out_specs=vmem,
        out_shape=jax.ShapeDtypeStruct(displacement.shape, jnp.float32),
    )(force, edges)


def solution(mesh):
    placed = (P(None, "ply", "tile", None), P("ply"), P(), P())
    return jax.shard_map(
        local, mesh=mesh, in_specs=placed, out_specs=P(None, "ply", "tile", None), check_vma=False
    )
```

```python
import math

import jax
import jax.numpy as jnp
from jax import lax
from jax.experimental import pallas as pl
from jax.experimental.pallas import tpu as pltpu
from jax.sharding import PartitionSpec as P

bulk_modulus = 40.0


def bond_list():
    halves = []
    for shift_x in range(-3, 4):
        for shift_y in range(-3, 4):
            radius = shift_x * shift_x + shift_y * shift_y
            if 0 < radius <= 9 and (shift_x > 0 or (shift_x == 0 and shift_y > 0)):
                halves.append((shift_x, shift_y))
    result = []
    for shift_x in range(-3, 4):
        for shift_y in range(-3, 4):
            radius = shift_x * shift_x + shift_y * shift_y
            if 0 < radius <= 9:
                if (shift_x, shift_y) in halves:
                    column = halves.index((shift_x, shift_y))
                else:
                    column = halves.index((-shift_x, -shift_y))
                result.append((shift_x, shift_y, math.sqrt(radius), column))
    return result


def halo(shard, axis, dim, width):
    peers, length = lax.axis_size(axis), shard.shape[dim]
    up = [(i, (i + 1) % peers) for i in range(peers)]
    down = [(j, i) for i, j in up]
    last = lax.slice_in_dim(shard, length - width, length, axis=dim)
    first = lax.slice_in_dim(shard, 0, width, axis=dim)
    before = lax.ppermute(last, axis, up)
    after = lax.ppermute(first, axis, down)
    return jnp.concatenate([before, shard, after], axis=dim)


def shift_lanes(x, b):
    if b == 0:
        return x
    return pltpu.roll(x, (-b) % x.shape[-1], 1)


MESH = pl.DeviceIdType.MESH


def make_kernel(plies, cols, rows, x_total, nsprings):
    bonds = bond_list()
    wide = cols + 6
    shifts = sorted({a for a, _, _, _ in bonds})
    lanes = sorted({b for _, b, _, _ in bonds})

    def kernel(angle_ref, table_ref, spring_ref, u_hbm, o_ref, ext, ply_halo, wq_ref, fmask_ref,
               hmask_ref, wm_ref, sx_ref, sy_ref, sz_ref, pa_ref, pb_ref, sems, send_t, recv_t):
        t = lax.axis_index("tile")
        nt = lax.axis_size("tile")
        q = lax.axis_index("ply")
        nq = lax.axis_size("ply")
        x0 = t * cols
        own = pltpu.make_async_copy(u_hbm, ext.at[:, :, cols:2 * cols, :], sems.at[0])
        own.start()
        has = ((t > 0), (t < nt - 1), (q > 0), (q < nq - 1))
        peers = ({"tile": t - 1}, {"tile": t + 1}, {"ply": q - 1}, {"ply": q + 1})
        barrier = pltpu.get_barrier_semaphore()
        for cond, dev in zip(has, peers):
            @pl.when(cond)
            def _():
                pl.semaphore_signal(barrier, inc=1, device_id=dev, device_id_type=MESH)
        count = sum(c.astype(jnp.int32) for c in has)
        pl.semaphore_wait(barrier, count)
        def tile_copy(d, p):
            rows_at = slice(2 * cols, 3 * cols) if d == 0 else slice(0, cols)
            return pltpu.make_async_remote_copy(
                u_hbm.at[:, p], ext.at[:, p, rows_at, :], send_t.at[d, p], recv_t.at[d, p],
                device_id=peers[d], device_id_type=MESH)

        ply_copies = (
            pltpu.make_async_remote_copy(
                u_hbm.at[:, 0], ply_halo.at[1], sems.at[1], sems.at[3],
                device_id=peers[2], device_id_type=MESH),
            pltpu.make_async_remote_copy(
                u_hbm.at[:, plies - 1], ply_halo.at[0], sems.at[2], sems.at[4],
                device_id=peers[3], device_id_type=MESH),
        )
        ahead = min(2, plies)
        for p in range(ahead):
            for d in range(2):
                pl.when(has[d])(tile_copy(d, p).start)
        for cond, cp in zip(has[2:], ply_copies):
            pl.when(cond)(cp.start)

        sub = lax.broadcasted_iota(jnp.int32, (cols, rows), 0)
        lane = lax.broadcasted_iota(jnp.int32, (cols, rows), 1)
        core_x = sub + x0
        edge_x = jnp.where(sub < 3, x0 - 3 + sub, x0 + cols - 3 + sub)
        edge_ok = sub < 6

        def bond_masks(xg, ok0, out_ref):
            own_x = ok0 & (xg >= 0) & (xg < x_total)
            total = jnp.zeros((cols, rows), jnp.float32)
            for i, (a, b, length, column) in enumerate(bonds):
                ok = own_x & (xg + a >= 0) & (xg + a < x_total) & (lane + b >= 0) & (lane + b < rows)
                m = jnp.where(ok, 1.0, 0.0)
                out_ref[i] = m
                total = total + m * length
            return total

        mass_c = bond_masks(core_x, sub >= 0, fmask_ref)
        mass_e = bond_masks(edge_x, edge_ok, hmask_ref)
        w_c = 1.0 / jnp.where(mass_c > 0, mass_c, 1.0)
        w_e = jnp.where(mass_e > 0, 1.0 / jnp.where(mass_e > 0, mass_e, 1.0), 0.0)
        wq_ref[0, 0:3, :] = w_e[0:3]
        wq_ref[0, 3:3 + cols, :] = w_c
        wq_ref[0, 3 + cols:6 + cols, :] = w_e[3:6]
        groups = {}
        for i, (a, b, length, column) in enumerate(bonds):
            groups.setdefault(a, []).append((i, b, length, column))
        for a, members in groups.items():
            w_slab = wq_ref[0, 3 + a:3 + a + cols, :]
            for i, b, length, column in members:
                wm_ref[i] = fmask_ref[i] * (w_c + shift_lanes(w_slab, b))

        @pl.when(t == 0)
        def _():
            ext[:, :, 0:cols, :] = jnp.zeros((3, plies, cols, rows), jnp.float32)

        @pl.when(t == nt - 1)
        def _():
            ext[:, :, 2 * cols:3 * cols, :] = jnp.zeros((3, plies, cols, rows), jnp.float32)

        @pl.when(q == 0)
        def _():
            ply_halo[0] = jnp.zeros((3, cols, rows), jnp.float32)

        @pl.when(q == nq - 1)
        def _():
            ply_halo[1] = jnp.zeros((3, cols, rows), jnp.float32)

        own.wait()

        def ply_body(p, carry):
            for d in range(2):
                pl.when(has[d] & (p + ahead < plies))(
                    lambda d=d: tile_copy(d, jnp.minimum(p + ahead, plies - 1)).start())
            pl.when(has[1])(tile_copy(0, p).wait_recv)
            pl.when(has[0])(tile_copy(1, p).wait_recv)
            gp = q * plies + p
            kind = angle_ref[p]
            low = lax.broadcasted_iota(jnp.int32, (cols, rows), 0) < 3

            def edge_rows(k, a):
                return jnp.where(low, ext[k, p, cols - 3 + a:2 * cols - 3 + a, :],
                                 ext[k, p, 2 * cols - 3 + a:3 * cols - 3 + a, :])

            uc = [ext[k, p, cols:2 * cols, :] for k in range(3)]
            ue = [edge_rows(k, 0) for k in range(3)]
            uc_y = {b: uc[1] - b for b in lanes}
            ue_y = {b: ue[1] - b for b in lanes}
            dil_c = jnp.zeros((cols, rows), jnp.float32)
            dil_e = jnp.zeros((cols, rows), jnp.float32)
            for a, members in groups.items():
                cs = [ext[k, p, cols + a:2 * cols + a, :] for k in range(3)]
                es = [edge_rows(k, a) for k in range(3)]
                uc_x = uc[0] - a
                ue_x = ue[0] - a
                for i, b, length, column in members:
                    sx = shift_lanes(cs[0], b) - uc_x
                    sy = shift_lanes(cs[1], b) - uc_y[b]
                    sz = shift_lanes(cs[2], b) - uc[2]
                    s2 = sx * sx + sy * sy + sz * sz
                    inv = lax.rsqrt(s2)
                    e = s2 * inv - length
                    m = fmask_ref[i]
                    dil_c = dil_c + e * m
                    sx_ref[i] = sx
                    sy_ref[i] = sy
                    sz_ref[i] = sz
                    pa_ref[i] = (inv * e) * wm_ref[i]
                    pb_ref[i] = inv * m
                    hx = shift_lanes(es[0], b) - ue_x
                    hy = shift_lanes(es[1], b) - ue_y[b]
                    hz = shift_lanes(es[2], b) - ue[2]
                    h2 = hx * hx + hy * hy + hz * hz
                    dil_e = dil_e + (h2 * lax.rsqrt(h2) - length) * hmask_ref[i]
            q_c = (3.0 * dil_c * w_c) * w_c
            q_e = (3.0 * dil_e * w_e) * w_e
            wq_ref[1, 0:3, :] = q_e[0:3]
            wq_ref[1, 3:3 + cols, :] = q_c
            wq_ref[1, 3 + cols:6 + cols, :] = q_e[3:6]

            fx = jnp.zeros((cols, rows), jnp.float32)
            fy = jnp.zeros((cols, rows), jnp.float32)
            fz = jnp.zeros((cols, rows), jnp.float32)
            for a, members in groups.items():
                q_slab = wq_ref[1, 3 + a:3 + a + cols, :]
                for i, b, length, column in members:
                    shear = table_ref[kind, column]
                    alpha = shear * (15.0 / length)
                    beta = 3.0 * bulk_modulus - 5.0 * shear
                    f = alpha * pa_ref[i] + beta * (pb_ref[i] * (q_c + shift_lanes(q_slab, b)))
                    fx = fx + f * sx_ref[i]
                    fy = fy + f * sy_ref[i]
                    fz = fz + f * sz_ref[i]
            above = jnp.where(gp < nsprings, spring_ref[jnp.minimum(gp, nsprings - 1)], 0.0)
            below = jnp.where(gp > 0, spring_ref[jnp.maximum(gp - 1, 0)], 0.0)
            hi_p = jnp.minimum(p + 1, plies - 1)
            lo_p = jnp.maximum(p - 1, 0)
            for k, fk in enumerate((fx, fy, fz)):
                hi = jnp.where(p == plies - 1, uc[k], ext[k, hi_p, cols:2 * cols, :])
                lo = jnp.where(p == 0, uc[k], ext[k, lo_p, cols:2 * cols, :])
                o_ref[k, p] = fk + (above * (hi - uc[k]) + below * (lo - uc[k]))
            return carry

        lax.fori_loop(0, plies, ply_body, 0)
        pl.when(has[3])(ply_copies[0].wait_recv)
        pl.when(has[2])(ply_copies[1].wait_recv)
        g0 = q * plies
        below = jnp.where(g0 > 0, spring_ref[jnp.maximum(g0 - 1, 0)], 0.0)
        gl = q * plies + plies - 1
        above = jnp.where(gl < nsprings, spring_ref[jnp.minimum(gl, nsprings - 1)], 0.0)
        for k in range(3):
            o_ref[k, 0] = o_ref[k, 0] + below * (ply_halo[0, k] - ext[k, 0, cols:2 * cols, :])
            o_ref[k, plies - 1] = o_ref[k, plies - 1] + above * (
                ply_halo[1, k] - ext[k, plies - 1, cols:2 * cols, :])
        for p in range(plies):
            for d in range(2):
                pl.when(has[d])(tile_copy(d, p).wait_send)
        for cond, cp in zip(has[2:], ply_copies):
            pl.when(cond)(cp.wait_send)

    return kernel


def local(displacement, angle_index, bond_table, interface_stiffness):
    comp_count, ply_count, col_count, row_count = displacement.shape
    x_total = col_count * lax.axis_size("tile")
    kernel = make_kernel(ply_count, col_count, row_count, x_total, interface_stiffness.shape[0])
    nbond = len(bond_list())
    smem = pl.BlockSpec(memory_space=pltpu.SMEM)
    return pl.pallas_call(
        kernel,
        in_specs=[smem, smem, smem, pl.BlockSpec(memory_space=pl.ANY)],
        out_specs=pl.BlockSpec(memory_space=pltpu.VMEM),
        out_shape=jax.ShapeDtypeStruct(displacement.shape, jnp.float32),
        scratch_shapes=[
            pltpu.VMEM((3, ply_count, 3 * col_count, row_count), jnp.float32),
            pltpu.VMEM((2, 3, col_count, row_count), jnp.float32),
            pltpu.VMEM((2, col_count + 6, row_count), jnp.float32),
            pltpu.VMEM((nbond, col_count, row_count), jnp.float32),
            pltpu.VMEM((nbond, col_count, row_count), jnp.float32),
            pltpu.VMEM((nbond, col_count, row_count), jnp.float32),
            pltpu.VMEM((nbond, col_count, row_count), jnp.float32),
            pltpu.VMEM((nbond, col_count, row_count), jnp.float32),
            pltpu.VMEM((nbond, col_count, row_count), jnp.float32),
            pltpu.VMEM((nbond, col_count, row_count), jnp.float32),
            pltpu.VMEM((nbond, col_count, row_count), jnp.float32),
            pltpu.SemaphoreType.DMA((5,)),
            pltpu.SemaphoreType.DMA((2, ply_count)),
            pltpu.SemaphoreType.DMA((2, ply_count)),
        ],
        compiler_params=pltpu.CompilerParams(collective_id=0, has_side_effects=True),
    )(angle_index, bond_table, interface_stiffness, displacement)


def solution(mesh):
    placed = (P(None, "ply", "tile", None), P("ply"), P(), P())
    return jax.shard_map(
        local, mesh=mesh, in_specs=placed, out_specs=P(None, "ply", "tile", None), check_vma=False
    )
```

```python
import math

import jax
import jax.numpy as jnp
from jax import lax
from jax.experimental import pallas as pl
from jax.experimental.pallas import tpu as pltpu
from jax.sharding import PartitionSpec as P

bulk_modulus = 40.0


def bond_list():
    halves = []
    for shift_x in range(-3, 4):
        for shift_y in range(-3, 4):
            radius = shift_x * shift_x + shift_y * shift_y
            if 0 < radius <= 9 and (shift_x > 0 or (shift_x == 0 and shift_y > 0)):
                halves.append((shift_x, shift_y))
    result = []
    for shift_x in range(-3, 4):
        for shift_y in range(-3, 4):
            radius = shift_x * shift_x + shift_y * shift_y
            if 0 < radius <= 9:
                if (shift_x, shift_y) in halves:
                    column = halves.index((shift_x, shift_y))
                else:
                    column = halves.index((-shift_x, -shift_y))
                result.append((shift_x, shift_y, math.sqrt(radius), column))
    return result


def halo(shard, axis, dim, width):
    peers, length = lax.axis_size(axis), shard.shape[dim]
    up = [(i, (i + 1) % peers) for i in range(peers)]
    down = [(j, i) for i, j in up]
    last = lax.slice_in_dim(shard, length - width, length, axis=dim)
    first = lax.slice_in_dim(shard, 0, width, axis=dim)
    before = lax.ppermute(last, axis, up)
    after = lax.ppermute(first, axis, down)
    return jnp.concatenate([before, shard, after], axis=dim)


def shift_lanes(x, b):
    if b == 0:
        return x
    return pltpu.roll(x, (-b) % x.shape[-1], 1)


MESH = pl.DeviceIdType.MESH


def make_kernel(plies, cols, rows, x_total, nsprings):
    bonds = bond_list()
    wide = cols + 6
    shifts = sorted({a for a, _, _, _ in bonds})
    lanes = sorted({b for _, b, _, _ in bonds})

    def kernel(angle_ref, table_ref, spring_ref, u_hbm, o_ref, ext, ply_halo, wq_ref, fmask_ref,
               hmask_ref, wm_ref, sx_ref, sy_ref, sz_ref, pa_ref, pb_ref, sems, send_t, recv_t):
        t = lax.axis_index("tile")
        nt = lax.axis_size("tile")
        q = lax.axis_index("ply")
        nq = lax.axis_size("ply")
        x0 = t * cols
        own = pltpu.make_async_copy(u_hbm, ext.at[:, :, cols:2 * cols, :], sems.at[0])
        own.start()
        has = ((t > 0), (t < nt - 1), (q > 0), (q < nq - 1))
        peers = ({"tile": t - 1}, {"tile": t + 1}, {"ply": q - 1}, {"ply": q + 1})
        barrier = pltpu.get_barrier_semaphore()
        for cond, dev in zip(has, peers):
            @pl.when(cond)
            def _():
                pl.semaphore_signal(barrier, inc=1, device_id=dev, device_id_type=MESH)
        count = sum(c.astype(jnp.int32) for c in has)
        pl.semaphore_wait(barrier, count)
        def tile_copy(d, p):
            if d == 0:
                src, dst = slice(0, 6), slice(2 * cols, 2 * cols + 6)
            else:
                src, dst = slice(cols - 6, cols), slice(cols - 6, cols)
            return pltpu.make_async_remote_copy(
                u_hbm.at[:, p, src, :], ext.at[:, p, dst, :], send_t.at[d, p], recv_t.at[d, p],
                device_id=peers[d], device_id_type=MESH)

        ply_copies = (
            pltpu.make_async_remote_copy(
                u_hbm.at[:, 0], ply_halo.at[1], sems.at[1], sems.at[3],
                device_id=peers[2], device_id_type=MESH),
            pltpu.make_async_remote_copy(
                u_hbm.at[:, plies - 1], ply_halo.at[0], sems.at[2], sems.at[4],
                device_id=peers[3], device_id_type=MESH),
        )
        ahead = min(2, plies)
        for p in range(ahead):
            for d in range(2):
                pl.when(has[d])(tile_copy(d, p).start)
        for cond, cp in zip(has[2:], ply_copies):
            pl.when(cond)(cp.start)

        sub = lax.broadcasted_iota(jnp.int32, (cols, rows), 0)
        lane = lax.broadcasted_iota(jnp.int32, (cols, rows), 1)
        core_x = sub + x0
        edge_x = jnp.where(sub < 3, x0 - 3 + sub, x0 + cols - 3 + sub)
        edge_ok = sub < 6

        def bond_masks(xg, ok0, out_ref):
            own_x = ok0 & (xg >= 0) & (xg < x_total)
            total = jnp.zeros((cols, rows), jnp.float32)
            for i, (a, b, length, column) in enumerate(bonds):
                ok = own_x & (xg + a >= 0) & (xg + a < x_total) & (lane + b >= 0) & (lane + b < rows)
                m = jnp.where(ok, 1.0, 0.0)
                out_ref[i] = m
                total = total + m * length
            return total

        mass_c = bond_masks(core_x, sub >= 0, fmask_ref)
        mass_e = bond_masks(edge_x, edge_ok, hmask_ref)
        w_c = 1.0 / jnp.where(mass_c > 0, mass_c, 1.0)
        w_e = jnp.where(mass_e > 0, 1.0 / jnp.where(mass_e > 0, mass_e, 1.0), 0.0)
        wq_ref[0, 0:3, :] = w_e[0:3]
        wq_ref[0, 3:3 + cols, :] = w_c
        wq_ref[0, 3 + cols:6 + cols, :] = w_e[3:6]
        groups = {}
        for i, (a, b, length, column) in enumerate(bonds):
            groups.setdefault(a, []).append((i, b, length, column))
        for a, members in groups.items():
            w_slab = wq_ref[0, 3 + a:3 + a + cols, :]
            for i, b, length, column in members:
                wm_ref[i] = fmask_ref[i] * (w_c + shift_lanes(w_slab, b))

        @pl.when(t == 0)
        def _():
            ext[:, :, 0:cols, :] = jnp.zeros((3, plies, cols, rows), jnp.float32)

        @pl.when(t == nt - 1)
        def _():
            ext[:, :, 2 * cols:3 * cols, :] = jnp.zeros((3, plies, cols, rows), jnp.float32)

        @pl.when(q == 0)
        def _():
            ply_halo[0] = jnp.zeros((3, cols, rows), jnp.float32)

        @pl.when(q == nq - 1)
        def _():
            ply_halo[1] = jnp.zeros((3, cols, rows), jnp.float32)

        own.wait()

        def ply_body(p, carry):
            for d in range(2):
                pl.when(has[d] & (p + ahead < plies))(
                    lambda d=d: tile_copy(d, jnp.minimum(p + ahead, plies - 1)).start())
            pl.when(has[1])(tile_copy(0, p).wait_recv)
            pl.when(has[0])(tile_copy(1, p).wait_recv)
            gp = q * plies + p
            kind = angle_ref[p]
            low = lax.broadcasted_iota(jnp.int32, (cols, rows), 0) < 3

            def edge_rows(k, a):
                return jnp.where(low, ext[k, p, cols - 3 + a:2 * cols - 3 + a, :],
                                 ext[k, p, 2 * cols - 3 + a:3 * cols - 3 + a, :])

            uc = [ext[k, p, cols:2 * cols, :] for k in range(3)]
            ue = [edge_rows(k, 0) for k in range(3)]
            uc_y = {b: uc[1] - b for b in lanes}
            ue_y = {b: ue[1] - b for b in lanes}
            dil_c = jnp.zeros((cols, rows), jnp.float32)
            dil_e = jnp.zeros((cols, rows), jnp.float32)
            for a, members in groups.items():
                cs = [ext[k, p, cols + a:2 * cols + a, :] for k in range(3)]
                es = [edge_rows(k, a) for k in range(3)]
                uc_x = uc[0] - a
                ue_x = ue[0] - a
                for i, b, length, column in members:
                    sx = shift_lanes(cs[0], b) - uc_x
                    sy = shift_lanes(cs[1], b) - uc_y[b]
                    sz = shift_lanes(cs[2], b) - uc[2]
                    s2 = sx * sx + sy * sy + sz * sz
                    inv = lax.rsqrt(s2)
                    e = s2 * inv - length
                    m = fmask_ref[i]
                    dil_c = dil_c + e * m
                    sx_ref[i] = sx
                    sy_ref[i] = sy
                    sz_ref[i] = sz
                    pa_ref[i] = (inv * e) * wm_ref[i]
                    pb_ref[i] = inv * m
                    hx = shift_lanes(es[0], b) - ue_x
                    hy = shift_lanes(es[1], b) - ue_y[b]
                    hz = shift_lanes(es[2], b) - ue[2]
                    h2 = hx * hx + hy * hy + hz * hz
                    dil_e = dil_e + (h2 * lax.rsqrt(h2) - length) * hmask_ref[i]
            q_c = (3.0 * dil_c * w_c) * w_c
            q_e = (3.0 * dil_e * w_e) * w_e
            wq_ref[1, 0:3, :] = q_e[0:3]
            wq_ref[1, 3:3 + cols, :] = q_c
            wq_ref[1, 3 + cols:6 + cols, :] = q_e[3:6]

            fx = jnp.zeros((cols, rows), jnp.float32)
            fy = jnp.zeros((cols, rows), jnp.float32)
            fz = jnp.zeros((cols, rows), jnp.float32)
            for a, members in groups.items():
                q_slab = wq_ref[1, 3 + a:3 + a + cols, :]
                for i, b, length, column in members:
                    shear = table_ref[kind, column]
                    alpha = shear * (15.0 / length)
                    beta = 3.0 * bulk_modulus - 5.0 * shear
                    f = alpha * pa_ref[i] + beta * (pb_ref[i] * (q_c + shift_lanes(q_slab, b)))
                    fx = fx + f * sx_ref[i]
                    fy = fy + f * sy_ref[i]
                    fz = fz + f * sz_ref[i]
            above = jnp.where(gp < nsprings, spring_ref[jnp.minimum(gp, nsprings - 1)], 0.0)
            below = jnp.where(gp > 0, spring_ref[jnp.maximum(gp - 1, 0)], 0.0)
            hi_p = jnp.minimum(p + 1, plies - 1)
            lo_p = jnp.maximum(p - 1, 0)
            for k, fk in enumerate((fx, fy, fz)):
                hi = jnp.where(p == plies - 1, uc[k], ext[k, hi_p, cols:2 * cols, :])
                lo = jnp.where(p == 0, uc[k], ext[k, lo_p, cols:2 * cols, :])
                o_ref[k, p] = fk + (above * (hi - uc[k]) + below * (lo - uc[k]))
            return carry

        lax.fori_loop(0, plies, ply_body, 0)
        pl.when(has[3])(ply_copies[0].wait_recv)
        pl.when(has[2])(ply_copies[1].wait_recv)
        g0 = q * plies
        below = jnp.where(g0 > 0, spring_ref[jnp.maximum(g0 - 1, 0)], 0.0)
        gl = q * plies + plies - 1
        above = jnp.where(gl < nsprings, spring_ref[jnp.minimum(gl, nsprings - 1)], 0.0)
        for k in range(3):
            o_ref[k, 0] = o_ref[k, 0] + below * (ply_halo[0, k] - ext[k, 0, cols:2 * cols, :])
            o_ref[k, plies - 1] = o_ref[k, plies - 1] + above * (
                ply_halo[1, k] - ext[k, plies - 1, cols:2 * cols, :])
        for p in range(plies):
            for d in range(2):
                pl.when(has[d])(tile_copy(d, p).wait_send)
        for cond, cp in zip(has[2:], ply_copies):
            pl.when(cond)(cp.wait_send)

    return kernel


def local(displacement, angle_index, bond_table, interface_stiffness):
    comp_count, ply_count, col_count, row_count = displacement.shape
    x_total = col_count * lax.axis_size("tile")
    kernel = make_kernel(ply_count, col_count, row_count, x_total, interface_stiffness.shape[0])
    nbond = len(bond_list())
    smem = pl.BlockSpec(memory_space=pltpu.SMEM)
    return pl.pallas_call(
        kernel,
        in_specs=[smem, smem, smem, pl.BlockSpec(memory_space=pl.ANY)],
        out_specs=pl.BlockSpec(memory_space=pltpu.VMEM),
        out_shape=jax.ShapeDtypeStruct(displacement.shape, jnp.float32),
        scratch_shapes=[
            pltpu.VMEM((3, ply_count, 3 * col_count, row_count), jnp.float32),
            pltpu.VMEM((2, 3, col_count, row_count), jnp.float32),
            pltpu.VMEM((2, col_count + 6, row_count), jnp.float32),
            pltpu.VMEM((nbond, col_count, row_count), jnp.float32),
            pltpu.VMEM((nbond, col_count, row_count), jnp.float32),
            pltpu.VMEM((nbond, col_count, row_count), jnp.float32),
            pltpu.VMEM((nbond, col_count, row_count), jnp.float32),
            pltpu.VMEM((nbond, col_count, row_count), jnp.float32),
            pltpu.VMEM((nbond, col_count, row_count), jnp.float32),
            pltpu.VMEM((nbond, col_count, row_count), jnp.float32),
            pltpu.VMEM((nbond, col_count, row_count), jnp.float32),
            pltpu.SemaphoreType.DMA((5,)),
            pltpu.SemaphoreType.DMA((2, ply_count)),
            pltpu.SemaphoreType.DMA((2, ply_count)),
        ],
        compiler_params=pltpu.CompilerParams(collective_id=0, has_side_effects=True),
    )(angle_index, bond_table, interface_stiffness, displacement)


def solution(mesh):
    placed = (P(None, "ply", "tile", None), P("ply"), P(), P())
    return jax.shard_map(
        local, mesh=mesh, in_specs=placed, out_specs=P(None, "ply", "tile", None), check_vma=False
    )
```

```python
import math

import jax
import jax.numpy as jnp
from jax import lax
from jax.experimental import pallas as pl
from jax.experimental.pallas import tpu as pltpu
from jax.sharding import PartitionSpec as P

bulk_modulus = 40.0


def bond_list():
    halves = []
    for shift_x in range(-3, 4):
        for shift_y in range(-3, 4):
            radius = shift_x * shift_x + shift_y * shift_y
            if 0 < radius <= 9 and (shift_x > 0 or (shift_x == 0 and shift_y > 0)):
                halves.append((shift_x, shift_y))
    result = []
    for shift_x in range(-3, 4):
        for shift_y in range(-3, 4):
            radius = shift_x * shift_x + shift_y * shift_y
            if 0 < radius <= 9:
                if (shift_x, shift_y) in halves:
                    column = halves.index((shift_x, shift_y))
                else:
                    column = halves.index((-shift_x, -shift_y))
                result.append((shift_x, shift_y, math.sqrt(radius), column))
    return result


def halo(shard, axis, dim, width):
    peers, length = lax.axis_size(axis), shard.shape[dim]
    up = [(i, (i + 1) % peers) for i in range(peers)]
    down = [(j, i) for i, j in up]
    last = lax.slice_in_dim(shard, length - width, length, axis=dim)
    first = lax.slice_in_dim(shard, 0, width, axis=dim)
    before = lax.ppermute(last, axis, up)
    after = lax.ppermute(first, axis, down)
    return jnp.concatenate([before, shard, after], axis=dim)


def shift_lanes(x, b):
    if b == 0:
        return x
    return pltpu.roll(x, (-b) % x.shape[-1], 1)


MESH = pl.DeviceIdType.MESH


def make_kernel(plies, cols, rows, x_total, nsprings):
    bonds = bond_list()
    wide = cols + 6
    shifts = sorted({a for a, _, _, _ in bonds})
    lanes = sorted({b for _, b, _, _ in bonds})

    def kernel(angle_ref, table_ref, spring_ref, u_hbm, o_ref, ext, ply_halo, wq_ref, fmask_ref,
               hmask_ref, wm_ref, sx_ref, sy_ref, sz_ref, pa_ref, pb_ref, sems, send_t, recv_t):
        t = lax.axis_index("tile")
        nt = lax.axis_size("tile")
        q = lax.axis_index("ply")
        nq = lax.axis_size("ply")
        x0 = t * cols
        own = pltpu.make_async_copy(u_hbm, ext.at[:, :, cols:2 * cols, :], sems.at[0])
        own.start()
        has = ((t > 0), (t < nt - 1), (q > 0), (q < nq - 1))
        peers = ({"tile": t - 1}, {"tile": t + 1}, {"ply": q - 1}, {"ply": q + 1})
        barrier = pltpu.get_barrier_semaphore()
        for cond, dev in zip(has, peers):
            @pl.when(cond)
            def _():
                pl.semaphore_signal(barrier, inc=1, device_id=dev, device_id_type=MESH)
        count = sum(c.astype(jnp.int32) for c in has)
        pl.semaphore_wait(barrier, count)
        def tile_copy(d, p):
            if d == 0:
                src, dst = slice(0, 6), slice(2 * cols, 2 * cols + 6)
            else:
                src, dst = slice(cols - 6, cols), slice(cols - 6, cols)
            return pltpu.make_async_remote_copy(
                u_hbm.at[:, p, src, :], ext.at[:, p, dst, :], send_t.at[d, p], recv_t.at[d, p],
                device_id=peers[d], device_id_type=MESH)

        ply_copies = (
            pltpu.make_async_remote_copy(
                u_hbm.at[:, 0], ply_halo.at[1], sems.at[1], sems.at[3],
                device_id=peers[2], device_id_type=MESH),
            pltpu.make_async_remote_copy(
                u_hbm.at[:, plies - 1], ply_halo.at[0], sems.at[2], sems.at[4],
                device_id=peers[3], device_id_type=MESH),
        )
        ahead = plies
        for p in range(ahead):
            for d in range(2):
                pl.when(has[d])(tile_copy(d, p).start)
        for cond, cp in zip(has[2:], ply_copies):
            pl.when(cond)(cp.start)

        sub = lax.broadcasted_iota(jnp.int32, (cols, rows), 0)
        lane = lax.broadcasted_iota(jnp.int32, (cols, rows), 1)
        core_x = sub + x0
        edge_x = jnp.where(sub < 3, x0 - 3 + sub, x0 + cols - 3 + sub)
        edge_ok = sub < 6

        def bond_masks(xg, ok0, out_ref):
            own_x = ok0 & (xg >= 0) & (xg < x_total)
            total = jnp.zeros((cols, rows), jnp.float32)
            for i, (a, b, length, column) in enumerate(bonds):
                ok = own_x & (xg + a >= 0) & (xg + a < x_total) & (lane + b >= 0) & (lane + b < rows)
                m = jnp.where(ok, 1.0, 0.0)
                out_ref[i] = m
                total = total + m * length
            return total

        mass_c = bond_masks(core_x, sub >= 0, fmask_ref)
        mass_e = bond_masks(edge_x, edge_ok, hmask_ref)
        w_c = 1.0 / jnp.where(mass_c > 0, mass_c, 1.0)
        w_e = jnp.where(mass_e > 0, 1.0 / jnp.where(mass_e > 0, mass_e, 1.0), 0.0)
        wq_ref[0, 0:3, :] = w_e[0:3]
        wq_ref[0, 3:3 + cols, :] = w_c
        wq_ref[0, 3 + cols:6 + cols, :] = w_e[3:6]
        groups = {}
        for i, (a, b, length, column) in enumerate(bonds):
            groups.setdefault(a, []).append((i, b, length, column))
        for a, members in groups.items():
            w_slab = wq_ref[0, 3 + a:3 + a + cols, :]
            for i, b, length, column in members:
                wm_ref[i] = fmask_ref[i] * (w_c + shift_lanes(w_slab, b))

        @pl.when(t == 0)
        def _():
            ext[:, :, 0:cols, :] = jnp.zeros((3, plies, cols, rows), jnp.float32)

        @pl.when(t == nt - 1)
        def _():
            ext[:, :, 2 * cols:3 * cols, :] = jnp.zeros((3, plies, cols, rows), jnp.float32)

        @pl.when(q == 0)
        def _():
            ply_halo[0] = jnp.zeros((3, cols, rows), jnp.float32)

        @pl.when(q == nq - 1)
        def _():
            ply_halo[1] = jnp.zeros((3, cols, rows), jnp.float32)

        own.wait()

        def ply_body(p, carry):
            for d in range(2):
                pl.when(has[d] & (p + ahead < plies))(
                    lambda d=d: tile_copy(d, jnp.minimum(p + ahead, plies - 1)).start())
            pl.when(has[1])(tile_copy(0, p).wait_recv)
            pl.when(has[0])(tile_copy(1, p).wait_recv)
            gp = q * plies + p
            kind = angle_ref[p]
            low = lax.broadcasted_iota(jnp.int32, (cols, rows), 0) < 3

            def edge_rows(k, a):
                return jnp.where(low, ext[k, p, cols - 3 + a:2 * cols - 3 + a, :],
                                 ext[k, p, 2 * cols - 3 + a:3 * cols - 3 + a, :])

            uc = [ext[k, p, cols:2 * cols, :] for k in range(3)]
            ue = [edge_rows(k, 0) for k in range(3)]
            uc_y = {b: uc[1] - b for b in lanes}
            ue_y = {b: ue[1] - b for b in lanes}
            dil_c = jnp.zeros((cols, rows), jnp.float32)
            dil_e = jnp.zeros((cols, rows), jnp.float32)
            for a, members in groups.items():
                cs = [ext[k, p, cols + a:2 * cols + a, :] for k in range(3)]
                es = [edge_rows(k, a) for k in range(3)]
                uc_x = uc[0] - a
                ue_x = ue[0] - a
                for i, b, length, column in members:
                    sx = shift_lanes(cs[0], b) - uc_x
                    sy = shift_lanes(cs[1], b) - uc_y[b]
                    sz = shift_lanes(cs[2], b) - uc[2]
                    s2 = sx * sx + sy * sy + sz * sz
                    inv = lax.rsqrt(s2)
                    e = s2 * inv - length
                    m = fmask_ref[i]
                    dil_c = dil_c + e * m
                    sx_ref[i] = sx
                    sy_ref[i] = sy
                    sz_ref[i] = sz
                    pa_ref[i] = (inv * e) * wm_ref[i]
                    pb_ref[i] = inv * m
                    hx = shift_lanes(es[0], b) - ue_x
                    hy = shift_lanes(es[1], b) - ue_y[b]
                    hz = shift_lanes(es[2], b) - ue[2]
                    h2 = hx * hx + hy * hy + hz * hz
                    dil_e = dil_e + (h2 * lax.rsqrt(h2) - length) * hmask_ref[i]
            q_c = (3.0 * dil_c * w_c) * w_c
            q_e = (3.0 * dil_e * w_e) * w_e
            wq_ref[1, 0:3, :] = q_e[0:3]
            wq_ref[1, 3:3 + cols, :] = q_c
            wq_ref[1, 3 + cols:6 + cols, :] = q_e[3:6]

            fx = jnp.zeros((cols, rows), jnp.float32)
            fy = jnp.zeros((cols, rows), jnp.float32)
            fz = jnp.zeros((cols, rows), jnp.float32)
            for a, members in groups.items():
                q_slab = wq_ref[1, 3 + a:3 + a + cols, :]
                for i, b, length, column in members:
                    shear = table_ref[kind, column]
                    alpha = shear * (15.0 / length)
                    beta = 3.0 * bulk_modulus - 5.0 * shear
                    f = alpha * pa_ref[i] + beta * (pb_ref[i] * (q_c + shift_lanes(q_slab, b)))
                    fx = fx + f * sx_ref[i]
                    fy = fy + f * sy_ref[i]
                    fz = fz + f * sz_ref[i]
            above = jnp.where(gp < nsprings, spring_ref[jnp.minimum(gp, nsprings - 1)], 0.0)
            below = jnp.where(gp > 0, spring_ref[jnp.maximum(gp - 1, 0)], 0.0)
            hi_p = jnp.minimum(p + 1, plies - 1)
            lo_p = jnp.maximum(p - 1, 0)
            for k, fk in enumerate((fx, fy, fz)):
                hi = jnp.where(p == plies - 1, uc[k], ext[k, hi_p, cols:2 * cols, :])
                lo = jnp.where(p == 0, uc[k], ext[k, lo_p, cols:2 * cols, :])
                o_ref[k, p] = fk + (above * (hi - uc[k]) + below * (lo - uc[k]))
            return carry

        lax.fori_loop(0, plies, ply_body, 0)
        pl.when(has[3])(ply_copies[0].wait_recv)
        pl.when(has[2])(ply_copies[1].wait_recv)
        g0 = q * plies
        below = jnp.where(g0 > 0, spring_ref[jnp.maximum(g0 - 1, 0)], 0.0)
        gl = q * plies + plies - 1
        above = jnp.where(gl < nsprings, spring_ref[jnp.minimum(gl, nsprings - 1)], 0.0)
        for k in range(3):
            o_ref[k, 0] = o_ref[k, 0] + below * (ply_halo[0, k] - ext[k, 0, cols:2 * cols, :])
            o_ref[k, plies - 1] = o_ref[k, plies - 1] + above * (
                ply_halo[1, k] - ext[k, plies - 1, cols:2 * cols, :])
        for p in range(plies):
            for d in range(2):
                pl.when(has[d])(tile_copy(d, p).wait_send)
        for cond, cp in zip(has[2:], ply_copies):
            pl.when(cond)(cp.wait_send)

    return kernel


def local(displacement, angle_index, bond_table, interface_stiffness):
    comp_count, ply_count, col_count, row_count = displacement.shape
    x_total = col_count * lax.axis_size("tile")
    kernel = make_kernel(ply_count, col_count, row_count, x_total, interface_stiffness.shape[0])
    nbond = len(bond_list())
    smem = pl.BlockSpec(memory_space=pltpu.SMEM)
    return pl.pallas_call(
        kernel,
        in_specs=[smem, smem, smem, pl.BlockSpec(memory_space=pl.ANY)],
        out_specs=pl.BlockSpec(memory_space=pltpu.VMEM),
        out_shape=jax.ShapeDtypeStruct(displacement.shape, jnp.float32),
        scratch_shapes=[
            pltpu.VMEM((3, ply_count, 3 * col_count, row_count), jnp.float32),
            pltpu.VMEM((2, 3, col_count, row_count), jnp.float32),
            pltpu.VMEM((2, col_count + 6, row_count), jnp.float32),
            pltpu.VMEM((nbond, col_count, row_count), jnp.float32),
            pltpu.VMEM((nbond, col_count, row_count), jnp.float32),
            pltpu.VMEM((nbond, col_count, row_count), jnp.float32),
            pltpu.VMEM((nbond, col_count, row_count), jnp.float32),
            pltpu.VMEM((nbond, col_count, row_count), jnp.float32),
            pltpu.VMEM((nbond, col_count, row_count), jnp.float32),
            pltpu.VMEM((nbond, col_count, row_count), jnp.float32),
            pltpu.VMEM((nbond, col_count, row_count), jnp.float32),
            pltpu.SemaphoreType.DMA((5,)),
            pltpu.SemaphoreType.DMA((2, ply_count)),
            pltpu.SemaphoreType.DMA((2, ply_count)),
        ],
        compiler_params=pltpu.CompilerParams(collective_id=0, has_side_effects=True),
    )(angle_index, bond_table, interface_stiffness, displacement)


def solution(mesh):
    placed = (P(None, "ply", "tile", None), P("ply"), P(), P())
    return jax.shard_map(
        local, mesh=mesh, in_specs=placed, out_specs=P(None, "ply", "tile", None), check_vma=False
    )
```

```python
import math

import jax
import jax.numpy as jnp
from jax import lax
from jax.experimental import pallas as pl
from jax.experimental.pallas import tpu as pltpu
from jax.sharding import PartitionSpec as P

bulk_modulus = 40.0


def bond_list():
    halves = []
    for shift_x in range(-3, 4):
        for shift_y in range(-3, 4):
            radius = shift_x * shift_x + shift_y * shift_y
            if 0 < radius <= 9 and (shift_x > 0 or (shift_x == 0 and shift_y > 0)):
                halves.append((shift_x, shift_y))
    result = []
    for shift_x in range(-3, 4):
        for shift_y in range(-3, 4):
            radius = shift_x * shift_x + shift_y * shift_y
            if 0 < radius <= 9:
                if (shift_x, shift_y) in halves:
                    column = halves.index((shift_x, shift_y))
                else:
                    column = halves.index((-shift_x, -shift_y))
                result.append((shift_x, shift_y, math.sqrt(radius), column))
    return result


def halo(shard, axis, dim, width):
    peers, length = lax.axis_size(axis), shard.shape[dim]
    up = [(i, (i + 1) % peers) for i in range(peers)]
    down = [(j, i) for i, j in up]
    last = lax.slice_in_dim(shard, length - width, length, axis=dim)
    first = lax.slice_in_dim(shard, 0, width, axis=dim)
    before = lax.ppermute(last, axis, up)
    after = lax.ppermute(first, axis, down)
    return jnp.concatenate([before, shard, after], axis=dim)


def shift_lanes(x, b):
    if b == 0:
        return x
    return pltpu.roll(x, (-b) % x.shape[-1], 1)


MESH = pl.DeviceIdType.MESH


def make_kernel(plies, cols, rows, x_total, nsprings):
    bonds = bond_list()
    wide = cols + 6
    shifts = sorted({a for a, _, _, _ in bonds})
    lanes = sorted({b for _, b, _, _ in bonds})

    def kernel(angle_ref, table_ref, spring_ref, u_hbm, o_ref, ext, wq_ref, fmask_ref,
               hmask_ref, wm_ref, sx_ref, sy_ref, sz_ref, pa_ref, pb_ref, sems, send_t, recv_t):
        t = lax.axis_index("tile")
        nt = lax.axis_size("tile")
        q = lax.axis_index("ply")
        nq = lax.axis_size("ply")
        x0 = t * cols
        own = pltpu.make_async_copy(u_hbm, ext.at[:, :, cols:2 * cols, :], sems.at[0])
        own.start()
        has = ((t > 0), (t < nt - 1))
        peers = ({"tile": t - 1}, {"tile": t + 1})
        barrier = pltpu.get_barrier_semaphore()
        for cond, dev in zip(has, peers):
            @pl.when(cond)
            def _():
                pl.semaphore_signal(barrier, inc=1, device_id=dev, device_id_type=MESH)
        count = sum(c.astype(jnp.int32) for c in has)
        pl.semaphore_wait(barrier, count)
        def tile_copy(d, p):
            if d == 0:
                src, dst = slice(0, 6), slice(2 * cols, 2 * cols + 6)
            else:
                src, dst = slice(cols - 6, cols), slice(cols - 6, cols)
            return pltpu.make_async_remote_copy(
                u_hbm.at[:, p, src, :], ext.at[:, p, dst, :], send_t.at[d, p], recv_t.at[d, p],
                device_id=peers[d], device_id_type=MESH)

        ahead = min(2, plies)
        for p in range(ahead):
            for d in range(2):
                pl.when(has[d])(tile_copy(d, p).start)

        sub = lax.broadcasted_iota(jnp.int32, (cols, rows), 0)
        lane = lax.broadcasted_iota(jnp.int32, (cols, rows), 1)
        core_x = sub + x0
        edge_x = jnp.where(sub < 3, x0 - 3 + sub, x0 + cols - 3 + sub)
        edge_ok = sub < 6

        def bond_masks(xg, ok0, out_ref):
            own_x = ok0 & (xg >= 0) & (xg < x_total)
            total = jnp.zeros((cols, rows), jnp.float32)
            for i, (a, b, length, column) in enumerate(bonds):
                ok = own_x & (xg + a >= 0) & (xg + a < x_total) & (lane + b >= 0) & (lane + b < rows)
                m = jnp.where(ok, 1.0, 0.0)
                out_ref[i] = m
                total = total + m * length
            return total

        mass_c = bond_masks(core_x, sub >= 0, fmask_ref)
        mass_e = bond_masks(edge_x, edge_ok, hmask_ref)
        w_c = 1.0 / jnp.where(mass_c > 0, mass_c, 1.0)
        w_e = jnp.where(mass_e > 0, 1.0 / jnp.where(mass_e > 0, mass_e, 1.0), 0.0)
        wq_ref[0, 0:3, :] = w_e[0:3]
        wq_ref[0, 3:3 + cols, :] = w_c
        wq_ref[0, 3 + cols:6 + cols, :] = w_e[3:6]
        groups = {}
        for i, (a, b, length, column) in enumerate(bonds):
            groups.setdefault(a, []).append((i, b, length, column))
        for a, members in groups.items():
            w_slab = wq_ref[0, 3 + a:3 + a + cols, :]
            for i, b, length, column in members:
                wm_ref[i] = fmask_ref[i] * (w_c + shift_lanes(w_slab, b))

        @pl.when(t == 0)
        def _():
            ext[:, :, 0:cols, :] = jnp.zeros((3, plies, cols, rows), jnp.float32)

        @pl.when(t == nt - 1)
        def _():
            ext[:, :, 2 * cols:3 * cols, :] = jnp.zeros((3, plies, cols, rows), jnp.float32)

        own.wait()

        def ply_body(p, carry):
            for d in range(2):
                pl.when(has[d] & (p + ahead < plies))(
                    lambda d=d: tile_copy(d, jnp.minimum(p + ahead, plies - 1)).start())
            pl.when(has[1])(tile_copy(0, p).wait_recv)
            pl.when(has[0])(tile_copy(1, p).wait_recv)
            gp = q * plies + p
            kind = angle_ref[p]
            low = lax.broadcasted_iota(jnp.int32, (cols, rows), 0) < 3

            def edge_rows(k, a):
                return jnp.where(low, ext[k, p, cols - 3 + a:2 * cols - 3 + a, :],
                                 ext[k, p, 2 * cols - 3 + a:3 * cols - 3 + a, :])

            uc = [ext[k, p, cols:2 * cols, :] for k in range(3)]
            ue = [edge_rows(k, 0) for k in range(3)]
            uc_y = {b: uc[1] - b for b in lanes}
            ue_y = {b: ue[1] - b for b in lanes}
            dil_c = jnp.zeros((cols, rows), jnp.float32)
            dil_e = jnp.zeros((cols, rows), jnp.float32)
            for a, members in groups.items():
                cs = [ext[k, p, cols + a:2 * cols + a, :] for k in range(3)]
                es = [edge_rows(k, a) for k in range(3)]
                uc_x = uc[0] - a
                ue_x = ue[0] - a
                for i, b, length, column in members:
                    sx = shift_lanes(cs[0], b) - uc_x
                    sy = shift_lanes(cs[1], b) - uc_y[b]
                    sz = shift_lanes(cs[2], b) - uc[2]
                    s2 = sx * sx + sy * sy + sz * sz
                    inv = lax.rsqrt(s2)
                    e = s2 * inv - length
                    m = fmask_ref[i]
                    dil_c = dil_c + e * m
                    sx_ref[i] = sx
                    sy_ref[i] = sy
                    sz_ref[i] = sz
                    pa_ref[i] = (inv * e) * wm_ref[i]
                    pb_ref[i] = inv * m
                    hx = shift_lanes(es[0], b) - ue_x
                    hy = shift_lanes(es[1], b) - ue_y[b]
                    hz = shift_lanes(es[2], b) - ue[2]
                    h2 = hx * hx + hy * hy + hz * hz
                    dil_e = dil_e + (h2 * lax.rsqrt(h2) - length) * hmask_ref[i]
            q_c = (3.0 * dil_c * w_c) * w_c
            q_e = (3.0 * dil_e * w_e) * w_e
            wq_ref[1, 0:3, :] = q_e[0:3]
            wq_ref[1, 3:3 + cols, :] = q_c
            wq_ref[1, 3 + cols:6 + cols, :] = q_e[3:6]

            fx = jnp.zeros((cols, rows), jnp.float32)
            fy = jnp.zeros((cols, rows), jnp.float32)
            fz = jnp.zeros((cols, rows), jnp.float32)
            for a, members in groups.items():
                q_slab = wq_ref[1, 3 + a:3 + a + cols, :]
                for i, b, length, column in members:
                    shear = table_ref[kind, column]
                    alpha = shear * (15.0 / length)
                    beta = 3.0 * bulk_modulus - 5.0 * shear
                    f = alpha * pa_ref[i] + beta * (pb_ref[i] * (q_c + shift_lanes(q_slab, b)))
                    fx = fx + f * sx_ref[i]
                    fy = fy + f * sy_ref[i]
                    fz = fz + f * sz_ref[i]
            above = jnp.where(gp < nsprings, spring_ref[jnp.minimum(gp, nsprings - 1)], 0.0)
            below = jnp.where(gp > 0, spring_ref[jnp.maximum(gp - 1, 0)], 0.0)
            hi_p = jnp.minimum(p + 1, plies - 1)
            lo_p = jnp.maximum(p - 1, 0)
            for k, fk in enumerate((fx, fy, fz)):
                hi = jnp.where(p == plies - 1, uc[k], ext[k, hi_p, cols:2 * cols, :])
                lo = jnp.where(p == 0, uc[k], ext[k, lo_p, cols:2 * cols, :])
                o_ref[k, p] = fk + (above * (hi - uc[k]) + below * (lo - uc[k]))
            return carry

        lax.fori_loop(0, plies, ply_body, 0)
        for p in range(plies):
            for d in range(2):
                pl.when(has[d])(tile_copy(d, p).wait_send)

    return kernel


def local(displacement, angle_index, bond_table, interface_stiffness):
    comp_count, ply_count, col_count, row_count = displacement.shape
    x_total = col_count * lax.axis_size("tile")
    kernel = make_kernel(ply_count, col_count, row_count, x_total, interface_stiffness.shape[0])
    nbond = len(bond_list())
    smem = pl.BlockSpec(memory_space=pltpu.SMEM)
    force = pl.pallas_call(
        kernel,
        in_specs=[smem, smem, smem, pl.BlockSpec(memory_space=pl.ANY)],
        out_specs=pl.BlockSpec(memory_space=pltpu.VMEM),
        out_shape=jax.ShapeDtypeStruct(displacement.shape, jnp.float32),
        scratch_shapes=[
            pltpu.VMEM((3, ply_count, 3 * col_count, row_count), jnp.float32),
            pltpu.VMEM((2, col_count + 6, row_count), jnp.float32),
            pltpu.VMEM((nbond, col_count, row_count), jnp.float32),
            pltpu.VMEM((nbond, col_count, row_count), jnp.float32),
            pltpu.VMEM((nbond, col_count, row_count), jnp.float32),
            pltpu.VMEM((nbond, col_count, row_count), jnp.float32),
            pltpu.VMEM((nbond, col_count, row_count), jnp.float32),
            pltpu.VMEM((nbond, col_count, row_count), jnp.float32),
            pltpu.VMEM((nbond, col_count, row_count), jnp.float32),
            pltpu.VMEM((nbond, col_count, row_count), jnp.float32),
            pltpu.SemaphoreType.DMA((5,)),
            pltpu.SemaphoreType.DMA((2, ply_count)),
            pltpu.SemaphoreType.DMA((2, ply_count)),
        ],
        compiler_params=pltpu.CompilerParams(collective_id=0, has_side_effects=True),
    )(angle_index, bond_table, interface_stiffness, displacement)
    peers = lax.axis_size("ply")
    up = [(i, i + 1) for i in range(peers - 1)]
    down = [(i + 1, i) for i in range(peers - 1)]
    lo = lax.ppermute(displacement[:, ply_count - 1], "ply", up)
    hi = lax.ppermute(displacement[:, 0], "ply", down)
    zero_end = jnp.zeros((1,), jnp.float32)
    coupling = jnp.concatenate([zero_end, interface_stiffness, zero_end])
    local_coupling = lax.dynamic_slice_in_dim(
        coupling, lax.axis_index("ply") * ply_count, ply_count + 1
    )
    first = force[:, 0] + local_coupling[0] * (lo - displacement[:, 0])
    last = force[:, ply_count - 1] + local_coupling[ply_count] * (
        hi - displacement[:, ply_count - 1])
    return force.at[:, 0].set(first).at[:, ply_count - 1].set(last)


def solution(mesh):
    placed = (P(None, "ply", "tile", None), P("ply"), P(), P())
    return jax.shard_map(
        local, mesh=mesh, in_specs=placed, out_specs=P(None, "ply", "tile", None), check_vma=False
    )
```

```python
import math

import jax
import jax.numpy as jnp
from jax import lax
from jax.experimental import pallas as pl
from jax.experimental.pallas import tpu as pltpu
from jax.sharding import PartitionSpec as P

bulk_modulus = 40.0


def bond_list():
    halves = []
    for shift_x in range(-3, 4):
        for shift_y in range(-3, 4):
            radius = shift_x * shift_x + shift_y * shift_y
            if 0 < radius <= 9 and (shift_x > 0 or (shift_x == 0 and shift_y > 0)):
                halves.append((shift_x, shift_y))
    result = []
    for shift_x in range(-3, 4):
        for shift_y in range(-3, 4):
            radius = shift_x * shift_x + shift_y * shift_y
            if 0 < radius <= 9:
                if (shift_x, shift_y) in halves:
                    column = halves.index((shift_x, shift_y))
                else:
                    column = halves.index((-shift_x, -shift_y))
                result.append((shift_x, shift_y, math.sqrt(radius), column))
    return result


def halo(shard, axis, dim, width):
    peers, length = lax.axis_size(axis), shard.shape[dim]
    up = [(i, (i + 1) % peers) for i in range(peers)]
    down = [(j, i) for i, j in up]
    last = lax.slice_in_dim(shard, length - width, length, axis=dim)
    first = lax.slice_in_dim(shard, 0, width, axis=dim)
    before = lax.ppermute(last, axis, up)
    after = lax.ppermute(first, axis, down)
    return jnp.concatenate([before, shard, after], axis=dim)


def shift_lanes(x, b):
    if b == 0:
        return x
    return pltpu.roll(x, (-b) % x.shape[-1], 1)


MESH = pl.DeviceIdType.MESH


def make_kernel(plies, cols, rows, x_total, nsprings):
    bonds = bond_list()
    wide = cols + 6
    shifts = sorted({a for a, _, _, _ in bonds})
    lanes = sorted({b for _, b, _, _ in bonds})

    def kernel(angle_ref, table_ref, spring_ref, u_hbm, o_ref, ext, ply_halo, wq_ref, fmask_ref,
               hmask_ref, wm_ref, sx_ref, sy_ref, sz_ref, pa_ref, pb_ref, qx_ref, sems, send_t,
               recv_t, send_q, recv_q):
        t = lax.axis_index("tile")
        nt = lax.axis_size("tile")
        q = lax.axis_index("ply")
        nq = lax.axis_size("ply")
        x0 = t * cols
        own = pltpu.make_async_copy(u_hbm, ext.at[:, :, cols:2 * cols, :], sems.at[0])
        own.start()
        has = ((t > 0), (t < nt - 1), (q > 0), (q < nq - 1))
        peers = ({"tile": t - 1}, {"tile": t + 1}, {"ply": q - 1}, {"ply": q + 1})
        barrier = pltpu.get_barrier_semaphore()
        for cond, dev in zip(has, peers):
            @pl.when(cond)
            def _():
                pl.semaphore_signal(barrier, inc=1, device_id=dev, device_id_type=MESH)
        count = sum(c.astype(jnp.int32) for c in has)
        pl.semaphore_wait(barrier, count)
        def tile_copy(d, p):
            if d == 0:
                src, dst = slice(0, 3), slice(2 * cols, 2 * cols + 3)
            else:
                src, dst = slice(cols - 3, cols), slice(cols - 3, cols)
            return pltpu.make_async_remote_copy(
                u_hbm.at[:, p, src, :], ext.at[:, p, dst, :], send_t.at[d, p], recv_t.at[d, p],
                device_id=peers[d], device_id_type=MESH)

        def q_copy(d, p):
            if d == 0:
                src, dst = slice(cols, cols + 3), slice(2 * cols, 2 * cols + 3)
            else:
                src, dst = slice(2 * cols - 3, 2 * cols), slice(cols - 3, cols)
            return pltpu.make_async_remote_copy(
                qx_ref.at[p, src, :], qx_ref.at[p, dst, :], send_q.at[d, p], recv_q.at[d, p],
                device_id=peers[d], device_id_type=MESH)

        ply_copies = (
            pltpu.make_async_remote_copy(
                u_hbm.at[:, 0], ply_halo.at[1], sems.at[1], sems.at[3],
                device_id=peers[2], device_id_type=MESH),
            pltpu.make_async_remote_copy(
                u_hbm.at[:, plies - 1], ply_halo.at[0], sems.at[2], sems.at[4],
                device_id=peers[3], device_id_type=MESH),
        )
        ahead = min(2, plies)
        for p in range(ahead):
            for d in range(2):
                pl.when(has[d])(tile_copy(d, p).start)
        for cond, cp in zip(has[2:], ply_copies):
            pl.when(cond)(cp.start)

        sub = lax.broadcasted_iota(jnp.int32, (cols, rows), 0)
        lane = lax.broadcasted_iota(jnp.int32, (cols, rows), 1)
        core_x = sub + x0
        edge_x = jnp.where(sub < 3, x0 - 3 + sub, x0 + cols - 3 + sub)
        edge_ok = sub < 6

        def bond_masks(xg, ok0, out_ref):
            own_x = ok0 & (xg >= 0) & (xg < x_total)
            total = jnp.zeros((cols, rows), jnp.float32)
            for i, (a, b, length, column) in enumerate(bonds):
                ok = own_x & (xg + a >= 0) & (xg + a < x_total) & (lane + b >= 0) & (lane + b < rows)
                m = jnp.where(ok, 1.0, 0.0)
                out_ref[i] = m
                total = total + m * length
            return total

        mass_c = bond_masks(core_x, sub >= 0, fmask_ref)
        mass_e = bond_masks(edge_x, edge_ok, hmask_ref)
        w_c = 1.0 / jnp.where(mass_c > 0, mass_c, 1.0)
        w_e = jnp.where(mass_e > 0, 1.0 / jnp.where(mass_e > 0, mass_e, 1.0), 0.0)
        wq_ref[0, 0:3, :] = w_e[0:3]
        wq_ref[0, 3:3 + cols, :] = w_c
        wq_ref[0, 3 + cols:6 + cols, :] = w_e[3:6]
        groups = {}
        for i, (a, b, length, column) in enumerate(bonds):
            groups.setdefault(a, []).append((i, b, length, column))
        for a, members in groups.items():
            w_slab = wq_ref[0, 3 + a:3 + a + cols, :]
            for i, b, length, column in members:
                wm_ref[i] = fmask_ref[i] * (w_c + shift_lanes(w_slab, b))

        @pl.when(t == 0)
        def _():
            ext[:, :, 0:cols, :] = jnp.zeros((3, plies, cols, rows), jnp.float32)
            qx_ref[:, 0:cols, :] = jnp.zeros((plies, cols, rows), jnp.float32)

        @pl.when(t == nt - 1)
        def _():
            ext[:, :, 2 * cols:3 * cols, :] = jnp.zeros((3, plies, cols, rows), jnp.float32)
            qx_ref[:, 2 * cols:3 * cols, :] = jnp.zeros((plies, cols, rows), jnp.float32)

        @pl.when(q == 0)
        def _():
            ply_halo[0] = jnp.zeros((3, cols, rows), jnp.float32)

        @pl.when(q == nq - 1)
        def _():
            ply_halo[1] = jnp.zeros((3, cols, rows), jnp.float32)

        own.wait()

        def dil_phase(p):
            slot = p % 2
            for d in range(2):
                pl.when(has[d] & (p + ahead < plies))(
                    lambda d=d: tile_copy(d, jnp.minimum(p + ahead, plies - 1)).start())
            pl.when(has[1])(tile_copy(0, p).wait_recv)
            pl.when(has[0])(tile_copy(1, p).wait_recv)
            uc = [ext[k, p, cols:2 * cols, :] for k in range(3)]
            uc_y = {b: uc[1] - b for b in lanes}
            dil_c = jnp.zeros((cols, rows), jnp.float32)
            for a, members in groups.items():
                cs = [ext[k, p, cols + a:2 * cols + a, :] for k in range(3)]
                uc_x = uc[0] - a
                for i, b, length, column in members:
                    sx = shift_lanes(cs[0], b) - uc_x
                    sy = shift_lanes(cs[1], b) - uc_y[b]
                    sz = shift_lanes(cs[2], b) - uc[2]
                    s2 = sx * sx + sy * sy + sz * sz
                    inv = lax.rsqrt(s2)
                    e = s2 * inv - length
                    m = fmask_ref[i]
                    dil_c = dil_c + e * m
                    sx_ref[slot, i] = sx
                    sy_ref[slot, i] = sy
                    sz_ref[slot, i] = sz
                    pa_ref[slot, i] = (inv * e) * wm_ref[i]
                    pb_ref[slot, i] = inv * m
            qx_ref[p, cols:2 * cols, :] = (3.0 * dil_c * w_c) * w_c
            for d in range(2):
                pl.when(has[d])(q_copy(d, p).start)

        def force_phase(p):
            slot = p % 2
            gp = q * plies + p
            kind = angle_ref[p]
            pl.when(has[1])(q_copy(0, p).wait_recv)
            pl.when(has[0])(q_copy(1, p).wait_recv)
            uc = [ext[k, p, cols:2 * cols, :] for k in range(3)]
            q_c = qx_ref[p, cols:2 * cols, :]
            fx = jnp.zeros((cols, rows), jnp.float32)
            fy = jnp.zeros((cols, rows), jnp.float32)
            fz = jnp.zeros((cols, rows), jnp.float32)
            for a, members in groups.items():
                q_slab = qx_ref[p, cols + a:2 * cols + a, :]
                for i, b, length, column in members:
                    shear = table_ref[kind, column]
                    alpha = shear * (15.0 / length)
                    beta = 3.0 * bulk_modulus - 5.0 * shear
                    f = alpha * pa_ref[slot, i] + beta * (
                        pb_ref[slot, i] * (q_c + shift_lanes(q_slab, b)))
                    fx = fx + f * sx_ref[slot, i]
                    fy = fy + f * sy_ref[slot, i]
                    fz = fz + f * sz_ref[slot, i]
            above = jnp.where(gp < nsprings, spring_ref[jnp.minimum(gp, nsprings - 1)], 0.0)
            below = jnp.where(gp > 0, spring_ref[jnp.maximum(gp - 1, 0)], 0.0)
            hi_p = jnp.minimum(p + 1, plies - 1)
            lo_p = jnp.maximum(p - 1, 0)
            for k, fk in enumerate((fx, fy, fz)):
                hi = jnp.where(p == plies - 1, uc[k], ext[k, hi_p, cols:2 * cols, :])
                lo = jnp.where(p == 0, uc[k], ext[k, lo_p, cols:2 * cols, :])
                o_ref[k, p] = fk + (above * (hi - uc[k]) + below * (lo - uc[k]))

        dil_phase(0)

        def ply_body(p, carry):
            pl.when(p + 1 < plies)(lambda: dil_phase(jnp.minimum(p + 1, plies - 1)))
            force_phase(p)
            return carry

        lax.fori_loop(0, plies, ply_body, 0)
        pl.when(has[3])(ply_copies[0].wait_recv)
        pl.when(has[2])(ply_copies[1].wait_recv)
        g0 = q * plies
        below = jnp.where(g0 > 0, spring_ref[jnp.maximum(g0 - 1, 0)], 0.0)
        gl = q * plies + plies - 1
        above = jnp.where(gl < nsprings, spring_ref[jnp.minimum(gl, nsprings - 1)], 0.0)
        for k in range(3):
            o_ref[k, 0] = o_ref[k, 0] + below * (ply_halo[0, k] - ext[k, 0, cols:2 * cols, :])
            o_ref[k, plies - 1] = o_ref[k, plies - 1] + above * (
                ply_halo[1, k] - ext[k, plies - 1, cols:2 * cols, :])
        for p in range(plies):
            for d in range(2):
                pl.when(has[d])(tile_copy(d, p).wait_send)
                pl.when(has[d])(q_copy(d, p).wait_send)
        for cond, cp in zip(has[2:], ply_copies):
            pl.when(cond)(cp.wait_send)

    return kernel


def local(displacement, angle_index, bond_table, interface_stiffness):
    comp_count, ply_count, col_count, row_count = displacement.shape
    x_total = col_count * lax.axis_size("tile")
    kernel = make_kernel(ply_count, col_count, row_count, x_total, interface_stiffness.shape[0])
    nbond = len(bond_list())
    smem = pl.BlockSpec(memory_space=pltpu.SMEM)
    return pl.pallas_call(
        kernel,
        in_specs=[smem, smem, smem, pl.BlockSpec(memory_space=pl.ANY)],
        out_specs=pl.BlockSpec(memory_space=pltpu.VMEM),
        out_shape=jax.ShapeDtypeStruct(displacement.shape, jnp.float32),
        scratch_shapes=[
            pltpu.VMEM((3, ply_count, 3 * col_count, row_count), jnp.float32),
            pltpu.VMEM((2, 3, col_count, row_count), jnp.float32),
            pltpu.VMEM((2, col_count + 6, row_count), jnp.float32),
            pltpu.VMEM((nbond, col_count, row_count), jnp.float32),
            pltpu.VMEM((nbond, col_count, row_count), jnp.float32),
            pltpu.VMEM((nbond, col_count, row_count), jnp.float32),
            pltpu.VMEM((2, nbond, col_count, row_count), jnp.float32),
            pltpu.VMEM((2, nbond, col_count, row_count), jnp.float32),
            pltpu.VMEM((2, nbond, col_count, row_count), jnp.float32),
            pltpu.VMEM((2, nbond, col_count, row_count), jnp.float32),
            pltpu.VMEM((2, nbond, col_count, row_count), jnp.float32),
            pltpu.VMEM((ply_count, 3 * col_count, row_count), jnp.float32),
            pltpu.SemaphoreType.DMA((5,)),
            pltpu.SemaphoreType.DMA((2, ply_count)),
            pltpu.SemaphoreType.DMA((2, ply_count)),
            pltpu.SemaphoreType.DMA((2, ply_count)),
            pltpu.SemaphoreType.DMA((2, ply_count)),
        ],
        compiler_params=pltpu.CompilerParams(collective_id=0, has_side_effects=True),
    )(angle_index, bond_table, interface_stiffness, displacement)


def solution(mesh):
    placed = (P(None, "ply", "tile", None), P("ply"), P(), P())
    return jax.shard_map(
        local, mesh=mesh, in_specs=placed, out_specs=P(None, "ply", "tile", None), check_vma=False
    )
```

```python
import math

import jax
import jax.numpy as jnp
from jax import lax
from jax.experimental import pallas as pl
from jax.experimental.pallas import tpu as pltpu
from jax.sharding import PartitionSpec as P

bulk_modulus = 40.0


def bond_list():
    halves = []
    for shift_x in range(-3, 4):
        for shift_y in range(-3, 4):
            radius = shift_x * shift_x + shift_y * shift_y
            if 0 < radius <= 9 and (shift_x > 0 or (shift_x == 0 and shift_y > 0)):
                halves.append((shift_x, shift_y))
    result = []
    for shift_x in range(-3, 4):
        for shift_y in range(-3, 4):
            radius = shift_x * shift_x + shift_y * shift_y
            if 0 < radius <= 9:
                if (shift_x, shift_y) in halves:
                    column = halves.index((shift_x, shift_y))
                else:
                    column = halves.index((-shift_x, -shift_y))
                result.append((shift_x, shift_y, math.sqrt(radius), column))
    return result


def halo(shard, axis, dim, width):
    peers, length = lax.axis_size(axis), shard.shape[dim]
    up = [(i, (i + 1) % peers) for i in range(peers)]
    down = [(j, i) for i, j in up]
    last = lax.slice_in_dim(shard, length - width, length, axis=dim)
    first = lax.slice_in_dim(shard, 0, width, axis=dim)
    before = lax.ppermute(last, axis, up)
    after = lax.ppermute(first, axis, down)
    return jnp.concatenate([before, shard, after], axis=dim)


def shift_lanes(x, b):
    if b == 0:
        return x
    return pltpu.roll(x, (-b) % x.shape[-1], 1)


MESH = pl.DeviceIdType.MESH


def make_kernel(plies, cols, rows, x_total, nsprings):
    bonds = bond_list()
    wide = cols + 6
    shifts = sorted({a for a, _, _, _ in bonds})
    lanes = sorted({b for _, b, _, _ in bonds})

    def kernel(angle_ref, table_ref, spring_ref, u_hbm, o_ref, ext, ply_halo, wq_ref, fmask_ref,
               hmask_ref, wm_ref, qx_ref, sems, send_t,
               recv_t, send_q, recv_q):
        t = lax.axis_index("tile")
        nt = lax.axis_size("tile")
        q = lax.axis_index("ply")
        nq = lax.axis_size("ply")
        x0 = t * cols
        own = pltpu.make_async_copy(u_hbm, ext.at[:, :, cols:2 * cols, :], sems.at[0])
        own.start()
        has = ((t > 0), (t < nt - 1), (q > 0), (q < nq - 1))
        peers = ({"tile": t - 1}, {"tile": t + 1}, {"ply": q - 1}, {"ply": q + 1})
        barrier = pltpu.get_barrier_semaphore()
        for cond, dev in zip(has, peers):
            @pl.when(cond)
            def _():
                pl.semaphore_signal(barrier, inc=1, device_id=dev, device_id_type=MESH)
        count = sum(c.astype(jnp.int32) for c in has)
        pl.semaphore_wait(barrier, count)
        def tile_copy(d, p):
            if d == 0:
                src, dst = slice(0, 3), slice(2 * cols, 2 * cols + 3)
            else:
                src, dst = slice(cols - 3, cols), slice(cols - 3, cols)
            return pltpu.make_async_remote_copy(
                u_hbm.at[:, p, src, :], ext.at[:, p, dst, :], send_t.at[d, p], recv_t.at[d, p],
                device_id=peers[d], device_id_type=MESH)

        def q_copy(d, p):
            if d == 0:
                src, dst = slice(cols, cols + 3), slice(2 * cols, 2 * cols + 3)
            else:
                src, dst = slice(2 * cols - 3, 2 * cols), slice(cols - 3, cols)
            return pltpu.make_async_remote_copy(
                qx_ref.at[p, src, :], qx_ref.at[p, dst, :], send_q.at[d, p], recv_q.at[d, p],
                device_id=peers[d], device_id_type=MESH)

        ply_copies = (
            pltpu.make_async_remote_copy(
                u_hbm.at[:, 0], ply_halo.at[1], sems.at[1], sems.at[3],
                device_id=peers[2], device_id_type=MESH),
            pltpu.make_async_remote_copy(
                u_hbm.at[:, plies - 1], ply_halo.at[0], sems.at[2], sems.at[4],
                device_id=peers[3], device_id_type=MESH),
        )
        ahead = min(2, plies)
        for p in range(ahead):
            for d in range(2):
                pl.when(has[d])(tile_copy(d, p).start)
        for cond, cp in zip(has[2:], ply_copies):
            pl.when(cond)(cp.start)

        sub = lax.broadcasted_iota(jnp.int32, (cols, rows), 0)
        lane = lax.broadcasted_iota(jnp.int32, (cols, rows), 1)
        core_x = sub + x0
        edge_x = jnp.where(sub < 3, x0 - 3 + sub, x0 + cols - 3 + sub)
        edge_ok = sub < 6

        def bond_masks(xg, ok0, out_ref):
            own_x = ok0 & (xg >= 0) & (xg < x_total)
            total = jnp.zeros((cols, rows), jnp.float32)
            for i, (a, b, length, column) in enumerate(bonds):
                ok = own_x & (xg + a >= 0) & (xg + a < x_total) & (lane + b >= 0) & (lane + b < rows)
                m = jnp.where(ok, 1.0, 0.0)
                out_ref[i] = m
                total = total + m * length
            return total

        mass_c = bond_masks(core_x, sub >= 0, fmask_ref)
        mass_e = bond_masks(edge_x, edge_ok, hmask_ref)
        w_c = 1.0 / jnp.where(mass_c > 0, mass_c, 1.0)
        w_e = jnp.where(mass_e > 0, 1.0 / jnp.where(mass_e > 0, mass_e, 1.0), 0.0)
        wq_ref[0, 0:3, :] = w_e[0:3]
        wq_ref[0, 3:3 + cols, :] = w_c
        wq_ref[0, 3 + cols:6 + cols, :] = w_e[3:6]
        groups = {}
        for i, (a, b, length, column) in enumerate(bonds):
            groups.setdefault(a, []).append((i, b, length, column))
        for a, members in groups.items():
            w_slab = wq_ref[0, 3 + a:3 + a + cols, :]
            for i, b, length, column in members:
                wm_ref[i] = fmask_ref[i] * (w_c + shift_lanes(w_slab, b))

        @pl.when(t == 0)
        def _():
            ext[:, :, 0:cols, :] = jnp.zeros((3, plies, cols, rows), jnp.float32)
            qx_ref[:, 0:cols, :] = jnp.zeros((plies, cols, rows), jnp.float32)

        @pl.when(t == nt - 1)
        def _():
            ext[:, :, 2 * cols:3 * cols, :] = jnp.zeros((3, plies, cols, rows), jnp.float32)
            qx_ref[:, 2 * cols:3 * cols, :] = jnp.zeros((plies, cols, rows), jnp.float32)

        @pl.when(q == 0)
        def _():
            ply_halo[0] = jnp.zeros((3, cols, rows), jnp.float32)

        @pl.when(q == nq - 1)
        def _():
            ply_halo[1] = jnp.zeros((3, cols, rows), jnp.float32)

        own.wait()

        def dil_phase(p):
            slot = p % 2
            for d in range(2):
                pl.when(has[d] & (p + ahead < plies))(
                    lambda d=d: tile_copy(d, jnp.minimum(p + ahead, plies - 1)).start())
            pl.when(has[1])(tile_copy(0, p).wait_recv)
            pl.when(has[0])(tile_copy(1, p).wait_recv)
            uc = [ext[k, p, cols:2 * cols, :] for k in range(3)]
            uc_y = {b: uc[1] - b for b in lanes}
            dil_c = jnp.zeros((cols, rows), jnp.float32)
            for a, members in groups.items():
                cs = [ext[k, p, cols + a:2 * cols + a, :] for k in range(3)]
                uc_x = uc[0] - a
                for i, b, length, column in members:
                    sx = shift_lanes(cs[0], b) - uc_x
                    sy = shift_lanes(cs[1], b) - uc_y[b]
                    sz = shift_lanes(cs[2], b) - uc[2]
                    s2 = sx * sx + sy * sy + sz * sz
                    inv = lax.rsqrt(s2)
                    dil_c = dil_c + (s2 * inv - length) * fmask_ref[i]
            qx_ref[p, cols:2 * cols, :] = (3.0 * dil_c * w_c) * w_c
            for d in range(2):
                pl.when(has[d])(q_copy(d, p).start)

        def force_phase(p):
            slot = p % 2
            gp = q * plies + p
            kind = angle_ref[p]
            pl.when(has[1])(q_copy(0, p).wait_recv)
            pl.when(has[0])(q_copy(1, p).wait_recv)
            uc = [ext[k, p, cols:2 * cols, :] for k in range(3)]
            uc_y = {b: uc[1] - b for b in lanes}
            q_c = qx_ref[p, cols:2 * cols, :]
            fx = jnp.zeros((cols, rows), jnp.float32)
            fy = jnp.zeros((cols, rows), jnp.float32)
            fz = jnp.zeros((cols, rows), jnp.float32)
            for a, members in groups.items():
                cs = [ext[k, p, cols + a:2 * cols + a, :] for k in range(3)]
                uc_x = uc[0] - a
                q_slab = qx_ref[p, cols + a:2 * cols + a, :]
                for i, b, length, column in members:
                    sx = shift_lanes(cs[0], b) - uc_x
                    sy = shift_lanes(cs[1], b) - uc_y[b]
                    sz = shift_lanes(cs[2], b) - uc[2]
                    s2 = sx * sx + sy * sy + sz * sz
                    inv = lax.rsqrt(s2)
                    e = s2 * inv - length
                    shear = table_ref[kind, column]
                    alpha = shear * (15.0 / length)
                    beta = 3.0 * bulk_modulus - 5.0 * shear
                    tb = alpha * e * wm_ref[i] + beta * (
                        fmask_ref[i] * (q_c + shift_lanes(q_slab, b)))
                    f = tb * inv
                    fx = fx + f * sx
                    fy = fy + f * sy
                    fz = fz + f * sz
            above = jnp.where(gp < nsprings, spring_ref[jnp.minimum(gp, nsprings - 1)], 0.0)
            below = jnp.where(gp > 0, spring_ref[jnp.maximum(gp - 1, 0)], 0.0)
            hi_p = jnp.minimum(p + 1, plies - 1)
            lo_p = jnp.maximum(p - 1, 0)
            for k, fk in enumerate((fx, fy, fz)):
                hi = jnp.where(p == plies - 1, uc[k], ext[k, hi_p, cols:2 * cols, :])
                lo = jnp.where(p == 0, uc[k], ext[k, lo_p, cols:2 * cols, :])
                o_ref[k, p] = fk + (above * (hi - uc[k]) + below * (lo - uc[k]))

        def dil_body(p, carry):
            dil_phase(p)
            return carry

        def force_body(p, carry):
            force_phase(p)
            return carry

        lax.fori_loop(0, plies, dil_body, 0)
        lax.fori_loop(0, plies, force_body, 0)
        pl.when(has[3])(ply_copies[0].wait_recv)
        pl.when(has[2])(ply_copies[1].wait_recv)
        g0 = q * plies
        below = jnp.where(g0 > 0, spring_ref[jnp.maximum(g0 - 1, 0)], 0.0)
        gl = q * plies + plies - 1
        above = jnp.where(gl < nsprings, spring_ref[jnp.minimum(gl, nsprings - 1)], 0.0)
        for k in range(3):
            o_ref[k, 0] = o_ref[k, 0] + below * (ply_halo[0, k] - ext[k, 0, cols:2 * cols, :])
            o_ref[k, plies - 1] = o_ref[k, plies - 1] + above * (
                ply_halo[1, k] - ext[k, plies - 1, cols:2 * cols, :])
        for p in range(plies):
            for d in range(2):
                pl.when(has[d])(tile_copy(d, p).wait_send)
                pl.when(has[d])(q_copy(d, p).wait_send)
        for cond, cp in zip(has[2:], ply_copies):
            pl.when(cond)(cp.wait_send)

    return kernel


def local(displacement, angle_index, bond_table, interface_stiffness):
    comp_count, ply_count, col_count, row_count = displacement.shape
    x_total = col_count * lax.axis_size("tile")
    kernel = make_kernel(ply_count, col_count, row_count, x_total, interface_stiffness.shape[0])
    nbond = len(bond_list())
    smem = pl.BlockSpec(memory_space=pltpu.SMEM)
    return pl.pallas_call(
        kernel,
        in_specs=[smem, smem, smem, pl.BlockSpec(memory_space=pl.ANY)],
        out_specs=pl.BlockSpec(memory_space=pltpu.VMEM),
        out_shape=jax.ShapeDtypeStruct(displacement.shape, jnp.float32),
        scratch_shapes=[
            pltpu.VMEM((3, ply_count, 3 * col_count, row_count), jnp.float32),
            pltpu.VMEM((2, 3, col_count, row_count), jnp.float32),
            pltpu.VMEM((2, col_count + 6, row_count), jnp.float32),
            pltpu.VMEM((nbond, col_count, row_count), jnp.float32),
            pltpu.VMEM((nbond, col_count, row_count), jnp.float32),
            pltpu.VMEM((nbond, col_count, row_count), jnp.float32),
            pltpu.VMEM((ply_count, 3 * col_count, row_count), jnp.float32),
            pltpu.SemaphoreType.DMA((5,)),
            pltpu.SemaphoreType.DMA((2, ply_count)),
            pltpu.SemaphoreType.DMA((2, ply_count)),
            pltpu.SemaphoreType.DMA((2, ply_count)),
            pltpu.SemaphoreType.DMA((2, ply_count)),
        ],
        compiler_params=pltpu.CompilerParams(collective_id=0, has_side_effects=True),
    )(angle_index, bond_table, interface_stiffness, displacement)


def solution(mesh):
    placed = (P(None, "ply", "tile", None), P("ply"), P(), P())
    return jax.shard_map(
        local, mesh=mesh, in_specs=placed, out_specs=P(None, "ply", "tile", None), check_vma=False
    )
```

```python
import math

import jax
import jax.numpy as jnp
from jax import lax
from jax.experimental import pallas as pl
from jax.experimental.pallas import tpu as pltpu
from jax.sharding import PartitionSpec as P

bulk_modulus = 40.0


def bond_list():
    halves = []
    for shift_x in range(-3, 4):
        for shift_y in range(-3, 4):
            radius = shift_x * shift_x + shift_y * shift_y
            if 0 < radius <= 9 and (shift_x > 0 or (shift_x == 0 and shift_y > 0)):
                halves.append((shift_x, shift_y))
    result = []
    for shift_x in range(-3, 4):
        for shift_y in range(-3, 4):
            radius = shift_x * shift_x + shift_y * shift_y
            if 0 < radius <= 9:
                if (shift_x, shift_y) in halves:
                    column = halves.index((shift_x, shift_y))
                else:
                    column = halves.index((-shift_x, -shift_y))
                result.append((shift_x, shift_y, math.sqrt(radius), column))
    return result


def halo(shard, axis, dim, width):
    peers, length = lax.axis_size(axis), shard.shape[dim]
    up = [(i, (i + 1) % peers) for i in range(peers)]
    down = [(j, i) for i, j in up]
    last = lax.slice_in_dim(shard, length - width, length, axis=dim)
    first = lax.slice_in_dim(shard, 0, width, axis=dim)
    before = lax.ppermute(last, axis, up)
    after = lax.ppermute(first, axis, down)
    return jnp.concatenate([before, shard, after], axis=dim)


def shift_lanes(x, b):
    if b == 0:
        return x
    return pltpu.roll(x, (-b) % x.shape[-1], 1)


MESH = pl.DeviceIdType.MESH


def make_kernel(plies, cols, rows, x_total, nsprings):
    bonds = bond_list()
    wide = cols + 6
    shifts = sorted({a for a, _, _, _ in bonds})
    lanes = sorted({b for _, b, _, _ in bonds})

    def kernel(angle_ref, table_ref, spring_ref, u_hbm, o_ref, ext, ply_halo, wq_ref, fmask_ref,
               hmask_ref, wm_ref, sx_ref, sy_ref, sz_ref, pa_ref, pb_ref, sems, send_t, recv_t):
        t = lax.axis_index("tile")
        nt = lax.axis_size("tile")
        q = lax.axis_index("ply")
        nq = lax.axis_size("ply")
        x0 = t * cols
        own = pltpu.make_async_copy(u_hbm, ext.at[:, :, cols:2 * cols, :], sems.at[0])
        own.start()
        has = ((t > 0), (t < nt - 1), (q > 0), (q < nq - 1))
        peers = ({"tile": t - 1}, {"tile": t + 1}, {"ply": q - 1}, {"ply": q + 1})
        barrier = pltpu.get_barrier_semaphore()
        for cond, dev in zip(has, peers):
            @pl.when(cond)
            def _():
                pl.semaphore_signal(barrier, inc=1, device_id=dev, device_id_type=MESH)
        count = sum(c.astype(jnp.int32) for c in has)
        pl.semaphore_wait(barrier, count)
        def tile_copy(d, p):
            if d == 0:
                src, dst = slice(0, 6), slice(2 * cols, 2 * cols + 6)
            else:
                src, dst = slice(cols - 6, cols), slice(cols - 6, cols)
            return pltpu.make_async_remote_copy(
                u_hbm.at[:, p, src, :], ext.at[:, p, dst, :], send_t.at[d, p], recv_t.at[d, p],
                device_id=peers[d], device_id_type=MESH)

        ply_copies = (
            pltpu.make_async_remote_copy(
                u_hbm.at[:, 0], ply_halo.at[1], sems.at[1], sems.at[3],
                device_id=peers[2], device_id_type=MESH),
            pltpu.make_async_remote_copy(
                u_hbm.at[:, plies - 1], ply_halo.at[0], sems.at[2], sems.at[4],
                device_id=peers[3], device_id_type=MESH),
        )
        ahead = min(2, plies)
        for p in range(ahead):
            for d in range(2):
                pl.when(has[d])(tile_copy(d, p).start)

        sub = lax.broadcasted_iota(jnp.int32, (cols, rows), 0)
        lane = lax.broadcasted_iota(jnp.int32, (cols, rows), 1)
        core_x = sub + x0
        edge_x = jnp.where(sub < 3, x0 - 3 + sub, x0 + cols - 3 + sub)
        edge_ok = sub < 6

        def bond_masks(xg, ok0, out_ref):
            own_x = ok0 & (xg >= 0) & (xg < x_total)
            total = jnp.zeros((cols, rows), jnp.float32)
            for i, (a, b, length, column) in enumerate(bonds):
                ok = own_x & (xg + a >= 0) & (xg + a < x_total) & (lane + b >= 0) & (lane + b < rows)
                m = jnp.where(ok, 1.0, 0.0)
                out_ref[i] = m
                total = total + m * length
            return total

        mass_c = bond_masks(core_x, sub >= 0, fmask_ref)
        mass_e = bond_masks(edge_x, edge_ok, hmask_ref)
        w_c = 1.0 / jnp.where(mass_c > 0, mass_c, 1.0)
        w_e = jnp.where(mass_e > 0, 1.0 / jnp.where(mass_e > 0, mass_e, 1.0), 0.0)
        wq_ref[0, 0:3, :] = w_e[0:3]
        wq_ref[0, 3:3 + cols, :] = w_c
        wq_ref[0, 3 + cols:6 + cols, :] = w_e[3:6]
        groups = {}
        for i, (a, b, length, column) in enumerate(bonds):
            groups.setdefault(a, []).append((i, b, length, column))
        for a, members in groups.items():
            w_slab = wq_ref[0, 3 + a:3 + a + cols, :]
            for i, b, length, column in members:
                wm_ref[i] = fmask_ref[i] * (w_c + shift_lanes(w_slab, b))

        @pl.when(t == 0)
        def _():
            ext[:, :, 0:cols, :] = jnp.zeros((3, plies, cols, rows), jnp.float32)

        @pl.when(t == nt - 1)
        def _():
            ext[:, :, 2 * cols:3 * cols, :] = jnp.zeros((3, plies, cols, rows), jnp.float32)

        @pl.when(q == 0)
        def _():
            ply_halo[0] = jnp.zeros((3, cols, rows), jnp.float32)

        @pl.when(q == nq - 1)
        def _():
            ply_halo[1] = jnp.zeros((3, cols, rows), jnp.float32)

        own.wait()

        def ply_body(p, carry):
            for d in range(2):
                pl.when(has[d] & (p + ahead < plies))(
                    lambda d=d: tile_copy(d, jnp.minimum(p + ahead, plies - 1)).start())
            pl.when(has[1])(tile_copy(0, p).wait_recv)
            pl.when(has[0])(tile_copy(1, p).wait_recv)
            for cond, cp in zip(has[2:], ply_copies):
                pl.when(cond & (p == min(2, plies - 1)))(cp.start)
            gp = q * plies + p
            kind = angle_ref[p]
            low = lax.broadcasted_iota(jnp.int32, (cols, rows), 0) < 3

            def edge_rows(k, a):
                return jnp.where(low, ext[k, p, cols - 3 + a:2 * cols - 3 + a, :],
                                 ext[k, p, 2 * cols - 3 + a:3 * cols - 3 + a, :])

            uc = [ext[k, p, cols:2 * cols, :] for k in range(3)]
            ue = [edge_rows(k, 0) for k in range(3)]
            uc_y = {b: uc[1] - b for b in lanes}
            ue_y = {b: ue[1] - b for b in lanes}
            dil_c = jnp.zeros((cols, rows), jnp.float32)
            dil_e = jnp.zeros((cols, rows), jnp.float32)
            for a, members in groups.items():
                cs = [ext[k, p, cols + a:2 * cols + a, :] for k in range(3)]
                es = [edge_rows(k, a) for k in range(3)]
                uc_x = uc[0] - a
                ue_x = ue[0] - a
                for i, b, length, column in members:
                    sx = shift_lanes(cs[0], b) - uc_x
                    sy = shift_lanes(cs[1], b) - uc_y[b]
                    sz = shift_lanes(cs[2], b) - uc[2]
                    s2 = sx * sx + sy * sy + sz * sz
                    inv = lax.rsqrt(s2)
                    e = s2 * inv - length
                    m = fmask_ref[i]
                    dil_c = dil_c + e * m
                    sx_ref[i] = sx
                    sy_ref[i] = sy
                    sz_ref[i] = sz
                    pa_ref[i] = (inv * e) * wm_ref[i]
                    pb_ref[i] = inv * m
                    hx = shift_lanes(es[0], b) - ue_x
                    hy = shift_lanes(es[1], b) - ue_y[b]
                    hz = shift_lanes(es[2], b) - ue[2]
                    h2 = hx * hx + hy * hy + hz * hz
                    dil_e = dil_e + (h2 * lax.rsqrt(h2) - length) * hmask_ref[i]
            q_c = (3.0 * dil_c * w_c) * w_c
            q_e = (3.0 * dil_e * w_e) * w_e
            wq_ref[1, 0:3, :] = q_e[0:3]
            wq_ref[1, 3:3 + cols, :] = q_c
            wq_ref[1, 3 + cols:6 + cols, :] = q_e[3:6]

            fx = jnp.zeros((cols, rows), jnp.float32)
            fy = jnp.zeros((cols, rows), jnp.float32)
            fz = jnp.zeros((cols, rows), jnp.float32)
            for a, members in groups.items():
                q_slab = wq_ref[1, 3 + a:3 + a + cols, :]
                for i, b, length, column in members:
                    shear = table_ref[kind, column]
                    alpha = shear * (15.0 / length)
                    beta = 3.0 * bulk_modulus - 5.0 * shear
                    f = alpha * pa_ref[i] + beta * (pb_ref[i] * (q_c + shift_lanes(q_slab, b)))
                    fx = fx + f * sx_ref[i]
                    fy = fy + f * sy_ref[i]
                    fz = fz + f * sz_ref[i]
            above = jnp.where(gp < nsprings, spring_ref[jnp.minimum(gp, nsprings - 1)], 0.0)
            below = jnp.where(gp > 0, spring_ref[jnp.maximum(gp - 1, 0)], 0.0)
            hi_p = jnp.minimum(p + 1, plies - 1)
            lo_p = jnp.maximum(p - 1, 0)
            for k, fk in enumerate((fx, fy, fz)):
                hi = jnp.where(p == plies - 1, uc[k], ext[k, hi_p, cols:2 * cols, :])
                lo = jnp.where(p == 0, uc[k], ext[k, lo_p, cols:2 * cols, :])
                o_ref[k, p] = fk + (above * (hi - uc[k]) + below * (lo - uc[k]))
            return carry

        lax.fori_loop(0, plies, ply_body, 0)
        pl.when(has[3])(ply_copies[0].wait_recv)
        pl.when(has[2])(ply_copies[1].wait_recv)
        g0 = q * plies
        below = jnp.where(g0 > 0, spring_ref[jnp.maximum(g0 - 1, 0)], 0.0)
        gl = q * plies + plies - 1
        above = jnp.where(gl < nsprings, spring_ref[jnp.minimum(gl, nsprings - 1)], 0.0)
        for k in range(3):
            o_ref[k, 0] = o_ref[k, 0] + below * (ply_halo[0, k] - ext[k, 0, cols:2 * cols, :])
            o_ref[k, plies - 1] = o_ref[k, plies - 1] + above * (
                ply_halo[1, k] - ext[k, plies - 1, cols:2 * cols, :])
        for p in range(plies):
            for d in range(2):
                pl.when(has[d])(tile_copy(d, p).wait_send)
        for cond, cp in zip(has[2:], ply_copies):
            pl.when(cond)(cp.wait_send)

    return kernel


def local(displacement, angle_index, bond_table, interface_stiffness):
    comp_count, ply_count, col_count, row_count = displacement.shape
    x_total = col_count * lax.axis_size("tile")
    kernel = make_kernel(ply_count, col_count, row_count, x_total, interface_stiffness.shape[0])
    nbond = len(bond_list())
    smem = pl.BlockSpec(memory_space=pltpu.SMEM)
    return pl.pallas_call(
        kernel,
        in_specs=[smem, smem, smem, pl.BlockSpec(memory_space=pl.ANY)],
        out_specs=pl.BlockSpec(memory_space=pltpu.VMEM),
        out_shape=jax.ShapeDtypeStruct(displacement.shape, jnp.float32),
        scratch_shapes=[
            pltpu.VMEM((3, ply_count, 3 * col_count, row_count), jnp.float32),
            pltpu.VMEM((2, 3, col_count, row_count), jnp.float32),
            pltpu.VMEM((2, col_count + 6, row_count), jnp.float32),
            pltpu.VMEM((nbond, col_count, row_count), jnp.float32),
            pltpu.VMEM((nbond, col_count, row_count), jnp.float32),
            pltpu.VMEM((nbond, col_count, row_count), jnp.float32),
            pltpu.VMEM((nbond, col_count, row_count), jnp.float32),
            pltpu.VMEM((nbond, col_count, row_count), jnp.float32),
            pltpu.VMEM((nbond, col_count, row_count), jnp.float32),
            pltpu.VMEM((nbond, col_count, row_count), jnp.float32),
            pltpu.VMEM((nbond, col_count, row_count), jnp.float32),
            pltpu.SemaphoreType.DMA((5,)),
            pltpu.SemaphoreType.DMA((2, ply_count)),
            pltpu.SemaphoreType.DMA((2, ply_count)),
        ],
        compiler_params=pltpu.CompilerParams(collective_id=0, has_side_effects=True),
    )(angle_index, bond_table, interface_stiffness, displacement)


def solution(mesh):
    placed = (P(None, "ply", "tile", None), P("ply"), P(), P())
    return jax.shard_map(
        local, mesh=mesh, in_specs=placed, out_specs=P(None, "ply", "tile", None), check_vma=False
    )
```

```python
import math

import jax
import jax.numpy as jnp
from jax import lax
from jax.experimental import pallas as pl
from jax.experimental.pallas import tpu as pltpu
from jax.sharding import PartitionSpec as P

bulk_modulus = 40.0


def bond_list():
    halves = []
    for shift_x in range(-3, 4):
        for shift_y in range(-3, 4):
            radius = shift_x * shift_x + shift_y * shift_y
            if 0 < radius <= 9 and (shift_x > 0 or (shift_x == 0 and shift_y > 0)):
                halves.append((shift_x, shift_y))
    result = []
    for shift_x in range(-3, 4):
        for shift_y in range(-3, 4):
            radius = shift_x * shift_x + shift_y * shift_y
            if 0 < radius <= 9:
                if (shift_x, shift_y) in halves:
                    column = halves.index((shift_x, shift_y))
                else:
                    column = halves.index((-shift_x, -shift_y))
                result.append((shift_x, shift_y, math.sqrt(radius), column))
    return result


def halo(shard, axis, dim, width):
    peers, length = lax.axis_size(axis), shard.shape[dim]
    up = [(i, (i + 1) % peers) for i in range(peers)]
    down = [(j, i) for i, j in up]
    last = lax.slice_in_dim(shard, length - width, length, axis=dim)
    first = lax.slice_in_dim(shard, 0, width, axis=dim)
    before = lax.ppermute(last, axis, up)
    after = lax.ppermute(first, axis, down)
    return jnp.concatenate([before, shard, after], axis=dim)


def shift_lanes(x, b):
    if b == 0:
        return x
    return pltpu.roll(x, (-b) % x.shape[-1], 1)


MESH = pl.DeviceIdType.MESH


def make_kernel(plies, cols, rows, x_total, nsprings):
    bonds = bond_list()
    wide = cols + 6
    shifts = sorted({a for a, _, _, _ in bonds})
    lanes = sorted({b for _, b, _, _ in bonds})

    def kernel(angle_ref, table_ref, spring_ref, u_hbm, o_ref, ext, ply_halo, wq_ref, fmask_ref,
               hmask_ref, wm_ref, sx_ref, sy_ref, sz_ref, pa_ref, pb_ref, sems, send_t, recv_t):
        t = lax.axis_index("tile")
        nt = lax.axis_size("tile")
        q = lax.axis_index("ply")
        nq = lax.axis_size("ply")
        x0 = t * cols
        own = pltpu.make_async_copy(u_hbm, ext.at[:, :, cols:2 * cols, :], sems.at[0])
        own.start()
        has = ((t > 0), (t < nt - 1), (q > 0), (q < nq - 1))
        peers = ({"tile": t - 1}, {"tile": t + 1}, {"ply": q - 1}, {"ply": q + 1})
        barrier = pltpu.get_barrier_semaphore()
        for cond, dev in zip(has, peers):
            @pl.when(cond)
            def _():
                pl.semaphore_signal(barrier, inc=1, device_id=dev, device_id_type=MESH)
        count = sum(c.astype(jnp.int32) for c in has)
        pl.semaphore_wait(barrier, count)
        def tile_copy(d, p):
            if d == 0:
                src, dst = slice(0, 6), slice(2 * cols, 2 * cols + 6)
            else:
                src, dst = slice(cols - 6, cols), slice(cols - 6, cols)
            return pltpu.make_async_remote_copy(
                u_hbm.at[:, p, src, :], ext.at[:, p, dst, :], send_t.at[d, p], recv_t.at[d, p],
                device_id=peers[d], device_id_type=MESH)

        ply_copies = (
            pltpu.make_async_remote_copy(
                u_hbm.at[:, 0], ply_halo.at[1], sems.at[1], sems.at[3],
                device_id=peers[2], device_id_type=MESH),
            pltpu.make_async_remote_copy(
                u_hbm.at[:, plies - 1], ply_halo.at[0], sems.at[2], sems.at[4],
                device_id=peers[3], device_id_type=MESH),
        )
        ahead = 1
        for p in range(ahead):
            for d in range(2):
                pl.when(has[d])(tile_copy(d, p).start)
        for cond, cp in zip(has[2:], ply_copies):
            pl.when(cond)(cp.start)

        sub = lax.broadcasted_iota(jnp.int32, (cols, rows), 0)
        lane = lax.broadcasted_iota(jnp.int32, (cols, rows), 1)
        core_x = sub + x0
        edge_x = jnp.where(sub < 3, x0 - 3 + sub, x0 + cols - 3 + sub)
        edge_ok = sub < 6

        def bond_masks(xg, ok0, out_ref):
            own_x = ok0 & (xg >= 0) & (xg < x_total)
            total = jnp.zeros((cols, rows), jnp.float32)
            for i, (a, b, length, column) in enumerate(bonds):
                ok = own_x & (xg + a >= 0) & (xg + a < x_total) & (lane + b >= 0) & (lane + b < rows)
                m = jnp.where(ok, 1.0, 0.0)
                out_ref[i] = m
                total = total + m * length
            return total

        mass_c = bond_masks(core_x, sub >= 0, fmask_ref)
        mass_e = bond_masks(edge_x, edge_ok, hmask_ref)
        w_c = 1.0 / jnp.where(mass_c > 0, mass_c, 1.0)
        w_e = jnp.where(mass_e > 0, 1.0 / jnp.where(mass_e > 0, mass_e, 1.0), 0.0)
        wq_ref[0, 0:3, :] = w_e[0:3]
        wq_ref[0, 3:3 + cols, :] = w_c
        wq_ref[0, 3 + cols:6 + cols, :] = w_e[3:6]
        groups = {}
        for i, (a, b, length, column) in enumerate(bonds):
            groups.setdefault(a, []).append((i, b, length, column))
        for a, members in groups.items():
            w_slab = wq_ref[0, 3 + a:3 + a + cols, :]
            for i, b, length, column in members:
                wm_ref[i] = fmask_ref[i] * (w_c + shift_lanes(w_slab, b))

        @pl.when(t == 0)
        def _():
            ext[:, :, 0:cols, :] = jnp.zeros((3, plies, cols, rows), jnp.float32)

        @pl.when(t == nt - 1)
        def _():
            ext[:, :, 2 * cols:3 * cols, :] = jnp.zeros((3, plies, cols, rows), jnp.float32)

        @pl.when(q == 0)
        def _():
            ply_halo[0] = jnp.zeros((3, cols, rows), jnp.float32)

        @pl.when(q == nq - 1)
        def _():
            ply_halo[1] = jnp.zeros((3, cols, rows), jnp.float32)

        own.wait()

        def ply_body(p, carry):
            for d in range(2):
                pl.when(has[d] & (p + ahead < plies))(
                    lambda d=d: tile_copy(d, jnp.minimum(p + ahead, plies - 1)).start())
            pl.when(has[1])(tile_copy(0, p).wait_recv)
            pl.when(has[0])(tile_copy(1, p).wait_recv)
            gp = q * plies + p
            kind = angle_ref[p]
            low = lax.broadcasted_iota(jnp.int32, (cols, rows), 0) < 3

            def edge_rows(k, a):
                return jnp.where(low, ext[k, p, cols - 3 + a:2 * cols - 3 + a, :],
                                 ext[k, p, 2 * cols - 3 + a:3 * cols - 3 + a, :])

            uc = [ext[k, p, cols:2 * cols, :] for k in range(3)]
            ue = [edge_rows(k, 0) for k in range(3)]
            uc_y = {b: uc[1] - b for b in lanes}
            ue_y = {b: ue[1] - b for b in lanes}
            dil_c = jnp.zeros((cols, rows), jnp.float32)
            dil_e = jnp.zeros((cols, rows), jnp.float32)
            for a, members in groups.items():
                cs = [ext[k, p, cols + a:2 * cols + a, :] for k in range(3)]
                es = [edge_rows(k, a) for k in range(3)]
                uc_x = uc[0] - a
                ue_x = ue[0] - a
                for i, b, length, column in members:
                    sx = shift_lanes(cs[0], b) - uc_x
                    sy = shift_lanes(cs[1], b) - uc_y[b]
                    sz = shift_lanes(cs[2], b) - uc[2]
                    s2 = sx * sx + sy * sy + sz * sz
                    inv = lax.rsqrt(s2)
                    e = s2 * inv - length
                    m = fmask_ref[i]
                    dil_c = dil_c + e * m
                    sx_ref[i] = sx
                    sy_ref[i] = sy
                    sz_ref[i] = sz
                    pa_ref[i] = (inv * e) * wm_ref[i]
                    pb_ref[i] = inv * m
                    hx = shift_lanes(es[0], b) - ue_x
                    hy = shift_lanes(es[1], b) - ue_y[b]
                    hz = shift_lanes(es[2], b) - ue[2]
                    h2 = hx * hx + hy * hy + hz * hz
                    dil_e = dil_e + (h2 * lax.rsqrt(h2) - length) * hmask_ref[i]
            q_c = (3.0 * dil_c * w_c) * w_c
            q_e = (3.0 * dil_e * w_e) * w_e
            wq_ref[1, 0:3, :] = q_e[0:3]
            wq_ref[1, 3:3 + cols, :] = q_c
            wq_ref[1, 3 + cols:6 + cols, :] = q_e[3:6]

            fx = jnp.zeros((cols, rows), jnp.float32)
            fy = jnp.zeros((cols, rows), jnp.float32)
            fz = jnp.zeros((cols, rows), jnp.float32)
            for a, members in groups.items():
                q_slab = wq_ref[1, 3 + a:3 + a + cols, :]
                for i, b, length, column in members:
                    shear = table_ref[kind, column]
                    alpha = shear * (15.0 / length)
                    beta = 3.0 * bulk_modulus - 5.0 * shear
                    f = alpha * pa_ref[i] + beta * (pb_ref[i] * (q_c + shift_lanes(q_slab, b)))
                    fx = fx + f * sx_ref[i]
                    fy = fy + f * sy_ref[i]
                    fz = fz + f * sz_ref[i]
            above = jnp.where(gp < nsprings, spring_ref[jnp.minimum(gp, nsprings - 1)], 0.0)
            below = jnp.where(gp > 0, spring_ref[jnp.maximum(gp - 1, 0)], 0.0)
            hi_p = jnp.minimum(p + 1, plies - 1)
            lo_p = jnp.maximum(p - 1, 0)
            for k, fk in enumerate((fx, fy, fz)):
                hi = jnp.where(p == plies - 1, uc[k], ext[k, hi_p, cols:2 * cols, :])
                lo = jnp.where(p == 0, uc[k], ext[k, lo_p, cols:2 * cols, :])
                o_ref[k, p] = fk + (above * (hi - uc[k]) + below * (lo - uc[k]))
            return carry

        lax.fori_loop(0, plies, ply_body, 0)
        pl.when(has[3])(ply_copies[0].wait_recv)
        pl.when(has[2])(ply_copies[1].wait_recv)
        g0 = q * plies
        below = jnp.where(g0 > 0, spring_ref[jnp.maximum(g0 - 1, 0)], 0.0)
        gl = q * plies + plies - 1
        above = jnp.where(gl < nsprings, spring_ref[jnp.minimum(gl, nsprings - 1)], 0.0)
        for k in range(3):
            o_ref[k, 0] = o_ref[k, 0] + below * (ply_halo[0, k] - ext[k, 0, cols:2 * cols, :])
            o_ref[k, plies - 1] = o_ref[k, plies - 1] + above * (
                ply_halo[1, k] - ext[k, plies - 1, cols:2 * cols, :])
        for p in range(plies):
            for d in range(2):
                pl.when(has[d])(tile_copy(d, p).wait_send)
        for cond, cp in zip(has[2:], ply_copies):
            pl.when(cond)(cp.wait_send)

    return kernel


def local(displacement, angle_index, bond_table, interface_stiffness):
    comp_count, ply_count, col_count, row_count = displacement.shape
    x_total = col_count * lax.axis_size("tile")
    kernel = make_kernel(ply_count, col_count, row_count, x_total, interface_stiffness.shape[0])
    nbond = len(bond_list())
    smem = pl.BlockSpec(memory_space=pltpu.SMEM)
    return pl.pallas_call(
        kernel,
        in_specs=[smem, smem, smem, pl.BlockSpec(memory_space=pl.ANY)],
        out_specs=pl.BlockSpec(memory_space=pltpu.VMEM),
        out_shape=jax.ShapeDtypeStruct(displacement.shape, jnp.float32),
        scratch_shapes=[
            pltpu.VMEM((3, ply_count, 3 * col_count, row_count), jnp.float32),
            pltpu.VMEM((2, 3, col_count, row_count), jnp.float32),
            pltpu.VMEM((2, col_count + 6, row_count), jnp.float32),
            pltpu.VMEM((nbond, col_count, row_count), jnp.float32),
            pltpu.VMEM((nbond, col_count, row_count), jnp.float32),
            pltpu.VMEM((nbond, col_count, row_count), jnp.float32),
            pltpu.VMEM((nbond, col_count, row_count), jnp.float32),
            pltpu.VMEM((nbond, col_count, row_count), jnp.float32),
            pltpu.VMEM((nbond, col_count, row_count), jnp.float32),
            pltpu.VMEM((nbond, col_count, row_count), jnp.float32),
            pltpu.VMEM((nbond, col_count, row_count), jnp.float32),
            pltpu.SemaphoreType.DMA((5,)),
            pltpu.SemaphoreType.DMA((2, ply_count)),
            pltpu.SemaphoreType.DMA((2, ply_count)),
        ],
        compiler_params=pltpu.CompilerParams(collective_id=0, has_side_effects=True),
    )(angle_index, bond_table, interface_stiffness, displacement)


def solution(mesh):
    placed = (P(None, "ply", "tile", None), P("ply"), P(), P())
    return jax.shard_map(
        local, mesh=mesh, in_specs=placed, out_specs=P(None, "ply", "tile", None), check_vma=False
    )
```

```python
import math

import jax
import jax.numpy as jnp
from jax import lax
from jax.experimental import pallas as pl
from jax.experimental.pallas import tpu as pltpu
from jax.sharding import PartitionSpec as P

bulk_modulus = 40.0


def bond_list():
    halves = []
    for shift_x in range(-3, 4):
        for shift_y in range(-3, 4):
            radius = shift_x * shift_x + shift_y * shift_y
            if 0 < radius <= 9 and (shift_x > 0 or (shift_x == 0 and shift_y > 0)):
                halves.append((shift_x, shift_y))
    result = []
    for shift_x in range(-3, 4):
        for shift_y in range(-3, 4):
            radius = shift_x * shift_x + shift_y * shift_y
            if 0 < radius <= 9:
                if (shift_x, shift_y) in halves:
                    column = halves.index((shift_x, shift_y))
                else:
                    column = halves.index((-shift_x, -shift_y))
                result.append((shift_x, shift_y, math.sqrt(radius), column))
    return result


def halo(shard, axis, dim, width):
    peers, length = lax.axis_size(axis), shard.shape[dim]
    up = [(i, (i + 1) % peers) for i in range(peers)]
    down = [(j, i) for i, j in up]
    last = lax.slice_in_dim(shard, length - width, length, axis=dim)
    first = lax.slice_in_dim(shard, 0, width, axis=dim)
    before = lax.ppermute(last, axis, up)
    after = lax.ppermute(first, axis, down)
    return jnp.concatenate([before, shard, after], axis=dim)


def shift_lanes(x, b):
    if b == 0:
        return x
    return pltpu.roll(x, (-b) % x.shape[-1], 1)


MESH = pl.DeviceIdType.MESH


def make_kernel(plies, cols, rows, x_total, nsprings):
    bonds = bond_list()
    wide = cols + 6
    shifts = sorted({a for a, _, _, _ in bonds})
    lanes = sorted({b for _, b, _, _ in bonds})

    def kernel(angle_ref, table_ref, spring_ref, u_hbm, o_ref, ext, ply_halo, wq_ref, fmask_ref,
               hmask_ref, wm_ref, sx_ref, sy_ref, sz_ref, pa_ref, pb_ref, sems, send_t, recv_t):
        t = lax.axis_index("tile")
        nt = lax.axis_size("tile")
        q = lax.axis_index("ply")
        nq = lax.axis_size("ply")
        x0 = t * cols
        own = pltpu.make_async_copy(u_hbm, ext.at[:, :, cols:2 * cols, :], sems.at[0])
        own.start()
        has = ((t > 0), (t < nt - 1), (q > 0), (q < nq - 1))
        peers = ({"tile": t - 1}, {"tile": t + 1}, {"ply": q - 1}, {"ply": q + 1})
        barrier = pltpu.get_barrier_semaphore()
        for cond, dev in zip(has, peers):
            @pl.when(cond)
            def _():
                pl.semaphore_signal(barrier, inc=1, device_id=dev, device_id_type=MESH)
        count = sum(c.astype(jnp.int32) for c in has)
        pl.semaphore_wait(barrier, count)
        def tile_copy(d, p):
            if d == 0:
                src, dst = slice(0, 6), slice(2 * cols, 2 * cols + 6)
            else:
                src, dst = slice(cols - 6, cols), slice(cols - 6, cols)
            return pltpu.make_async_remote_copy(
                u_hbm.at[:, p, src, :], ext.at[:, p, dst, :], send_t.at[d, p], recv_t.at[d, p],
                device_id=peers[d], device_id_type=MESH)

        ply_copies = (
            pltpu.make_async_remote_copy(
                u_hbm.at[:, 0], ply_halo.at[1], sems.at[1], sems.at[3],
                device_id=peers[2], device_id_type=MESH),
            pltpu.make_async_remote_copy(
                u_hbm.at[:, plies - 1], ply_halo.at[0], sems.at[2], sems.at[4],
                device_id=peers[3], device_id_type=MESH),
        )
        ahead = min(2, plies)
        for p in range(ahead):
            for d in range(2):
                pl.when(has[d])(tile_copy(d, p).start)
        for cond, cp in zip(has[2:], ply_copies):
            pl.when(cond)(cp.start)

        sub = lax.broadcasted_iota(jnp.int32, (cols, rows), 0)
        lane = lax.broadcasted_iota(jnp.int32, (cols, rows), 1)
        core_x = sub + x0
        edge_x = jnp.where(sub < 3, x0 - 3 + sub, x0 + cols - 3 + sub)
        edge_ok = sub < 6

        def bond_masks(xg, ok0, out_ref):
            own_x = ok0 & (xg >= 0) & (xg < x_total)
            total = jnp.zeros((cols, rows), jnp.float32)
            for i, (a, b, length, column) in enumerate(bonds):
                ok = own_x & (xg + a >= 0) & (xg + a < x_total) & (lane + b >= 0) & (lane + b < rows)
                m = jnp.where(ok, 1.0, 0.0)
                out_ref[i] = m
                total = total + m * length
            return total

        mass_c = bond_masks(core_x, sub >= 0, fmask_ref)
        mass_e = bond_masks(edge_x, edge_ok, hmask_ref)
        w_c = 1.0 / jnp.where(mass_c > 0, mass_c, 1.0)
        w_e = jnp.where(mass_e > 0, 1.0 / jnp.where(mass_e > 0, mass_e, 1.0), 0.0)
        wq_ref[0, 0:3, :] = w_e[0:3]
        wq_ref[0, 3:3 + cols, :] = w_c
        wq_ref[0, 3 + cols:6 + cols, :] = w_e[3:6]
        groups = {}
        for i, (a, b, length, column) in enumerate(bonds):
            groups.setdefault(a, []).append((i, b, length, column))
        for a, members in groups.items():
            w_slab = wq_ref[0, 3 + a:3 + a + cols, :]
            for i, b, length, column in members:
                wm_ref[i] = fmask_ref[i] * (w_c + shift_lanes(w_slab, b))

        @pl.when(t == 0)
        def _():
            ext[:, :, 0:cols, :] = jnp.zeros((3, plies, cols, rows), jnp.float32)

        @pl.when(t == nt - 1)
        def _():
            ext[:, :, 2 * cols:3 * cols, :] = jnp.zeros((3, plies, cols, rows), jnp.float32)

        @pl.when(q == 0)
        def _():
            ply_halo[0] = jnp.zeros((3, cols, rows), jnp.float32)

        @pl.when(q == nq - 1)
        def _():
            ply_halo[1] = jnp.zeros((3, cols, rows), jnp.float32)

        own.wait()

        def ply_body(p, carry):
            for d in range(2):
                pl.when(has[d] & (p + ahead < plies))(
                    lambda d=d: tile_copy(d, jnp.minimum(p + ahead, plies - 1)).start())
            pl.when(has[1])(tile_copy(0, p).wait_recv)
            pl.when(has[0])(tile_copy(1, p).wait_recv)
            gp = q * plies + p
            kind = angle_ref[p]
            low = lax.broadcasted_iota(jnp.int32, (cols, rows), 0) < 3

            def edge_rows(k, a):
                return jnp.where(low, ext[k, p, cols - 3 + a:2 * cols - 3 + a, :],
                                 ext[k, p, 2 * cols - 3 + a:3 * cols - 3 + a, :])

            uc = [ext[k, p, cols:2 * cols, :] for k in range(3)]
            ue = [edge_rows(k, 0) for k in range(3)]
            uc_y = {b: uc[1] - b for b in lanes}
            ue_y = {b: ue[1] - b for b in lanes}
            dil_c = jnp.zeros((cols, rows), jnp.float32)
            dil_e = jnp.zeros((cols, rows), jnp.float32)
            for a, members in groups.items():
                cs = [ext[k, p, cols + a:2 * cols + a, :] for k in range(3)]
                es = [edge_rows(k, a) for k in range(3)]
                uc_x = uc[0] - a
                ue_x = ue[0] - a
                for i, b, length, column in members:
                    sx = shift_lanes(cs[0], b) - uc_x
                    sy = shift_lanes(cs[1], b) - uc_y[b]
                    sz = shift_lanes(cs[2], b) - uc[2]
                    s2 = sx * sx + sy * sy + sz * sz
                    inv = lax.rsqrt(s2)
                    e = s2 * inv - length
                    m = fmask_ref[i]
                    dil_c = dil_c + e * m
                    sx_ref[i] = sx
                    sy_ref[i] = sy
                    sz_ref[i] = sz
                    pa_ref[i] = e * wm_ref[i]
                    pb_ref[i] = inv * m
                    hx = shift_lanes(es[0], b) - ue_x
                    hy = shift_lanes(es[1], b) - ue_y[b]
                    hz = shift_lanes(es[2], b) - ue[2]
                    h2 = hx * hx + hy * hy + hz * hz
                    dil_e = dil_e + (h2 * lax.rsqrt(h2) - length) * hmask_ref[i]
            q_c = (3.0 * dil_c * w_c) * w_c
            q_e = (3.0 * dil_e * w_e) * w_e
            wq_ref[1, 0:3, :] = q_e[0:3]
            wq_ref[1, 3:3 + cols, :] = q_c
            wq_ref[1, 3 + cols:6 + cols, :] = q_e[3:6]

            fx = jnp.zeros((cols, rows), jnp.float32)
            fy = jnp.zeros((cols, rows), jnp.float32)
            fz = jnp.zeros((cols, rows), jnp.float32)
            for a, members in groups.items():
                q_slab = wq_ref[1, 3 + a:3 + a + cols, :]
                for i, b, length, column in members:
                    shear = table_ref[kind, column]
                    alpha = shear * (15.0 / length)
                    beta = 3.0 * bulk_modulus - 5.0 * shear
                    f = pb_ref[i] * (alpha * pa_ref[i] + beta * (q_c + shift_lanes(q_slab, b)))
                    fx = fx + f * sx_ref[i]
                    fy = fy + f * sy_ref[i]
                    fz = fz + f * sz_ref[i]
            above = jnp.where(gp < nsprings, spring_ref[jnp.minimum(gp, nsprings - 1)], 0.0)
            below = jnp.where(gp > 0, spring_ref[jnp.maximum(gp - 1, 0)], 0.0)
            hi_p = jnp.minimum(p + 1, plies - 1)
            lo_p = jnp.maximum(p - 1, 0)
            for k, fk in enumerate((fx, fy, fz)):
                hi = jnp.where(p == plies - 1, uc[k], ext[k, hi_p, cols:2 * cols, :])
                lo = jnp.where(p == 0, uc[k], ext[k, lo_p, cols:2 * cols, :])
                o_ref[k, p] = fk + (above * (hi - uc[k]) + below * (lo - uc[k]))
            return carry

        lax.fori_loop(0, plies, ply_body, 0)
        pl.when(has[3])(ply_copies[0].wait_recv)
        pl.when(has[2])(ply_copies[1].wait_recv)
        g0 = q * plies
        below = jnp.where(g0 > 0, spring_ref[jnp.maximum(g0 - 1, 0)], 0.0)
        gl = q * plies + plies - 1
        above = jnp.where(gl < nsprings, spring_ref[jnp.minimum(gl, nsprings - 1)], 0.0)
        for k in range(3):
            o_ref[k, 0] = o_ref[k, 0] + below * (ply_halo[0, k] - ext[k, 0, cols:2 * cols, :])
            o_ref[k, plies - 1] = o_ref[k, plies - 1] + above * (
                ply_halo[1, k] - ext[k, plies - 1, cols:2 * cols, :])
        for p in range(plies):
            for d in range(2):
                pl.when(has[d])(tile_copy(d, p).wait_send)
        for cond, cp in zip(has[2:], ply_copies):
            pl.when(cond)(cp.wait_send)

    return kernel


def local(displacement, angle_index, bond_table, interface_stiffness):
    comp_count, ply_count, col_count, row_count = displacement.shape
    x_total = col_count * lax.axis_size("tile")
    kernel = make_kernel(ply_count, col_count, row_count, x_total, interface_stiffness.shape[0])
    nbond = len(bond_list())
    smem = pl.BlockSpec(memory_space=pltpu.SMEM)
    return pl.pallas_call(
        kernel,
        in_specs=[smem, smem, smem, pl.BlockSpec(memory_space=pl.ANY)],
        out_specs=pl.BlockSpec(memory_space=pltpu.VMEM),
        out_shape=jax.ShapeDtypeStruct(displacement.shape, jnp.float32),
        scratch_shapes=[
            pltpu.VMEM((3, ply_count, 3 * col_count, row_count), jnp.float32),
            pltpu.VMEM((2, 3, col_count, row_count), jnp.float32),
            pltpu.VMEM((2, col_count + 6, row_count), jnp.float32),
            pltpu.VMEM((nbond, col_count, row_count), jnp.float32),
            pltpu.VMEM((nbond, col_count, row_count), jnp.float32),
            pltpu.VMEM((nbond, col_count, row_count), jnp.float32),
            pltpu.VMEM((nbond, col_count, row_count), jnp.float32),
            pltpu.VMEM((nbond, col_count, row_count), jnp.float32),
            pltpu.VMEM((nbond, col_count, row_count), jnp.float32),
            pltpu.VMEM((nbond, col_count, row_count), jnp.float32),
            pltpu.VMEM((nbond, col_count, row_count), jnp.float32),
            pltpu.SemaphoreType.DMA((5,)),
            pltpu.SemaphoreType.DMA((2, ply_count)),
            pltpu.SemaphoreType.DMA((2, ply_count)),
        ],
        compiler_params=pltpu.CompilerParams(collective_id=0, has_side_effects=True),
    )(angle_index, bond_table, interface_stiffness, displacement)


def solution(mesh):
    placed = (P(None, "ply", "tile", None), P("ply"), P(), P())
    return jax.shard_map(
        local, mesh=mesh, in_specs=placed, out_specs=P(None, "ply", "tile", None), check_vma=False
    )
```

```python
import math

import jax
import jax.numpy as jnp
from jax import lax
from jax.experimental import pallas as pl
from jax.experimental.pallas import tpu as pltpu
from jax.sharding import PartitionSpec as P

bulk_modulus = 40.0


def bond_list():
    halves = []
    for shift_x in range(-3, 4):
        for shift_y in range(-3, 4):
            radius = shift_x * shift_x + shift_y * shift_y
            if 0 < radius <= 9 and (shift_x > 0 or (shift_x == 0 and shift_y > 0)):
                halves.append((shift_x, shift_y))
    result = []
    for shift_x in range(-3, 4):
        for shift_y in range(-3, 4):
            radius = shift_x * shift_x + shift_y * shift_y
            if 0 < radius <= 9:
                if (shift_x, shift_y) in halves:
                    column = halves.index((shift_x, shift_y))
                else:
                    column = halves.index((-shift_x, -shift_y))
                result.append((shift_x, shift_y, math.sqrt(radius), column))
    return result


def halo(shard, axis, dim, width):
    peers, length = lax.axis_size(axis), shard.shape[dim]
    up = [(i, (i + 1) % peers) for i in range(peers)]
    down = [(j, i) for i, j in up]
    last = lax.slice_in_dim(shard, length - width, length, axis=dim)
    first = lax.slice_in_dim(shard, 0, width, axis=dim)
    before = lax.ppermute(last, axis, up)
    after = lax.ppermute(first, axis, down)
    return jnp.concatenate([before, shard, after], axis=dim)


def shift_lanes(x, b):
    if b == 0:
        return x
    return pltpu.roll(x, (-b) % x.shape[-1], 1)


MESH = pl.DeviceIdType.MESH


def make_kernel(plies, cols, rows, x_total, nsprings):
    bonds = bond_list()
    wide = cols + 6
    shifts = sorted({a for a, _, _, _ in bonds})
    lanes = sorted({b for _, b, _, _ in bonds})

    def kernel(angle_ref, table_ref, spring_ref, u_hbm, o_ref, ext, ply_halo, wq_ref, fmask_ref,
               hmask_ref, wm_ref, sx_ref, sy_ref, sz_ref, pa_ref, pb_ref, sems, send_t, recv_t):
        t = lax.axis_index("tile")
        nt = lax.axis_size("tile")
        q = lax.axis_index("ply")
        nq = lax.axis_size("ply")
        x0 = t * cols
        own = pltpu.make_async_copy(u_hbm, ext.at[:, :, cols:2 * cols, :], sems.at[0])
        own.start()
        has = ((t > 0), (t < nt - 1), (q > 0), (q < nq - 1))
        peers = ({"tile": t - 1}, {"tile": t + 1}, {"ply": q - 1}, {"ply": q + 1})
        barrier = pltpu.get_barrier_semaphore()
        for cond, dev in zip(has, peers):
            @pl.when(cond)
            def _():
                pl.semaphore_signal(barrier, inc=1, device_id=dev, device_id_type=MESH)
        count = sum(c.astype(jnp.int32) for c in has)
        pl.semaphore_wait(barrier, count)
        def tile_copy(d, p):
            if d == 0:
                src, dst = slice(0, 6), slice(2 * cols, 2 * cols + 6)
            else:
                src, dst = slice(cols - 6, cols), slice(cols - 6, cols)
            return pltpu.make_async_remote_copy(
                u_hbm.at[:, p, src, :], ext.at[:, p, dst, :], send_t.at[d, p], recv_t.at[d, p],
                device_id=peers[d], device_id_type=MESH)

        ply_copies = (
            pltpu.make_async_remote_copy(
                u_hbm.at[:, 0], ply_halo.at[1], sems.at[1], sems.at[3],
                device_id=peers[2], device_id_type=MESH),
            pltpu.make_async_remote_copy(
                u_hbm.at[:, plies - 1], ply_halo.at[0], sems.at[2], sems.at[4],
                device_id=peers[3], device_id_type=MESH),
        )
        ahead = min(3, plies)
        for p in range(ahead):
            for d in range(2):
                pl.when(has[d])(tile_copy(d, p).start)
        for cond, cp in zip(has[2:], ply_copies):
            pl.when(cond)(cp.start)

        sub = lax.broadcasted_iota(jnp.int32, (cols, rows), 0)
        lane = lax.broadcasted_iota(jnp.int32, (cols, rows), 1)
        core_x = sub + x0
        edge_x = jnp.where(sub < 3, x0 - 3 + sub, x0 + cols - 3 + sub)
        edge_ok = sub < 6

        def bond_masks(xg, ok0, out_ref):
            own_x = ok0 & (xg >= 0) & (xg < x_total)
            total = jnp.zeros((cols, rows), jnp.float32)
            for i, (a, b, length, column) in enumerate(bonds):
                ok = own_x & (xg + a >= 0) & (xg + a < x_total) & (lane + b >= 0) & (lane + b < rows)
                m = jnp.where(ok, 1.0, 0.0)
                out_ref[i] = m
                total = total + m * length
            return total

        mass_c = bond_masks(core_x, sub >= 0, fmask_ref)
        mass_e = bond_masks(edge_x, edge_ok, hmask_ref)
        w_c = 1.0 / jnp.where(mass_c > 0, mass_c, 1.0)
        w_e = jnp.where(mass_e > 0, 1.0 / jnp.where(mass_e > 0, mass_e, 1.0), 0.0)
        wq_ref[0, 0:3, :] = w_e[0:3]
        wq_ref[0, 3:3 + cols, :] = w_c
        wq_ref[0, 3 + cols:6 + cols, :] = w_e[3:6]
        groups = {}
        for i, (a, b, length, column) in enumerate(bonds):
            groups.setdefault(a, []).append((i, b, length, column))
        for a, members in groups.items():
            w_slab = wq_ref[0, 3 + a:3 + a + cols, :]
            for i, b, length, column in members:
                wm_ref[i] = fmask_ref[i] * (w_c + shift_lanes(w_slab, b))

        @pl.when(t == 0)
        def _():
            ext[:, :, 0:cols, :] = jnp.zeros((3, plies, cols, rows), jnp.float32)

        @pl.when(t == nt - 1)
        def _():
            ext[:, :, 2 * cols:3 * cols, :] = jnp.zeros((3, plies, cols, rows), jnp.float32)

        @pl.when(q == 0)
        def _():
            ply_halo[0] = jnp.zeros((3, cols, rows), jnp.float32)

        @pl.when(q == nq - 1)
        def _():
            ply_halo[1] = jnp.zeros((3, cols, rows), jnp.float32)

        own.wait()

        def ply_body(p, carry):
            for d in range(2):
                pl.when(has[d] & (p + ahead < plies))(
                    lambda d=d: tile_copy(d, jnp.minimum(p + ahead, plies - 1)).start())
            pl.when(has[1])(tile_copy(0, p).wait_recv)
            pl.when(has[0])(tile_copy(1, p).wait_recv)
            gp = q * plies + p
            kind = angle_ref[p]
            low = lax.broadcasted_iota(jnp.int32, (cols, rows), 0) < 3

            def edge_rows(k, a):
                return jnp.where(low, ext[k, p, cols - 3 + a:2 * cols - 3 + a, :],
                                 ext[k, p, 2 * cols - 3 + a:3 * cols - 3 + a, :])

            uc = [ext[k, p, cols:2 * cols, :] for k in range(3)]
            ue = [edge_rows(k, 0) for k in range(3)]
            uc_y = {b: uc[1] - b for b in lanes}
            ue_y = {b: ue[1] - b for b in lanes}
            dil_c = jnp.zeros((cols, rows), jnp.float32)
            dil_e = jnp.zeros((cols, rows), jnp.float32)
            for a, members in groups.items():
                cs = [ext[k, p, cols + a:2 * cols + a, :] for k in range(3)]
                es = [edge_rows(k, a) for k in range(3)]
                uc_x = uc[0] - a
                ue_x = ue[0] - a
                for i, b, length, column in members:
                    sx = shift_lanes(cs[0], b) - uc_x
                    sy = shift_lanes(cs[1], b) - uc_y[b]
                    sz = shift_lanes(cs[2], b) - uc[2]
                    s2 = sx * sx + sy * sy + sz * sz
                    inv = lax.rsqrt(s2)
                    e = s2 * inv - length
                    m = fmask_ref[i]
                    dil_c = dil_c + e * m
                    sx_ref[i] = sx
                    sy_ref[i] = sy
                    sz_ref[i] = sz
                    pa_ref[i] = e * wm_ref[i]
                    pb_ref[i] = inv * m
                    hx = shift_lanes(es[0], b) - ue_x
                    hy = shift_lanes(es[1], b) - ue_y[b]
                    hz = shift_lanes(es[2], b) - ue[2]
                    h2 = hx * hx + hy * hy + hz * hz
                    dil_e = dil_e + (h2 * lax.rsqrt(h2) - length) * hmask_ref[i]
            q_c = (3.0 * dil_c * w_c) * w_c
            q_e = (3.0 * dil_e * w_e) * w_e
            wq_ref[1, 0:3, :] = q_e[0:3]
            wq_ref[1, 3:3 + cols, :] = q_c
            wq_ref[1, 3 + cols:6 + cols, :] = q_e[3:6]

            fx = jnp.zeros((cols, rows), jnp.float32)
            fy = jnp.zeros((cols, rows), jnp.float32)
            fz = jnp.zeros((cols, rows), jnp.float32)
            for a, members in groups.items():
                q_slab = wq_ref[1, 3 + a:3 + a + cols, :]
                for i, b, length, column in members:
                    shear = table_ref[kind, column]
                    alpha = shear * (15.0 / length)
                    beta = 3.0 * bulk_modulus - 5.0 * shear
                    f = pb_ref[i] * (alpha * pa_ref[i] + beta * (q_c + shift_lanes(q_slab, b)))
                    fx = fx + f * sx_ref[i]
                    fy = fy + f * sy_ref[i]
                    fz = fz + f * sz_ref[i]
            above = jnp.where(gp < nsprings, spring_ref[jnp.minimum(gp, nsprings - 1)], 0.0)
            below = jnp.where(gp > 0, spring_ref[jnp.maximum(gp - 1, 0)], 0.0)
            hi_p = jnp.minimum(p + 1, plies - 1)
            lo_p = jnp.maximum(p - 1, 0)
            for k, fk in enumerate((fx, fy, fz)):
                hi = jnp.where(p == plies - 1, uc[k], ext[k, hi_p, cols:2 * cols, :])
                lo = jnp.where(p == 0, uc[k], ext[k, lo_p, cols:2 * cols, :])
                o_ref[k, p] = fk + (above * (hi - uc[k]) + below * (lo - uc[k]))
            return carry

        lax.fori_loop(0, plies, ply_body, 0)
        pl.when(has[3])(ply_copies[0].wait_recv)
        pl.when(has[2])(ply_copies[1].wait_recv)
        g0 = q * plies
        below = jnp.where(g0 > 0, spring_ref[jnp.maximum(g0 - 1, 0)], 0.0)
        gl = q * plies + plies - 1
        above = jnp.where(gl < nsprings, spring_ref[jnp.minimum(gl, nsprings - 1)], 0.0)
        for k in range(3):
            o_ref[k, 0] = o_ref[k, 0] + below * (ply_halo[0, k] - ext[k, 0, cols:2 * cols, :])
            o_ref[k, plies - 1] = o_ref[k, plies - 1] + above * (
                ply_halo[1, k] - ext[k, plies - 1, cols:2 * cols, :])
        for p in range(plies):
            for d in range(2):
                pl.when(has[d])(tile_copy(d, p).wait_send)
        for cond, cp in zip(has[2:], ply_copies):
            pl.when(cond)(cp.wait_send)

    return kernel


def local(displacement, angle_index, bond_table, interface_stiffness):
    comp_count, ply_count, col_count, row_count = displacement.shape
    x_total = col_count * lax.axis_size("tile")
    kernel = make_kernel(ply_count, col_count, row_count, x_total, interface_stiffness.shape[0])
    nbond = len(bond_list())
    smem = pl.BlockSpec(memory_space=pltpu.SMEM)
    return pl.pallas_call(
        kernel,
        in_specs=[smem, smem, smem, pl.BlockSpec(memory_space=pl.ANY)],
        out_specs=pl.BlockSpec(memory_space=pltpu.VMEM),
        out_shape=jax.ShapeDtypeStruct(displacement.shape, jnp.float32),
        scratch_shapes=[
            pltpu.VMEM((3, ply_count, 3 * col_count, row_count), jnp.float32),
            pltpu.VMEM((2, 3, col_count, row_count), jnp.float32),
            pltpu.VMEM((2, col_count + 6, row_count), jnp.float32),
            pltpu.VMEM((nbond, col_count, row_count), jnp.float32),
            pltpu.VMEM((nbond, col_count, row_count), jnp.float32),
            pltpu.VMEM((nbond, col_count, row_count), jnp.float32),
            pltpu.VMEM((nbond, col_count, row_count), jnp.float32),
            pltpu.VMEM((nbond, col_count, row_count), jnp.float32),
            pltpu.VMEM((nbond, col_count, row_count), jnp.float32),
            pltpu.VMEM((nbond, col_count, row_count), jnp.float32),
            pltpu.VMEM((nbond, col_count, row_count), jnp.float32),
            pltpu.SemaphoreType.DMA((5,)),
            pltpu.SemaphoreType.DMA((2, ply_count)),
            pltpu.SemaphoreType.DMA((2, ply_count)),
        ],
        compiler_params=pltpu.CompilerParams(collective_id=0, has_side_effects=True),
    )(angle_index, bond_table, interface_stiffness, displacement)


def solution(mesh):
    placed = (P(None, "ply", "tile", None), P("ply"), P(), P())
    return jax.shard_map(
        local, mesh=mesh, in_specs=placed, out_specs=P(None, "ply", "tile", None), check_vma=False
    )
```

```python
import math

import jax
import jax.numpy as jnp
from jax import lax
from jax.experimental import pallas as pl
from jax.experimental.pallas import tpu as pltpu
from jax.sharding import PartitionSpec as P

bulk_modulus = 40.0


def bond_list():
    halves = []
    for shift_x in range(-3, 4):
        for shift_y in range(-3, 4):
            radius = shift_x * shift_x + shift_y * shift_y
            if 0 < radius <= 9 and (shift_x > 0 or (shift_x == 0 and shift_y > 0)):
                halves.append((shift_x, shift_y))
    result = []
    for shift_x in range(-3, 4):
        for shift_y in range(-3, 4):
            radius = shift_x * shift_x + shift_y * shift_y
            if 0 < radius <= 9:
                if (shift_x, shift_y) in halves:
                    column = halves.index((shift_x, shift_y))
                else:
                    column = halves.index((-shift_x, -shift_y))
                result.append((shift_x, shift_y, math.sqrt(radius), column))
    return result


def halo(shard, axis, dim, width):
    peers, length = lax.axis_size(axis), shard.shape[dim]
    up = [(i, (i + 1) % peers) for i in range(peers)]
    down = [(j, i) for i, j in up]
    last = lax.slice_in_dim(shard, length - width, length, axis=dim)
    first = lax.slice_in_dim(shard, 0, width, axis=dim)
    before = lax.ppermute(last, axis, up)
    after = lax.ppermute(first, axis, down)
    return jnp.concatenate([before, shard, after], axis=dim)


def shift_lanes(x, b):
    if b == 0:
        return x
    return pltpu.roll(x, (-b) % x.shape[-1], 1)


MESH = pl.DeviceIdType.MESH


def make_kernel(plies, cols, rows, x_total, nsprings):
    bonds = bond_list()
    wide = cols + 6
    shifts = sorted({a for a, _, _, _ in bonds})
    lanes = sorted({b for _, b, _, _ in bonds})

    def kernel(angle_ref, table_ref, spring_ref, u_hbm, o_ref, ext, ply_halo, wq_ref, fmask_ref,
               hmask_ref, wm_ref, sx_ref, sy_ref, sz_ref, pa_ref, pb_ref, sems, send_t, recv_t):
        t = lax.axis_index("tile")
        nt = lax.axis_size("tile")
        q = lax.axis_index("ply")
        nq = lax.axis_size("ply")
        x0 = t * cols
        own = pltpu.make_async_copy(u_hbm, ext.at[:, :, cols:2 * cols, :], sems.at[0])
        own.start()
        has = ((t > 0), (t < nt - 1), (q > 0), (q < nq - 1))
        peers = ({"tile": t - 1}, {"tile": t + 1}, {"ply": q - 1}, {"ply": q + 1})
        barrier = pltpu.get_barrier_semaphore()
        for cond, dev in zip(has, peers):
            @pl.when(cond)
            def _():
                pl.semaphore_signal(barrier, inc=1, device_id=dev, device_id_type=MESH)
        count = sum(c.astype(jnp.int32) for c in has)
        pl.semaphore_wait(barrier, count)
        def tile_copy(d, p):
            if d == 0:
                src, dst = slice(0, 6), slice(2 * cols, 2 * cols + 6)
            else:
                src, dst = slice(cols - 6, cols), slice(cols - 6, cols)
            return pltpu.make_async_remote_copy(
                u_hbm.at[:, p, src, :], ext.at[:, p, dst, :], send_t.at[d, p], recv_t.at[d, p],
                device_id=peers[d], device_id_type=MESH)

        ply_copies = (
            pltpu.make_async_remote_copy(
                u_hbm.at[:, 0], ply_halo.at[1], sems.at[1], sems.at[3],
                device_id=peers[2], device_id_type=MESH),
            pltpu.make_async_remote_copy(
                u_hbm.at[:, plies - 1], ply_halo.at[0], sems.at[2], sems.at[4],
                device_id=peers[3], device_id_type=MESH),
        )
        ahead = min(2, plies)
        for p in range(ahead):
            for d in range(2):
                pl.when(has[d])(tile_copy(d, p).start)
        for cond, cp in zip(has[2:], ply_copies):
            pl.when(cond)(cp.start)

        sub = lax.broadcasted_iota(jnp.int32, (cols, rows), 0)
        lane = lax.broadcasted_iota(jnp.int32, (cols, rows), 1)
        core_x = sub + x0
        edge_x = jnp.where(sub < 3, x0 - 3 + sub, x0 + cols - 3 + sub)
        edge_ok = sub < 6

        def bond_masks(xg, ok0, out_ref):
            own_x = ok0 & (xg >= 0) & (xg < x_total)
            total = jnp.zeros((cols, rows), jnp.float32)
            for i, (a, b, length, column) in enumerate(bonds):
                ok = own_x & (xg + a >= 0) & (xg + a < x_total) & (lane + b >= 0) & (lane + b < rows)
                m = jnp.where(ok, 1.0, 0.0)
                out_ref[i] = m
                total = total + m * length
            return total

        mass_c = bond_masks(core_x, sub >= 0, fmask_ref)
        mass_e = bond_masks(edge_x, edge_ok, hmask_ref)
        w_c = 1.0 / jnp.where(mass_c > 0, mass_c, 1.0)
        w_e = jnp.where(mass_e > 0, 1.0 / jnp.where(mass_e > 0, mass_e, 1.0), 0.0)
        wq_ref[0, 0:3, :] = w_e[0:3]
        wq_ref[0, 3:3 + cols, :] = w_c
        wq_ref[0, 3 + cols:6 + cols, :] = w_e[3:6]
        groups = {}
        for i, (a, b, length, column) in enumerate(bonds):
            groups.setdefault(a, []).append((i, b, length, column))
        for a, members in groups.items():
            w_slab = wq_ref[0, 3 + a:3 + a + cols, :]
            for i, b, length, column in members:
                wm_ref[i] = fmask_ref[i] * (w_c + shift_lanes(w_slab, b))

        @pl.when(t == 0)
        def _():
            ext[:, :, 0:cols, :] = jnp.zeros((3, plies, cols, rows), jnp.float32)

        @pl.when(t == nt - 1)
        def _():
            ext[:, :, 2 * cols:3 * cols, :] = jnp.zeros((3, plies, cols, rows), jnp.float32)

        @pl.when(q == 0)
        def _():
            ply_halo[0] = jnp.zeros((3, cols, rows), jnp.float32)

        @pl.when(q == nq - 1)
        def _():
            ply_halo[1] = jnp.zeros((3, cols, rows), jnp.float32)

        own.wait()
        for p in range(plies):
            gp = q * plies + p
            above = jnp.where(gp < nsprings, spring_ref[jnp.minimum(gp, nsprings - 1)], 0.0)
            below = jnp.where(gp > 0, spring_ref[jnp.maximum(gp - 1, 0)], 0.0)
            for k in range(3):
                u_p = ext[k, p, cols:2 * cols, :]
                hi = ext[k, p + 1, cols:2 * cols, :] if p + 1 < plies else u_p
                lo = ext[k, p - 1, cols:2 * cols, :] if p > 0 else u_p
                o_ref[k, p] = above * (hi - u_p) + below * (lo - u_p)

        def ply_body(p, carry):
            for d in range(2):
                pl.when(has[d] & (p + ahead < plies))(
                    lambda d=d: tile_copy(d, jnp.minimum(p + ahead, plies - 1)).start())
            pl.when(has[1])(tile_copy(0, p).wait_recv)
            pl.when(has[0])(tile_copy(1, p).wait_recv)
            gp = q * plies + p
            kind = angle_ref[p]
            low = lax.broadcasted_iota(jnp.int32, (cols, rows), 0) < 3

            def edge_rows(k, a):
                return jnp.where(low, ext[k, p, cols - 3 + a:2 * cols - 3 + a, :],
                                 ext[k, p, 2 * cols - 3 + a:3 * cols - 3 + a, :])

            uc = [ext[k, p, cols:2 * cols, :] for k in range(3)]
            ue = [edge_rows(k, 0) for k in range(3)]
            uc_y = {b: uc[1] - b for b in lanes}
            ue_y = {b: ue[1] - b for b in lanes}
            dil_c = jnp.zeros((cols, rows), jnp.float32)
            dil_e = jnp.zeros((cols, rows), jnp.float32)
            for a, members in groups.items():
                cs = [ext[k, p, cols + a:2 * cols + a, :] for k in range(3)]
                es = [edge_rows(k, a) for k in range(3)]
                uc_x = uc[0] - a
                ue_x = ue[0] - a
                for i, b, length, column in members:
                    sx = shift_lanes(cs[0], b) - uc_x
                    sy = shift_lanes(cs[1], b) - uc_y[b]
                    sz = shift_lanes(cs[2], b) - uc[2]
                    s2 = sx * sx + sy * sy + sz * sz
                    inv = lax.rsqrt(s2)
                    e = s2 * inv - length
                    m = fmask_ref[i]
                    dil_c = dil_c + e * m
                    sx_ref[i] = sx
                    sy_ref[i] = sy
                    sz_ref[i] = sz
                    pa_ref[i] = (inv * e) * wm_ref[i]
                    pb_ref[i] = inv * m
                    hx = shift_lanes(es[0], b) - ue_x
                    hy = shift_lanes(es[1], b) - ue_y[b]
                    hz = shift_lanes(es[2], b) - ue[2]
                    h2 = hx * hx + hy * hy + hz * hz
                    dil_e = dil_e + (h2 * lax.rsqrt(h2) - length) * hmask_ref[i]
            q_c = (3.0 * dil_c * w_c) * w_c
            q_e = (3.0 * dil_e * w_e) * w_e
            wq_ref[1, 0:3, :] = q_e[0:3]
            wq_ref[1, 3:3 + cols, :] = q_c
            wq_ref[1, 3 + cols:6 + cols, :] = q_e[3:6]

            fx = jnp.zeros((cols, rows), jnp.float32)
            fy = jnp.zeros((cols, rows), jnp.float32)
            fz = jnp.zeros((cols, rows), jnp.float32)
            for a, members in groups.items():
                q_slab = wq_ref[1, 3 + a:3 + a + cols, :]
                for i, b, length, column in members:
                    shear = table_ref[kind, column]
                    alpha = shear * (15.0 / length)
                    beta = 3.0 * bulk_modulus - 5.0 * shear
                    f = alpha * pa_ref[i] + beta * (pb_ref[i] * (q_c + shift_lanes(q_slab, b)))
                    fx = fx + f * sx_ref[i]
                    fy = fy + f * sy_ref[i]
                    fz = fz + f * sz_ref[i]
            for k, fk in enumerate((fx, fy, fz)):
                o_ref[k, p] = fk + o_ref[k, p]
            return carry

        lax.fori_loop(0, plies, ply_body, 0)
        pl.when(has[3])(ply_copies[0].wait_recv)
        pl.when(has[2])(ply_copies[1].wait_recv)
        g0 = q * plies
        below = jnp.where(g0 > 0, spring_ref[jnp.maximum(g0 - 1, 0)], 0.0)
        gl = q * plies + plies - 1
        above = jnp.where(gl < nsprings, spring_ref[jnp.minimum(gl, nsprings - 1)], 0.0)
        for k in range(3):
            o_ref[k, 0] = o_ref[k, 0] + below * (ply_halo[0, k] - ext[k, 0, cols:2 * cols, :])
            o_ref[k, plies - 1] = o_ref[k, plies - 1] + above * (
                ply_halo[1, k] - ext[k, plies - 1, cols:2 * cols, :])
        for p in range(plies):
            for d in range(2):
                pl.when(has[d])(tile_copy(d, p).wait_send)
        for cond, cp in zip(has[2:], ply_copies):
            pl.when(cond)(cp.wait_send)

    return kernel


def local(displacement, angle_index, bond_table, interface_stiffness):
    comp_count, ply_count, col_count, row_count = displacement.shape
    x_total = col_count * lax.axis_size("tile")
    kernel = make_kernel(ply_count, col_count, row_count, x_total, interface_stiffness.shape[0])
    nbond = len(bond_list())
    smem = pl.BlockSpec(memory_space=pltpu.SMEM)
    return pl.pallas_call(
        kernel,
        in_specs=[smem, smem, smem, pl.BlockSpec(memory_space=pl.ANY)],
        out_specs=pl.BlockSpec(memory_space=pltpu.VMEM),
        out_shape=jax.ShapeDtypeStruct(displacement.shape, jnp.float32),
        scratch_shapes=[
            pltpu.VMEM((3, ply_count, 3 * col_count, row_count), jnp.float32),
            pltpu.VMEM((2, 3, col_count, row_count), jnp.float32),
            pltpu.VMEM((2, col_count + 6, row_count), jnp.float32),
            pltpu.VMEM((nbond, col_count, row_count), jnp.float32),
            pltpu.VMEM((nbond, col_count, row_count), jnp.float32),
            pltpu.VMEM((nbond, col_count, row_count), jnp.float32),
            pltpu.VMEM((nbond, col_count, row_count), jnp.float32),
            pltpu.VMEM((nbond, col_count, row_count), jnp.float32),
            pltpu.VMEM((nbond, col_count, row_count), jnp.float32),
            pltpu.VMEM((nbond, col_count, row_count), jnp.float32),
            pltpu.VMEM((nbond, col_count, row_count), jnp.float32),
            pltpu.SemaphoreType.DMA((5,)),
            pltpu.SemaphoreType.DMA((2, ply_count)),
            pltpu.SemaphoreType.DMA((2, ply_count)),
        ],
        compiler_params=pltpu.CompilerParams(collective_id=0, has_side_effects=True),
    )(angle_index, bond_table, interface_stiffness, displacement)


def solution(mesh):
    placed = (P(None, "ply", "tile", None), P("ply"), P(), P())
    return jax.shard_map(
        local, mesh=mesh, in_specs=placed, out_specs=P(None, "ply", "tile", None), check_vma=False
    )
```

```python
import math

import jax
import jax.numpy as jnp
from jax import lax
from jax.experimental import pallas as pl
from jax.experimental.pallas import tpu as pltpu
from jax.sharding import PartitionSpec as P

bulk_modulus = 40.0


def bond_list():
    halves = []
    for shift_x in range(-3, 4):
        for shift_y in range(-3, 4):
            radius = shift_x * shift_x + shift_y * shift_y
            if 0 < radius <= 9 and (shift_x > 0 or (shift_x == 0 and shift_y > 0)):
                halves.append((shift_x, shift_y))
    result = []
    for shift_x in range(-3, 4):
        for shift_y in range(-3, 4):
            radius = shift_x * shift_x + shift_y * shift_y
            if 0 < radius <= 9:
                if (shift_x, shift_y) in halves:
                    column = halves.index((shift_x, shift_y))
                else:
                    column = halves.index((-shift_x, -shift_y))
                result.append((shift_x, shift_y, math.sqrt(radius), column))
    return result


def halo(shard, axis, dim, width):
    peers, length = lax.axis_size(axis), shard.shape[dim]
    up = [(i, (i + 1) % peers) for i in range(peers)]
    down = [(j, i) for i, j in up]
    last = lax.slice_in_dim(shard, length - width, length, axis=dim)
    first = lax.slice_in_dim(shard, 0, width, axis=dim)
    before = lax.ppermute(last, axis, up)
    after = lax.ppermute(first, axis, down)
    return jnp.concatenate([before, shard, after], axis=dim)


def shift_lanes(x, b):
    if b == 0:
        return x
    return pltpu.roll(x, (-b) % x.shape[-1], 1)


MESH = pl.DeviceIdType.MESH


def make_kernel(plies, cols, rows, x_total, nsprings):
    bonds = bond_list()
    wide = cols + 6
    shifts = sorted({a for a, _, _, _ in bonds})
    lanes = sorted({b for _, b, _, _ in bonds})

    def kernel(angle_ref, table_ref, spring_ref, u_hbm, o_ref, ext, ply_halo, wq_ref, fmask_ref,
               hmask_ref, wm_ref, sx_ref, sy_ref, sz_ref, pa_ref, pb_ref, sems, send_t, recv_t):
        t = lax.axis_index("tile")
        nt = lax.axis_size("tile")
        q = lax.axis_index("ply")
        nq = lax.axis_size("ply")
        x0 = t * cols
        own = pltpu.make_async_copy(u_hbm, ext.at[:, :, cols:2 * cols, :], sems.at[0])
        own.start()
        has = ((t > 0), (t < nt - 1), (q > 0), (q < nq - 1))
        peers = ({"tile": t - 1}, {"tile": t + 1}, {"ply": q - 1}, {"ply": q + 1})
        barrier = pltpu.get_barrier_semaphore()
        for cond, dev in zip(has, peers):
            @pl.when(cond)
            def _():
                pl.semaphore_signal(barrier, inc=1, device_id=dev, device_id_type=MESH)
        count = sum(c.astype(jnp.int32) for c in has)
        pl.semaphore_wait(barrier, count)
        def tile_copy(d, p):
            if d == 0:
                src, dst = slice(cols, cols + 6), slice(2 * cols, 2 * cols + 6)
            else:
                src, dst = slice(2 * cols - 6, 2 * cols), slice(cols - 6, cols)
            return pltpu.make_async_remote_copy(
                ext.at[:, p, src, :], ext.at[:, p, dst, :], send_t.at[d, p], recv_t.at[d, p],
                device_id=peers[d], device_id_type=MESH)

        ply_copies = (
            pltpu.make_async_remote_copy(
                u_hbm.at[:, 0], ply_halo.at[1], sems.at[1], sems.at[3],
                device_id=peers[2], device_id_type=MESH),
            pltpu.make_async_remote_copy(
                u_hbm.at[:, plies - 1], ply_halo.at[0], sems.at[2], sems.at[4],
                device_id=peers[3], device_id_type=MESH),
        )
        ahead = min(2, plies)
        own.wait()
        for p in range(ahead):
            for d in range(2):
                pl.when(has[d])(tile_copy(d, p).start)
        for cond, cp in zip(has[2:], ply_copies):
            pl.when(cond)(cp.start)

        sub = lax.broadcasted_iota(jnp.int32, (cols, rows), 0)
        lane = lax.broadcasted_iota(jnp.int32, (cols, rows), 1)
        core_x = sub + x0
        edge_x = jnp.where(sub < 3, x0 - 3 + sub, x0 + cols - 3 + sub)
        edge_ok = sub < 6

        def bond_masks(xg, ok0, out_ref):
            own_x = ok0 & (xg >= 0) & (xg < x_total)
            total = jnp.zeros((cols, rows), jnp.float32)
            for i, (a, b, length, column) in enumerate(bonds):
                ok = own_x & (xg + a >= 0) & (xg + a < x_total) & (lane + b >= 0) & (lane + b < rows)
                m = jnp.where(ok, 1.0, 0.0)
                out_ref[i] = m
                total = total + m * length
            return total

        mass_c = bond_masks(core_x, sub >= 0, fmask_ref)
        mass_e = bond_masks(edge_x, edge_ok, hmask_ref)
        w_c = 1.0 / jnp.where(mass_c > 0, mass_c, 1.0)
        w_e = jnp.where(mass_e > 0, 1.0 / jnp.where(mass_e > 0, mass_e, 1.0), 0.0)
        wq_ref[0, 0:3, :] = w_e[0:3]
        wq_ref[0, 3:3 + cols, :] = w_c
        wq_ref[0, 3 + cols:6 + cols, :] = w_e[3:6]
        groups = {}
        for i, (a, b, length, column) in enumerate(bonds):
            groups.setdefault(a, []).append((i, b, length, column))
        for a, members in groups.items():
            w_slab = wq_ref[0, 3 + a:3 + a + cols, :]
            for i, b, length, column in members:
                wm_ref[i] = fmask_ref[i] * (w_c + shift_lanes(w_slab, b))

        @pl.when(t == 0)
        def _():
            ext[:, :, 0:cols, :] = jnp.zeros((3, plies, cols, rows), jnp.float32)

        @pl.when(t == nt - 1)
        def _():
            ext[:, :, 2 * cols:3 * cols, :] = jnp.zeros((3, plies, cols, rows), jnp.float32)

        @pl.when(q == 0)
        def _():
            ply_halo[0] = jnp.zeros((3, cols, rows), jnp.float32)

        @pl.when(q == nq - 1)
        def _():
            ply_halo[1] = jnp.zeros((3, cols, rows), jnp.float32)


        def ply_body(p, carry):
            for d in range(2):
                pl.when(has[d] & (p + ahead < plies))(
                    lambda d=d: tile_copy(d, jnp.minimum(p + ahead, plies - 1)).start())
            pl.when(has[1])(tile_copy(0, p).wait_recv)
            pl.when(has[0])(tile_copy(1, p).wait_recv)
            gp = q * plies + p
            kind = angle_ref[p]
            low = lax.broadcasted_iota(jnp.int32, (cols, rows), 0) < 3

            def edge_rows(k, a):
                return jnp.where(low, ext[k, p, cols - 3 + a:2 * cols - 3 + a, :],
                                 ext[k, p, 2 * cols - 3 + a:3 * cols - 3 + a, :])

            uc = [ext[k, p, cols:2 * cols, :] for k in range(3)]
            ue = [edge_rows(k, 0) for k in range(3)]
            uc_y = {b: uc[1] - b for b in lanes}
            ue_y = {b: ue[1] - b for b in lanes}
            dil_c = jnp.zeros((cols, rows), jnp.float32)
            dil_e = jnp.zeros((cols, rows), jnp.float32)
            for a, members in groups.items():
                cs = [ext[k, p, cols + a:2 * cols + a, :] for k in range(3)]
                es = [edge_rows(k, a) for k in range(3)]
                uc_x = uc[0] - a
                ue_x = ue[0] - a
                for i, b, length, column in members:
                    sx = shift_lanes(cs[0], b) - uc_x
                    sy = shift_lanes(cs[1], b) - uc_y[b]
                    sz = shift_lanes(cs[2], b) - uc[2]
                    s2 = sx * sx + sy * sy + sz * sz
                    inv = lax.rsqrt(s2)
                    e = s2 * inv - length
                    m = fmask_ref[i]
                    dil_c = dil_c + e * m
                    sx_ref[i] = sx
                    sy_ref[i] = sy
                    sz_ref[i] = sz
                    pa_ref[i] = (inv * e) * wm_ref[i]
                    pb_ref[i] = inv * m
                    hx = shift_lanes(es[0], b) - ue_x
                    hy = shift_lanes(es[1], b) - ue_y[b]
                    hz = shift_lanes(es[2], b) - ue[2]
                    h2 = hx * hx + hy * hy + hz * hz
                    dil_e = dil_e + (h2 * lax.rsqrt(h2) - length) * hmask_ref[i]
            q_c = (3.0 * dil_c * w_c) * w_c
            q_e = (3.0 * dil_e * w_e) * w_e
            wq_ref[1, 0:3, :] = q_e[0:3]
            wq_ref[1, 3:3 + cols, :] = q_c
            wq_ref[1, 3 + cols:6 + cols, :] = q_e[3:6]

            fx = jnp.zeros((cols, rows), jnp.float32)
            fy = jnp.zeros((cols, rows), jnp.float32)
            fz = jnp.zeros((cols, rows), jnp.float32)
            for a, members in groups.items():
                q_slab = wq_ref[1, 3 + a:3 + a + cols, :]
                for i, b, length, column in members:
                    shear = table_ref[kind, column]
                    alpha = shear * (15.0 / length)
                    beta = 3.0 * bulk_modulus - 5.0 * shear
                    f = alpha * pa_ref[i] + beta * (pb_ref[i] * (q_c + shift_lanes(q_slab, b)))
                    fx = fx + f * sx_ref[i]
                    fy = fy + f * sy_ref[i]
                    fz = fz + f * sz_ref[i]
            above = jnp.where(gp < nsprings, spring_ref[jnp.minimum(gp, nsprings - 1)], 0.0)
            below = jnp.where(gp > 0, spring_ref[jnp.maximum(gp - 1, 0)], 0.0)
            hi_p = jnp.minimum(p + 1, plies - 1)
            lo_p = jnp.maximum(p - 1, 0)
            for k, fk in enumerate((fx, fy, fz)):
                hi = jnp.where(p == plies - 1, uc[k], ext[k, hi_p, cols:2 * cols, :])
                lo = jnp.where(p == 0, uc[k], ext[k, lo_p, cols:2 * cols, :])
                o_ref[k, p] = fk + (above * (hi - uc[k]) + below * (lo - uc[k]))
            return carry

        lax.fori_loop(0, plies, ply_body, 0)
        pl.when(has[3])(ply_copies[0].wait_recv)
        pl.when(has[2])(ply_copies[1].wait_recv)
        g0 = q * plies
        below = jnp.where(g0 > 0, spring_ref[jnp.maximum(g0 - 1, 0)], 0.0)
        gl = q * plies + plies - 1
        above = jnp.where(gl < nsprings, spring_ref[jnp.minimum(gl, nsprings - 1)], 0.0)
        for k in range(3):
            o_ref[k, 0] = o_ref[k, 0] + below * (ply_halo[0, k] - ext[k, 0, cols:2 * cols, :])
            o_ref[k, plies - 1] = o_ref[k, plies - 1] + above * (
                ply_halo[1, k] - ext[k, plies - 1, cols:2 * cols, :])
        for p in range(plies):
            for d in range(2):
                pl.when(has[d])(tile_copy(d, p).wait_send)
        for cond, cp in zip(has[2:], ply_copies):
            pl.when(cond)(cp.wait_send)

    return kernel


def local(displacement, angle_index, bond_table, interface_stiffness):
    comp_count, ply_count, col_count, row_count = displacement.shape
    x_total = col_count * lax.axis_size("tile")
    kernel = make_kernel(ply_count, col_count, row_count, x_total, interface_stiffness.shape[0])
    nbond = len(bond_list())
    smem = pl.BlockSpec(memory_space=pltpu.SMEM)
    return pl.pallas_call(
        kernel,
        in_specs=[smem, smem, smem, pl.BlockSpec(memory_space=pl.ANY)],
        out_specs=pl.BlockSpec(memory_space=pltpu.VMEM),
        out_shape=jax.ShapeDtypeStruct(displacement.shape, jnp.float32),
        scratch_shapes=[
            pltpu.VMEM((3, ply_count, 3 * col_count, row_count), jnp.float32),
            pltpu.VMEM((2, 3, col_count, row_count), jnp.float32),
            pltpu.VMEM((2, col_count + 6, row_count), jnp.float32),
            pltpu.VMEM((nbond, col_count, row_count), jnp.float32),
            pltpu.VMEM((nbond, col_count, row_count), jnp.float32),
            pltpu.VMEM((nbond, col_count, row_count), jnp.float32),
            pltpu.VMEM((nbond, col_count, row_count), jnp.float32),
            pltpu.VMEM((nbond, col_count, row_count), jnp.float32),
            pltpu.VMEM((nbond, col_count, row_count), jnp.float32),
            pltpu.VMEM((nbond, col_count, row_count), jnp.float32),
            pltpu.VMEM((nbond, col_count, row_count), jnp.float32),
            pltpu.SemaphoreType.DMA((5,)),
            pltpu.SemaphoreType.DMA((2, ply_count)),
            pltpu.SemaphoreType.DMA((2, ply_count)),
        ],
        compiler_params=pltpu.CompilerParams(collective_id=0, has_side_effects=True),
    )(angle_index, bond_table, interface_stiffness, displacement)


def solution(mesh):
    placed = (P(None, "ply", "tile", None), P("ply"), P(), P())
    return jax.shard_map(
        local, mesh=mesh, in_specs=placed, out_specs=P(None, "ply", "tile", None), check_vma=False
    )
```

```python
import math

import jax
import jax.numpy as jnp
from jax import lax
from jax.experimental import pallas as pl
from jax.experimental.pallas import tpu as pltpu
from jax.sharding import PartitionSpec as P

bulk_modulus = 40.0


def bond_list():
    halves = []
    for shift_x in range(-3, 4):
        for shift_y in range(-3, 4):
            radius = shift_x * shift_x + shift_y * shift_y
            if 0 < radius <= 9 and (shift_x > 0 or (shift_x == 0 and shift_y > 0)):
                halves.append((shift_x, shift_y))
    result = []
    for shift_x in range(-3, 4):
        for shift_y in range(-3, 4):
            radius = shift_x * shift_x + shift_y * shift_y
            if 0 < radius <= 9:
                if (shift_x, shift_y) in halves:
                    column = halves.index((shift_x, shift_y))
                else:
                    column = halves.index((-shift_x, -shift_y))
                result.append((shift_x, shift_y, math.sqrt(radius), column))
    return result


def halo(shard, axis, dim, width):
    peers, length = lax.axis_size(axis), shard.shape[dim]
    up = [(i, (i + 1) % peers) for i in range(peers)]
    down = [(j, i) for i, j in up]
    last = lax.slice_in_dim(shard, length - width, length, axis=dim)
    first = lax.slice_in_dim(shard, 0, width, axis=dim)
    before = lax.ppermute(last, axis, up)
    after = lax.ppermute(first, axis, down)
    return jnp.concatenate([before, shard, after], axis=dim)


def shift_lanes(x, b):
    if b == 0:
        return x
    return pltpu.roll(x, (-b) % x.shape[-1], 1)


MESH = pl.DeviceIdType.MESH


def make_kernel(plies, cols, rows, x_total, nsprings):
    bonds = bond_list()
    wide = cols + 6
    shifts = sorted({a for a, _, _, _ in bonds})
    lanes = sorted({b for _, b, _, _ in bonds})

    def kernel(angle_ref, table_ref, spring_ref, u_hbm, o_ref, ext, ply_halo, wq_ref, fmask_ref,
               hmask_ref, wm_ref, sx_ref, sy_ref, sz_ref, pa_ref, pb_ref, sems, send_t, recv_t):
        t = lax.axis_index("tile")
        nt = lax.axis_size("tile")
        q = lax.axis_index("ply")
        nq = lax.axis_size("ply")
        x0 = t * cols
        own = pltpu.make_async_copy(u_hbm, ext.at[:, :, cols:2 * cols, :], sems.at[0])
        own.start()
        has = ((t > 0), (t < nt - 1), (q > 0), (q < nq - 1))
        peers = ({"tile": t - 1}, {"tile": t + 1}, {"ply": q - 1}, {"ply": q + 1})
        barrier = pltpu.get_barrier_semaphore()
        for cond, dev in zip(has, peers):
            @pl.when(cond)
            def _():
                pl.semaphore_signal(barrier, inc=1, device_id=dev, device_id_type=MESH)
        count = sum(c.astype(jnp.int32) for c in has)
        pl.semaphore_wait(barrier, count)
        def tile_copy(d, p):
            if d == 0:
                src, dst = slice(cols, cols + 6), slice(2 * cols, 2 * cols + 6)
            else:
                src, dst = slice(2 * cols - 6, 2 * cols), slice(cols - 6, cols)
            return pltpu.make_async_remote_copy(
                ext.at[:, p, src, :], ext.at[:, p, dst, :], send_t.at[d, p], recv_t.at[d, p],
                device_id=peers[d], device_id_type=MESH)

        ply_copies = (
            pltpu.make_async_remote_copy(
                u_hbm.at[:, 0], ply_halo.at[1], sems.at[1], sems.at[3],
                device_id=peers[2], device_id_type=MESH),
            pltpu.make_async_remote_copy(
                u_hbm.at[:, plies - 1], ply_halo.at[0], sems.at[2], sems.at[4],
                device_id=peers[3], device_id_type=MESH),
        )
        ahead = min(2, plies)
        own.wait()
        for p in range(ahead):
            for d in range(2):
                pl.when(has[d])(tile_copy(d, p).start)
        for cond, cp in zip(has[2:], ply_copies):
            pl.when(cond)(cp.start)

        sub = lax.broadcasted_iota(jnp.int32, (cols, rows), 0)
        lane = lax.broadcasted_iota(jnp.int32, (cols, rows), 1)
        core_x = sub + x0
        edge_x = jnp.where(sub < 3, x0 - 3 + sub, x0 + cols - 3 + sub)
        edge_ok = sub < 6

        def bond_masks(xg, ok0, out_ref):
            own_x = ok0 & (xg >= 0) & (xg < x_total)
            total = jnp.zeros((cols, rows), jnp.float32)
            for i, (a, b, length, column) in enumerate(bonds):
                ok = own_x & (xg + a >= 0) & (xg + a < x_total) & (lane + b >= 0) & (lane + b < rows)
                m = jnp.where(ok, 1.0, 0.0)
                out_ref[i] = m
                total = total + m * length
            return total

        mass_c = bond_masks(core_x, sub >= 0, fmask_ref)
        mass_e = bond_masks(edge_x, edge_ok, hmask_ref)
        w_c = 1.0 / jnp.where(mass_c > 0, mass_c, 1.0)
        w_e = jnp.where(mass_e > 0, 1.0 / jnp.where(mass_e > 0, mass_e, 1.0), 0.0)
        wq_ref[0, 0:3, :] = w_e[0:3]
        wq_ref[0, 3:3 + cols, :] = w_c
        wq_ref[0, 3 + cols:6 + cols, :] = w_e[3:6]
        groups = {}
        for i, (a, b, length, column) in enumerate(bonds):
            groups.setdefault(a, []).append((i, b, length, column))
        for a, members in groups.items():
            w_slab = wq_ref[0, 3 + a:3 + a + cols, :]
            for i, b, length, column in members:
                wm_ref[i] = fmask_ref[i] * (w_c + shift_lanes(w_slab, b))

        @pl.when(t == 0)
        def _():
            ext[:, :, 0:cols, :] = jnp.zeros((3, plies, cols, rows), jnp.float32)

        @pl.when(t == nt - 1)
        def _():
            ext[:, :, 2 * cols:3 * cols, :] = jnp.zeros((3, plies, cols, rows), jnp.float32)

        @pl.when(q == 0)
        def _():
            ply_halo[0] = jnp.zeros((3, cols, rows), jnp.float32)

        @pl.when(q == nq - 1)
        def _():
            ply_halo[1] = jnp.zeros((3, cols, rows), jnp.float32)


        for p in range(plies):
            gp = q * plies + p
            above = jnp.where(gp < nsprings, spring_ref[jnp.minimum(gp, nsprings - 1)], 0.0)
            below = jnp.where(gp > 0, spring_ref[jnp.maximum(gp - 1, 0)], 0.0)
            for k in range(3):
                u_p = ext[k, p, cols:2 * cols, :]
                hi = ext[k, p + 1, cols:2 * cols, :] if p + 1 < plies else u_p
                lo = ext[k, p - 1, cols:2 * cols, :] if p > 0 else u_p
                o_ref[k, p] = above * (hi - u_p) + below * (lo - u_p)

        def ply_body(p, carry):
            for d in range(2):
                pl.when(has[d] & (p + ahead < plies))(
                    lambda d=d: tile_copy(d, jnp.minimum(p + ahead, plies - 1)).start())
            pl.when(has[1])(tile_copy(0, p).wait_recv)
            pl.when(has[0])(tile_copy(1, p).wait_recv)
            gp = q * plies + p
            kind = angle_ref[p]
            low = lax.broadcasted_iota(jnp.int32, (cols, rows), 0) < 3

            def edge_rows(k, a):
                return jnp.where(low, ext[k, p, cols - 3 + a:2 * cols - 3 + a, :],
                                 ext[k, p, 2 * cols - 3 + a:3 * cols - 3 + a, :])

            uc = [ext[k, p, cols:2 * cols, :] for k in range(3)]
            ue = [edge_rows(k, 0) for k in range(3)]
            uc_y = {b: uc[1] - b for b in lanes}
            ue_y = {b: ue[1] - b for b in lanes}
            dil_c = jnp.zeros((cols, rows), jnp.float32)
            dil_e = jnp.zeros((cols, rows), jnp.float32)
            for a, members in groups.items():
                cs = [ext[k, p, cols + a:2 * cols + a, :] for k in range(3)]
                es = [edge_rows(k, a) for k in range(3)]
                uc_x = uc[0] - a
                ue_x = ue[0] - a
                for i, b, length, column in members:
                    sx = shift_lanes(cs[0], b) - uc_x
                    sy = shift_lanes(cs[1], b) - uc_y[b]
                    sz = shift_lanes(cs[2], b) - uc[2]
                    s2 = sx * sx + sy * sy + sz * sz
                    inv = lax.rsqrt(s2)
                    e = s2 * inv - length
                    m = fmask_ref[i]
                    dil_c = dil_c + e * m
                    sx_ref[i] = sx
                    sy_ref[i] = sy
                    sz_ref[i] = sz
                    pa_ref[i] = e * wm_ref[i]
                    pb_ref[i] = inv * m
                    hx = shift_lanes(es[0], b) - ue_x
                    hy = shift_lanes(es[1], b) - ue_y[b]
                    hz = shift_lanes(es[2], b) - ue[2]
                    h2 = hx * hx + hy * hy + hz * hz
                    dil_e = dil_e + (h2 * lax.rsqrt(h2) - length) * hmask_ref[i]
            q_c = (3.0 * dil_c * w_c) * w_c
            q_e = (3.0 * dil_e * w_e) * w_e
            wq_ref[1, 0:3, :] = q_e[0:3]
            wq_ref[1, 3:3 + cols, :] = q_c
            wq_ref[1, 3 + cols:6 + cols, :] = q_e[3:6]

            fx = jnp.zeros((cols, rows), jnp.float32)
            fy = jnp.zeros((cols, rows), jnp.float32)
            fz = jnp.zeros((cols, rows), jnp.float32)
            for a, members in groups.items():
                q_slab = wq_ref[1, 3 + a:3 + a + cols, :]
                for i, b, length, column in members:
                    shear = table_ref[kind, column]
                    alpha = shear * (15.0 / length)
                    beta = 3.0 * bulk_modulus - 5.0 * shear
                    f = pb_ref[i] * (alpha * pa_ref[i] + beta * (q_c + shift_lanes(q_slab, b)))
                    fx = fx + f * sx_ref[i]
                    fy = fy + f * sy_ref[i]
                    fz = fz + f * sz_ref[i]
            for k, fk in enumerate((fx, fy, fz)):
                o_ref[k, p] = fk + o_ref[k, p]
            return carry

        lax.fori_loop(0, plies, ply_body, 0)
        pl.when(has[3])(ply_copies[0].wait_recv)
        pl.when(has[2])(ply_copies[1].wait_recv)
        g0 = q * plies
        below = jnp.where(g0 > 0, spring_ref[jnp.maximum(g0 - 1, 0)], 0.0)
        gl = q * plies + plies - 1
        above = jnp.where(gl < nsprings, spring_ref[jnp.minimum(gl, nsprings - 1)], 0.0)
        for k in range(3):
            o_ref[k, 0] = o_ref[k, 0] + below * (ply_halo[0, k] - ext[k, 0, cols:2 * cols, :])
            o_ref[k, plies - 1] = o_ref[k, plies - 1] + above * (
                ply_halo[1, k] - ext[k, plies - 1, cols:2 * cols, :])
        for p in range(plies):
            for d in range(2):
                pl.when(has[d])(tile_copy(d, p).wait_send)
        for cond, cp in zip(has[2:], ply_copies):
            pl.when(cond)(cp.wait_send)

    return kernel


def local(displacement, angle_index, bond_table, interface_stiffness):
    comp_count, ply_count, col_count, row_count = displacement.shape
    x_total = col_count * lax.axis_size("tile")
    kernel = make_kernel(ply_count, col_count, row_count, x_total, interface_stiffness.shape[0])
    nbond = len(bond_list())
    smem = pl.BlockSpec(memory_space=pltpu.SMEM)
    return pl.pallas_call(
        kernel,
        in_specs=[smem, smem, smem, pl.BlockSpec(memory_space=pl.ANY)],
        out_specs=pl.BlockSpec(memory_space=pltpu.VMEM),
        out_shape=jax.ShapeDtypeStruct(displacement.shape, jnp.float32),
        scratch_shapes=[
            pltpu.VMEM((3, ply_count, 3 * col_count, row_count), jnp.float32),
            pltpu.VMEM((2, 3, col_count, row_count), jnp.float32),
            pltpu.VMEM((2, col_count + 6, row_count), jnp.float32),
            pltpu.VMEM((nbond, col_count, row_count), jnp.float32),
            pltpu.VMEM((nbond, col_count, row_count), jnp.float32),
            pltpu.VMEM((nbond, col_count, row_count), jnp.float32),
            pltpu.VMEM((nbond, col_count, row_count), jnp.float32),
            pltpu.VMEM((nbond, col_count, row_count), jnp.float32),
            pltpu.VMEM((nbond, col_count, row_count), jnp.float32),
            pltpu.VMEM((nbond, col_count, row_count), jnp.float32),
            pltpu.VMEM((nbond, col_count, row_count), jnp.float32),
            pltpu.SemaphoreType.DMA((5,)),
            pltpu.SemaphoreType.DMA((2, ply_count)),
            pltpu.SemaphoreType.DMA((2, ply_count)),
        ],
        compiler_params=pltpu.CompilerParams(collective_id=0, has_side_effects=True),
    )(angle_index, bond_table, interface_stiffness, displacement)


def solution(mesh):
    placed = (P(None, "ply", "tile", None), P("ply"), P(), P())
    return jax.shard_map(
        local, mesh=mesh, in_specs=placed, out_specs=P(None, "ply", "tile", None), check_vma=False
    )
```

```python
import math

import jax
import jax.numpy as jnp
from jax import lax
from jax.experimental import pallas as pl
from jax.experimental.pallas import tpu as pltpu
from jax.sharding import PartitionSpec as P

bulk_modulus = 40.0


def bond_list():
    halves = []
    for shift_x in range(-3, 4):
        for shift_y in range(-3, 4):
            radius = shift_x * shift_x + shift_y * shift_y
            if 0 < radius <= 9 and (shift_x > 0 or (shift_x == 0 and shift_y > 0)):
                halves.append((shift_x, shift_y))
    result = []
    for shift_x in range(-3, 4):
        for shift_y in range(-3, 4):
            radius = shift_x * shift_x + shift_y * shift_y
            if 0 < radius <= 9:
                if (shift_x, shift_y) in halves:
                    column = halves.index((shift_x, shift_y))
                else:
                    column = halves.index((-shift_x, -shift_y))
                result.append((shift_x, shift_y, math.sqrt(radius), column))
    return result


def halo(shard, axis, dim, width):
    peers, length = lax.axis_size(axis), shard.shape[dim]
    up = [(i, (i + 1) % peers) for i in range(peers)]
    down = [(j, i) for i, j in up]
    last = lax.slice_in_dim(shard, length - width, length, axis=dim)
    first = lax.slice_in_dim(shard, 0, width, axis=dim)
    before = lax.ppermute(last, axis, up)
    after = lax.ppermute(first, axis, down)
    return jnp.concatenate([before, shard, after], axis=dim)


def shift_lanes(x, b):
    if b == 0:
        return x
    return pltpu.roll(x, (-b) % x.shape[-1], 1)


MESH = pl.DeviceIdType.MESH


def make_kernel(plies, cols, rows, x_total, nsprings):
    bonds = bond_list()
    wide = cols + 6
    shifts = sorted({a for a, _, _, _ in bonds})
    lanes = sorted({b for _, b, _, _ in bonds})

    def kernel(angle_ref, table_ref, spring_ref, u_hbm, o_ref, ext, ply_halo, wq_ref, fmask_ref,
               hmask_ref, wm_ref, sx_ref, sy_ref, sz_ref, pa_ref, pb_ref, sems, send_t, recv_t):
        t = lax.axis_index("tile")
        nt = lax.axis_size("tile")
        q = lax.axis_index("ply")
        nq = lax.axis_size("ply")
        x0 = t * cols
        own = pltpu.make_async_copy(u_hbm, ext.at[:, :, cols:2 * cols, :], sems.at[0])
        own.start()
        has = ((t > 0), (t < nt - 1), (q > 0), (q < nq - 1))
        peers = ({"tile": t - 1}, {"tile": t + 1}, {"ply": q - 1}, {"ply": q + 1})
        barrier = pltpu.get_barrier_semaphore()
        for cond, dev in zip(has, peers):
            @pl.when(cond)
            def _():
                pl.semaphore_signal(barrier, inc=1, device_id=dev, device_id_type=MESH)
        count = sum(c.astype(jnp.int32) for c in has)
        pl.semaphore_wait(barrier, count)
        def tile_copy(d, p):
            if d == 0:
                src, dst = slice(cols, cols + 6), slice(2 * cols, 2 * cols + 6)
            else:
                src, dst = slice(2 * cols - 6, 2 * cols), slice(cols - 6, cols)
            return pltpu.make_async_remote_copy(
                ext.at[:, p, src, :], ext.at[:, p, dst, :], send_t.at[d, p], recv_t.at[d, p],
                device_id=peers[d], device_id_type=MESH)

        ply_copies = (
            pltpu.make_async_remote_copy(
                ext.at[:, 0, cols:2 * cols, :], ply_halo.at[1], sems.at[1], sems.at[3],
                device_id=peers[2], device_id_type=MESH),
            pltpu.make_async_remote_copy(
                ext.at[:, plies - 1, cols:2 * cols, :], ply_halo.at[0], sems.at[2], sems.at[4],
                device_id=peers[3], device_id_type=MESH),
        )
        ahead = min(2, plies)
        own.wait()
        for p in range(ahead):
            for d in range(2):
                pl.when(has[d])(tile_copy(d, p).start)
        for cond, cp in zip(has[2:], ply_copies):
            pl.when(cond)(cp.start)

        sub = lax.broadcasted_iota(jnp.int32, (cols, rows), 0)
        lane = lax.broadcasted_iota(jnp.int32, (cols, rows), 1)
        core_x = sub + x0
        edge_x = jnp.where(sub < 3, x0 - 3 + sub, x0 + cols - 3 + sub)
        edge_ok = sub < 6

        def bond_masks(xg, ok0, out_ref):
            own_x = ok0 & (xg >= 0) & (xg < x_total)
            total = jnp.zeros((cols, rows), jnp.float32)
            for i, (a, b, length, column) in enumerate(bonds):
                ok = own_x & (xg + a >= 0) & (xg + a < x_total) & (lane + b >= 0) & (lane + b < rows)
                m = jnp.where(ok, 1.0, 0.0)
                out_ref[i] = m
                total = total + m * length
            return total

        mass_c = bond_masks(core_x, sub >= 0, fmask_ref)
        mass_e = bond_masks(edge_x, edge_ok, hmask_ref)
        w_c = 1.0 / jnp.where(mass_c > 0, mass_c, 1.0)
        w_e = jnp.where(mass_e > 0, 1.0 / jnp.where(mass_e > 0, mass_e, 1.0), 0.0)
        wq_ref[0, 0:3, :] = w_e[0:3]
        wq_ref[0, 3:3 + cols, :] = w_c
        wq_ref[0, 3 + cols:6 + cols, :] = w_e[3:6]
        groups = {}
        for i, (a, b, length, column) in enumerate(bonds):
            groups.setdefault(a, []).append((i, b, length, column))
        for a, members in groups.items():
            w_slab = wq_ref[0, 3 + a:3 + a + cols, :]
            for i, b, length, column in members:
                wm_ref[i] = fmask_ref[i] * (w_c + shift_lanes(w_slab, b))

        @pl.when(t == 0)
        def _():
            ext[:, :, 0:cols, :] = jnp.zeros((3, plies, cols, rows), jnp.float32)

        @pl.when(t == nt - 1)
        def _():
            ext[:, :, 2 * cols:3 * cols, :] = jnp.zeros((3, plies, cols, rows), jnp.float32)

        @pl.when(q == 0)
        def _():
            ply_halo[0] = jnp.zeros((3, cols, rows), jnp.float32)

        @pl.when(q == nq - 1)
        def _():
            ply_halo[1] = jnp.zeros((3, cols, rows), jnp.float32)


        def ply_body(p, carry):
            for d in range(2):
                pl.when(has[d] & (p + ahead < plies))(
                    lambda d=d: tile_copy(d, jnp.minimum(p + ahead, plies - 1)).start())
            pl.when(has[1])(tile_copy(0, p).wait_recv)
            pl.when(has[0])(tile_copy(1, p).wait_recv)
            gp = q * plies + p
            kind = angle_ref[p]
            low = lax.broadcasted_iota(jnp.int32, (cols, rows), 0) < 3

            def edge_rows(k, a):
                return jnp.where(low, ext[k, p, cols - 3 + a:2 * cols - 3 + a, :],
                                 ext[k, p, 2 * cols - 3 + a:3 * cols - 3 + a, :])

            uc = [ext[k, p, cols:2 * cols, :] for k in range(3)]
            ue = [edge_rows(k, 0) for k in range(3)]
            uc_y = {b: uc[1] - b for b in lanes}
            ue_y = {b: ue[1] - b for b in lanes}
            dil_c = jnp.zeros((cols, rows), jnp.float32)
            dil_e = jnp.zeros((cols, rows), jnp.float32)
            for a, members in groups.items():
                cs = [ext[k, p, cols + a:2 * cols + a, :] for k in range(3)]
                es = [edge_rows(k, a) for k in range(3)]
                uc_x = uc[0] - a
                ue_x = ue[0] - a
                for i, b, length, column in members:
                    sx = shift_lanes(cs[0], b) - uc_x
                    sy = shift_lanes(cs[1], b) - uc_y[b]
                    sz = shift_lanes(cs[2], b) - uc[2]
                    s2 = sx * sx + sy * sy + sz * sz
                    inv = lax.rsqrt(s2)
                    e = s2 * inv - length
                    m = fmask_ref[i]
                    dil_c = dil_c + e * m
                    sx_ref[i] = sx
                    sy_ref[i] = sy
                    sz_ref[i] = sz
                    pa_ref[i] = (inv * e) * wm_ref[i]
                    pb_ref[i] = inv * m
                    hx = shift_lanes(es[0], b) - ue_x
                    hy = shift_lanes(es[1], b) - ue_y[b]
                    hz = shift_lanes(es[2], b) - ue[2]
                    h2 = hx * hx + hy * hy + hz * hz
                    dil_e = dil_e + (h2 * lax.rsqrt(h2) - length) * hmask_ref[i]
            q_c = (3.0 * dil_c * w_c) * w_c
            q_e = (3.0 * dil_e * w_e) * w_e
            wq_ref[1, 0:3, :] = q_e[0:3]
            wq_ref[1, 3:3 + cols, :] = q_c
            wq_ref[1, 3 + cols:6 + cols, :] = q_e[3:6]

            fx = jnp.zeros((cols, rows), jnp.float32)
            fy = jnp.zeros((cols, rows), jnp.float32)
            fz = jnp.zeros((cols, rows), jnp.float32)
            for a, members in groups.items():
                q_slab = wq_ref[1, 3 + a:3 + a + cols, :]
                for i, b, length, column in members:
                    shear = table_ref[kind, column]
                    alpha = shear * (15.0 / length)
                    beta = 3.0 * bulk_modulus - 5.0 * shear
                    f = alpha * pa_ref[i] + beta * (pb_ref[i] * (q_c + shift_lanes(q_slab, b)))
                    fx = fx + f * sx_ref[i]
                    fy = fy + f * sy_ref[i]
                    fz = fz + f * sz_ref[i]
            above = jnp.where(gp < nsprings, spring_ref[jnp.minimum(gp, nsprings - 1)], 0.0)
            below = jnp.where(gp > 0, spring_ref[jnp.maximum(gp - 1, 0)], 0.0)
            hi_p = jnp.minimum(p + 1, plies - 1)
            lo_p = jnp.maximum(p - 1, 0)
            for k, fk in enumerate((fx, fy, fz)):
                hi = jnp.where(p == plies - 1, uc[k], ext[k, hi_p, cols:2 * cols, :])
                lo = jnp.where(p == 0, uc[k], ext[k, lo_p, cols:2 * cols, :])
                o_ref[k, p] = fk + (above * (hi - uc[k]) + below * (lo - uc[k]))
            return carry

        lax.fori_loop(0, plies, ply_body, 0)
        pl.when(has[3])(ply_copies[0].wait_recv)
        pl.when(has[2])(ply_copies[1].wait_recv)
        g0 = q * plies
        below = jnp.where(g0 > 0, spring_ref[jnp.maximum(g0 - 1, 0)], 0.0)
        gl = q * plies + plies - 1
        above = jnp.where(gl < nsprings, spring_ref[jnp.minimum(gl, nsprings - 1)], 0.0)
        for k in range(3):
            o_ref[k, 0] = o_ref[k, 0] + below * (ply_halo[0, k] - ext[k, 0, cols:2 * cols, :])
            o_ref[k, plies - 1] = o_ref[k, plies - 1] + above * (
                ply_halo[1, k] - ext[k, plies - 1, cols:2 * cols, :])
        for p in range(plies):
            for d in range(2):
                pl.when(has[d])(tile_copy(d, p).wait_send)
        for cond, cp in zip(has[2:], ply_copies):
            pl.when(cond)(cp.wait_send)

    return kernel


def local(displacement, angle_index, bond_table, interface_stiffness):
    comp_count, ply_count, col_count, row_count = displacement.shape
    x_total = col_count * lax.axis_size("tile")
    kernel = make_kernel(ply_count, col_count, row_count, x_total, interface_stiffness.shape[0])
    nbond = len(bond_list())
    smem = pl.BlockSpec(memory_space=pltpu.SMEM)
    return pl.pallas_call(
        kernel,
        in_specs=[smem, smem, smem, pl.BlockSpec(memory_space=pl.ANY)],
        out_specs=pl.BlockSpec(memory_space=pltpu.VMEM),
        out_shape=jax.ShapeDtypeStruct(displacement.shape, jnp.float32),
        scratch_shapes=[
            pltpu.VMEM((3, ply_count, 3 * col_count, row_count), jnp.float32),
            pltpu.VMEM((2, 3, col_count, row_count), jnp.float32),
            pltpu.VMEM((2, col_count + 6, row_count), jnp.float32),
            pltpu.VMEM((nbond, col_count, row_count), jnp.float32),
            pltpu.VMEM((nbond, col_count, row_count), jnp.float32),
            pltpu.VMEM((nbond, col_count, row_count), jnp.float32),
            pltpu.VMEM((nbond, col_count, row_count), jnp.float32),
            pltpu.VMEM((nbond, col_count, row_count), jnp.float32),
            pltpu.VMEM((nbond, col_count, row_count), jnp.float32),
            pltpu.VMEM((nbond, col_count, row_count), jnp.float32),
            pltpu.VMEM((nbond, col_count, row_count), jnp.float32),
            pltpu.SemaphoreType.DMA((5,)),
            pltpu.SemaphoreType.DMA((2, ply_count)),
            pltpu.SemaphoreType.DMA((2, ply_count)),
        ],
        compiler_params=pltpu.CompilerParams(collective_id=0, has_side_effects=True),
    )(angle_index, bond_table, interface_stiffness, displacement)


def solution(mesh):
    placed = (P(None, "ply", "tile", None), P("ply"), P(), P())
    return jax.shard_map(
        local, mesh=mesh, in_specs=placed, out_specs=P(None, "ply", "tile", None), check_vma=False
    )
```
